32 devices in a mesh: ep: 8 (over y, x, core), tp: 4 (over z).
Axes of the slice: x: 2, y: 2, z: 4, core: 2. Of those that a mesh axis runs over, the one named last changes fastest.
Arguments:
- layer_in: bfloat16 [2048, 2048], P('ep', 'tp'), may hold values from -6 to 6
- token_order: int32 [2048], replicated, may hold values from 0 to 2047, as said below
- seq_lengths: int32 [16, 3], P('ep'), may hold values from 1 to 64, 128 in all within a row
- routes: int32 [2048, 8], P('ep'), may hold values from 0 to 15, all different within a row; in each aligned block of 128 rows (0 to 127, 128 to 255, ...) at most 80 rows name the same one
- route_weights: float32 [2048, 8], P('ep'), may hold values from 0.25 to 0.75
- w_query: bfloat16 [2048, 4096], P('ep', 'tp'), may hold values from -0.125 to 0.125
- w_key: bfloat16 [2048, 512], P('ep', 'tp'), may hold values from -0.125 to 0.125
- w_value: bfloat16 [2048, 512], P('ep', 'tp'), may hold values from -0.125 to 0.125
- w_out: bfloat16 [2048, 4096], P('ep', 'tp'), may hold values from -0.5 to 0.5
- norm_attn: bfloat16 [2048], P('ep'), may hold values from 0.5 to 1.5
- norm_moe: bfloat16 [2048], P('ep'), may hold values from 0.5 to 1.5
- query_gain: bfloat16 [128], P('ep'), may hold values from 1 to 1.796875
- key_gain: bfloat16 [128], P('ep'), may hold values from 1 to 1.796875
- w_gate: bfloat16 [16, 768, 2048], P('ep', 'tp'), may hold values from -0.125 to 0.125
- w_up: bfloat16 [16, 768, 2048], P('ep', 'tp'), may hold values from -0.125 to 0.125
- w_down: bfloat16 [16, 768, 2048], P('ep', 'tp'), may hold values from -0.3125 to 0.3125
- grad_out: bfloat16 [2048, 2048], P('ep', 'tp'), may hold values from -6 to 6
Outputs:
- layer_out: bfloat16 [2048, 2048], P('ep', 'tp')
- grad_layer_in: float32 [2048, 2048], P('ep', 'tp')
- grad_w_query: float32 [2048, 4096], P('ep', 'tp')
- grad_w_key: float32 [2048, 512], P('ep', 'tp')
- grad_w_value: float32 [2048, 512], P('ep', 'tp')
- grad_w_out: float32 [2048, 4096], P('ep', 'tp')
- grad_norm_attn: float32 [2048], P('ep')
- grad_norm_moe: float32 [2048], P('ep')
- grad_query_gain: float32 [128], P('ep')
- grad_key_gain: float32 [128], P('ep')
- grad_w_gate: float32 [16, 768, 2048], P('ep', 'tp')
- grad_w_up: float32 [16, 768, 2048], P('ep', 'tp')
- grad_w_down: float32 [16, 768, 2048], P('ep', 'tp')
The draws below stay inside these ranges and needn't reach their ends.
Inputs may be any that keep to these rules, and one draw needn't show every extreme that they name: `token_order`: each row number appears once. Of the 256 dealt rows of one index of ep, exactly 32 are rows of each index of ep. `seq_lengths`: row b holds the lengths of the 3 sequences of block b of 128 dealt rows, in order; they sum to 128, and the longest is 64. `routes`: each row names 8 different experts. Within each aligned block of 128 dealt rows (one micro-batch of one index of ep) no expert is named by more than 80 rows; in some blocks one is named by exactly 80.
All inputs are finite; a program needn't handle non-finite values.
Results may differ from the reference program's by a relative error of at most 0.023.
Values may be sent and summed in bfloat16 or wider, within the bound.
A program may use at most 256 MiB of HBM per device.

```python
import math
import jax
import jax.numpy as jnp
import numpy as np
from jax import lax

D = 2048
HEADS = 32
KV_HEADS = 4
HEAD_DIM = 128
EXP_FF = 768
TOP = 8
MICRO = 2
NSEQ = 3
MB_TOK = 128
EXPERTS = 16
SEQ_MAX = 64
TOK_DEV = 256
TOKENS = 2048
CAP = 80
N_EP = 8


def draw_token_order(key, part):
    per_pair = TOK_DEV // N_EP
    local_keys = jax.random.split(jax.random.fold_in(key, 11), N_EP)

    def local_shuffle(one_key):
        return jax.random.permutation(one_key, TOK_DEV).astype(jnp.int32)
    local = jax.vmap(local_shuffle)(local_keys)
    anchor = local + (jnp.arange(N_EP, dtype=jnp.int32) * TOK_DEV)[:, None]
    grouped = anchor.reshape(N_EP, N_EP, per_pair)
    by_dest = jnp.transpose(grouped, (1, 0, 2)).reshape(N_EP, TOK_DEV)
    mix_keys = jax.random.split(jax.random.fold_in(key, 12), N_EP)

    def dest_shuffle(one_key, row_values):
        return jax.random.permutation(one_key, row_values)
    mixed = jax.vmap(dest_shuffle)(mix_keys, by_dest)
    return mixed.reshape(-1).astype(jnp.int32)


def levels(own_key, shape, cuts, low, high):
    def one(axis_at, blocks):
        heights = jax.random.uniform(jax.random.fold_in(jax.random.fold_in(own_key, 6), axis_at), (blocks,), jnp.float32, low / len(cuts), high / len(cuts))
        return jnp.repeat(jnp.exp(heights), shape[axis_at] // blocks).reshape((-1,) + (1,) * (len(shape) - axis_at - 1))

    level = one(*cuts[0])
    for cut in cuts[1:]:
        level = level * one(*cut)
    return level


def length_profile(number_of, total, most, skew):
    portions = [(1 << 20) // math.isqrt(rank ** skew) + 1 for rank in range(2, number_of + 1)]
    rest, counts = total - most - (number_of - 1), [1] * (number_of - 1)
    while rest > 0:
        candidates = [i for i in range(number_of - 1) if counts[i] < most]
        pool, budget = sum([portions[i] for i in candidates]), rest
        for i in candidates:
            addition = min(most - counts[i], max(1, budget * portions[i] // pool), rest)
            counts[i] = counts[i] + addition
            rest = rest - addition
    return np.array([most] + counts)


def ragged(rng, count, total, reach, skew):
    if count == 2:
        one = jax.random.randint(rng, (), max(1, total - reach), min(reach, total - 1) + 1)
        return jnp.stack([one, total - one])
    sizes = jnp.asarray(length_profile(count, total, reach, skew), jnp.int32)
    pairs = (count - 1) // 2
    donor, taker = sizes[1:1 + 2 * pairs:2], sizes[2:2 + 2 * pairs:2]
    slack = jnp.minimum(donor - 1, reach - taker)
    shifted = jax.random.randint(jax.random.fold_in(rng, 1), (pairs,), 0, 1 << 20) % (slack + 1)
    sizes = sizes.at[1:1 + 2 * pairs:2].set(donor - shifted).at[2:2 + 2 * pairs:2].set(taker + shifted)
    return sizes[jax.random.permutation(jax.random.fold_in(rng, 2), count)]


def shared_out(own_key, own, number, rows, amount, top, bound, slope):
    order = jax.random.permutation(own_key, amount)
    packed, common = shares(amount, rows * top, bound, slope, True), shares(amount, rows * top, bound, slope, False)
    places = jnp.arange(amount)

    def named(sizes, rotation):
        used = int((sizes > 0).sum())
        fixed = max(1, used // 4)
        moved = fixed + (places - fixed + rotation * (used - fixed)) % max(1, amount - fixed)
        return jnp.zeros((amount,), jnp.int32).at[order[jnp.where(places < fixed, places, moved)]].set(jnp.asarray(sizes, jnp.int32))

    sizes = jnp.where(number % 4 == 0, named(packed, number // 4), named(common, number - number // 4 - 1))
    mixed = jax.random.permutation(jax.random.fold_in(own, 3), amount)
    giver, taker = mixed[0:amount // 2 * 2:2], mixed[1:amount // 2 * 2:2]
    margin = jnp.minimum(sizes[giver] - 1, bound - sizes[taker]) // 2
    margin = jnp.where((giver == order[0]) | (taker == order[0]) | (sizes[taker] == 0), 0, jnp.maximum(margin, 0))
    moved = jax.random.randint(jax.random.fold_in(own, 4), (amount // 2,), 0, 1 << 20) % (margin + 1)
    sizes = sizes.at[giver].add(-moved).at[taker].add(moved)
    members = jnp.searchsorted(jnp.cumsum(sizes), jnp.arange(rows * top), side="right").astype(jnp.int32)
    listing = members.reshape(top, rows).T
    listing = listing[jax.random.permutation(jax.random.fold_in(own, 1), rows)]
    rotation = jax.random.randint(jax.random.fold_in(own, 2), (rows, 1), 0, top)
    return jnp.take_along_axis(listing, (jnp.arange(top)[None, :] + rotation) % top, axis=1)


def shares(count, total, most, skew, full):
    portions = [(1 << 20) // math.isqrt(rank ** skew) + 1 for rank in range(1, count + 1)]
    largest = most if full else min(most, max(-(-total // count), total * portions[0] // sum(portions)))
    least = 1 if total - largest >= count - 1 else 0
    given, rest = [largest] + [least] * (count - 1), total - largest - least * (count - 1)
    while rest > 0:
        candidates = [i for i in range(1, count) if given[i] < largest] or [i for i in range(1, count) if given[i] < most]
        mass, remaining = sum([portions[i] for i in candidates]), rest
        for i in candidates:
            extra = min(most - given[i], max(1, remaining * portions[i] // mass), rest)
            given[i] = given[i] + extra
            rest = rest - extra
    return np.array(given)


def bell_draw(key, dims, deviation, limit, cuts=(), kind=jnp.bfloat16):
    result = jax.random.normal(key, dims, jnp.float32) * deviation
    if len(cuts) > 0:
        result = levels(key, dims, cuts, -0.22, 0.18) * result
    return jnp.clip(result, min=-limit, max=limit).astype(kind)


def setup_inputs(seed: int = 0) -> dict:
    key_of = jax.random.split(jax.random.key(seed), 18)
    layer_in = bell_draw(key_of[0], (TOKENS, D), 1.0, 6.0, ((0, 8), (1, 4)))
    token_order = draw_token_order(jax.random.fold_in(key_of[17], 71), 0)
    seq_lengths = jax.vmap(lambda own: ragged(own, NSEQ, MB_TOK, SEQ_MAX, 1))(jax.random.split(key_of[2], (N_EP * MICRO))).reshape((N_EP * MICRO, NSEQ)).astype(jnp.int32)
    routes_keys = jax.random.split(jax.random.fold_in(key_of[3], 1), TOKENS // MB_TOK)
    routes_turns = jax.random.permutation(jax.random.fold_in(key_of[3], 3), TOKENS // MB_TOK)
    routes = jax.vmap(lambda own, number: shared_out(jax.random.fold_in(key_of[3], 2), own, number, MB_TOK, EXPERTS, TOP, CAP, 1))(routes_keys, routes_turns).reshape((TOKENS, TOP))
    route_weights = jnp.clip(0.25 + 0.5 * jax.random.uniform(key_of[4], (TOKENS, TOP), jnp.float32) ** levels(key_of[4], (TOKENS, TOP), ((0, 8),), -0.2, 0.2), 0.25, 0.75)
    w_query = bell_draw(key_of[5], (D, HEADS * HEAD_DIM), D ** -0.5, 0.125, ((0, 8), (1, 4)))
    w_key = bell_draw(key_of[6], (D, KV_HEADS * HEAD_DIM), D ** -0.5, 0.125, ((0, 8), (1, 4)))
    w_value = bell_draw(key_of[7], (D, KV_HEADS * HEAD_DIM), D ** -0.5, 0.125, ((0, 8), (1, 4)))
    w_out = bell_draw(key_of[8], (D, HEADS * HEAD_DIM), (HEADS * HEAD_DIM // 32) ** -0.5, 0.5, ((0, 8), (1, 4)))
    norm_attn = jnp.clip(1.0 + 0.1 * jax.random.normal(key_of[9], (D,), jnp.float32), 0.5, 1.5).astype(jnp.bfloat16)
    norm_moe = jnp.clip(1.0 + 0.1 * jax.random.normal(key_of[10], (D,), jnp.float32), 0.5, 1.5).astype(jnp.bfloat16)
    query_gain = jnp.clip(1.0 + 0.796875 * jax.random.uniform(key_of[11], (HEAD_DIM,), jnp.float32) ** levels(key_of[11], (HEAD_DIM,), ((0, 8),), -0.2, 0.2), 1.0, 1.796875).astype(jnp.bfloat16)
    key_gain = jnp.clip(1.0 + 0.796875 * jax.random.uniform(key_of[12], (HEAD_DIM,), jnp.float32) ** levels(key_of[12], (HEAD_DIM,), ((0, 8),), -0.2, 0.2), 1.0, 1.796875).astype(jnp.bfloat16)
    w_gate = bell_draw(key_of[13], (EXPERTS, EXP_FF, D), D ** -0.5, 0.125, ((0, 8), (1, 4)))
    w_up = bell_draw(key_of[14], (EXPERTS, EXP_FF, D), D ** -0.5, 0.125, ((0, 8), (1, 4)))
    w_down = bell_draw(key_of[15], (EXPERTS, EXP_FF, D), (EXP_FF // 2) ** -0.5, 0.3125, ((0, 8), (1, 4)))
    grad_out = bell_draw(key_of[16], (TOKENS, D), 1.0, 6.0, ((0, 8), (1, 4)))
    return dict(layer_in=layer_in, token_order=token_order, seq_lengths=seq_lengths, routes=routes, route_weights=route_weights, w_query=w_query, w_key=w_key, w_value=w_value, w_out=w_out, norm_attn=norm_attn, norm_moe=norm_moe, query_gain=query_gain, key_gain=key_gain, w_gate=w_gate, w_up=w_up, w_down=w_down, grad_out=grad_out)


epsilon = 1e-06
rope_base = 1000000.0
highest = lax.Precision.HIGHEST

@jax.custom_vjp
def low(v):
    return lax.optimization_barrier(v.astype(jnp.bfloat16)).astype(jnp.float32)

@jax.custom_vjp
def low_back(v):
    return v

def low_keep(v):
    return (low(v), None)

def low_pass(kept, grad):
    return (grad,)

def back_keep(v):
    return (v, None)

def back_low(kept, grad):
    return (low(grad),)
low.defvjp(low_keep, low_pass)
low_back.defvjp(back_keep, back_low)

def rms_scale(values, gain_vector):
    return values * lax.rsqrt(lax.optimization_barrier(jnp.mean(values * values, axis=-1, keepdims=True)) + epsilon) * gain_vector

def positions_of(lengths, row_count):
    offsets = jnp.arange(row_count, dtype=jnp.int32)
    seq_ends = jnp.cumsum(lengths).astype(jnp.int32)
    segment = lax.optimization_barrier(jnp.sum((offsets[:, None] >= seq_ends[None, :]).astype(jnp.int32), axis=1))
    starts = (seq_ends - lengths).astype(jnp.int32)
    in_segment = segment[:, None] == jnp.arange(lengths.shape[0], dtype=jnp.int32)[None, :]
    position = offsets - lax.optimization_barrier(jnp.sum(jnp.where(in_segment, starts[None, :], 0), axis=1)).astype(jnp.int32)
    return (segment, position)

def rope_tables(position, half_dim):
    frequency = rope_base ** (-jnp.arange(half_dim, dtype=jnp.float32) / half_dim)
    angles = position.astype(jnp.float32)[:, None] * frequency[None, :]
    return (jnp.cos(angles)[:, None, :], jnp.sin(angles)[:, None, :])

def rotate(values, cosine, sine_table):
    half_dim = values.shape[-1] // 2
    first_half = values[..., :half_dim]
    second_half = values[..., half_dim:]
    return jnp.concatenate([first_half * cosine - second_half * sine_table, second_half * cosine + first_half * sine_table], axis=-1)

def slot_tables(routes, experts, capacity, top_count):
    flat_routes = routes.reshape(-1).astype(jnp.int32)
    onehot = (flat_routes[:, None] == jnp.arange(experts, dtype=jnp.int32)[None, :]).astype(jnp.int32)
    before = jnp.cumsum(onehot, axis=0) - onehot
    slot_index = lax.optimization_barrier(jnp.sum(before * onehot, axis=1)).astype(jnp.int32)
    target = (flat_routes * capacity + slot_index).astype(jnp.int32)
    token_of = (jnp.arange(flat_routes.shape[0], dtype=jnp.int32) // top_count).astype(jnp.int32)
    source = jnp.zeros((experts * capacity,), jnp.int32).at[target].set(token_of)
    return (target, source)

def block_layer(layer_rows, lengths, routes, mix_weights, params):
    w_query, w_key, w_value, w_out, norm_attn, norm_moe, query_gain, key_gain, w_gate, w_up, w_down = params
    row_count = layer_rows.shape[0]
    group_size = HEADS // KV_HEADS
    segment, position = positions_of(lengths, row_count)
    normed = low(rms_scale(layer_rows, norm_attn))
    query_proj = low_back(jnp.dot(normed, w_query, precision=highest)).reshape(row_count, HEADS, HEAD_DIM)
    key_proj = low_back(jnp.dot(normed, w_key, precision=highest)).reshape(row_count, KV_HEADS, HEAD_DIM)
    value_proj = low_back(jnp.dot(normed, w_value, precision=highest)).reshape(row_count, KV_HEADS, HEAD_DIM)
    cosine, sine_table = rope_tables(position, HEAD_DIM // 2)
    queries = low(rotate(rms_scale(query_proj, query_gain), cosine, sine_table)).reshape(row_count, KV_HEADS, group_size, HEAD_DIM)
    key_rows = low(rotate(rms_scale(key_proj, key_gain), cosine, sine_table))
    values = low(value_proj)
    scores = low_back(jnp.einsum('qkgd,tkd->kgqt', queries, key_rows, precision=highest) * HEAD_DIM ** (-0.5))
    offsets = jnp.arange(row_count, dtype=jnp.int32)
    allowed = (segment[:, None] == segment[None, :]) & (offsets[None, :] <= offsets[:, None])
    scores = jnp.where(allowed, scores, -1e+30)
    row_peak = lax.optimization_barrier(jnp.max(scores, axis=-1, keepdims=True))
    exponent = jnp.exp(scores - row_peak)
    attn_probs = low(exponent / lax.optimization_barrier(jnp.sum(exponent, axis=-1, keepdims=True)))
    context = jnp.einsum('kgqt,tkd->qkgd', attn_probs, values, precision=highest).reshape(row_count, HEADS * HEAD_DIM)
    context = low(low_back(context))
    attn_out = low_back(jnp.einsum('qh,dh->qd', context, w_out, precision=highest))
    hidden = layer_rows + attn_out
    moe_in = low(rms_scale(hidden, norm_moe))
    target, source = slot_tables(routes, EXPERTS, CAP, TOP)
    routed = low_back(jnp.take(moe_in, source, axis=0)).reshape(EXPERTS, CAP, D)
    gate_pre = low_back(jnp.einsum('ecd,efd->ecf', routed, w_gate, precision=highest))
    up_pre = low_back(jnp.einsum('ecd,efd->ecf', routed, w_up, precision=highest))
    active = low(jax.nn.silu(gate_pre) * up_pre)
    expert_out = low_back(low(jnp.einsum('ecf,efd->ecd', active, w_down, precision=highest))).reshape(EXPERTS * CAP, D)
    picked = jnp.take(expert_out, target, axis=0).reshape(row_count, TOP, D)
    mixed = lax.optimization_barrier(jnp.sum(mix_weights[:, :, None] * picked, axis=1))
    return hidden + mixed

def reference(layer_in, token_order, seq_lengths, routes, route_weights, w_query, w_key, w_value, w_out, norm_attn, norm_moe, query_gain, key_gain, w_gate, w_up, w_down, grad_out):
    block_count = N_EP * MICRO
    order = token_order.astype(jnp.int32)
    inverse = jnp.zeros((TOKENS,), jnp.int32).at[order].set(jnp.arange(TOKENS, dtype=jnp.int32))
    params = tuple((weight.astype(jnp.float32) for weight in (w_query, w_key, w_value, w_out, norm_attn, norm_moe, query_gain, key_gain, w_gate, w_up, w_down)))
    rows_in = jnp.take(layer_in, order, axis=0).astype(jnp.float32).reshape(block_count, MB_TOK, D)
    grad_dealt = jnp.take(grad_out, order, axis=0).astype(jnp.float32).reshape(block_count, MB_TOK, D)
    route_blocks = routes.reshape(block_count, MB_TOK, TOP)
    weight_blocks = route_weights.astype(jnp.float32).reshape(block_count, MB_TOK, TOP)
    checked = jax.checkpoint(block_layer)

    def forward_all(rows_all, weights_all):

        def one_block(unused_carry, pieces):
            return (unused_carry, checked(pieces[0], pieces[1], pieces[2], pieces[3], weights_all))
        _, outputs = lax.scan(one_block, jnp.float32(0.0), (rows_all, seq_lengths, route_blocks, weight_blocks))
        return outputs
    outputs, pullback = jax.vjp(forward_all, rows_in, params)
    grad_rows, grad_params = pullback(grad_dealt)
    layer_out = jnp.take(outputs.reshape(TOKENS, D), inverse, axis=0).astype(jnp.bfloat16)
    grad_layer_in = jnp.take(grad_rows.reshape(TOKENS, D), inverse, axis=0)
    return (layer_out, grad_layer_in, grad_params[0], grad_params[1], grad_params[2], grad_params[3], grad_params[4], grad_params[5], grad_params[6], grad_params[7], grad_params[8], grad_params[9], grad_params[10])
```

```python
import jax
import jax.numpy as jnp
from jax import lax
from jax.sharding import PartitionSpec as P

HEAD_DIM = 128
MICRO = 2
F32 = jnp.float32
BF16 = jnp.bfloat16

epsilon = 1e-06
rope_base = 1000000.0


def positions_of(lengths, row_count):
    offsets = jnp.arange(row_count, dtype=jnp.int32)
    seq_ends = jnp.cumsum(lengths)
    segment = jnp.sum((offsets[:, None] >= seq_ends[None, :]).astype(jnp.int32), axis=1)
    starts = seq_ends - lengths
    in_segment = segment[:, None] == jnp.arange(lengths.shape[0], dtype=jnp.int32)[None, :]
    position = offsets - jnp.sum(jnp.where(in_segment, starts[None, :], 0), axis=1)
    return (segment, position)


def rope_tables(position, half_dim):
    frequency = rope_base ** (-jnp.arange(half_dim, dtype=F32) / half_dim)
    angles = position.astype(F32)[:, None] * frequency[None, :]
    return (jnp.cos(angles)[:, None, :], jnp.sin(angles)[:, None, :])


def rotate(values, cosine, sine_table):
    half_dim = values.shape[-1] // 2
    first_half = values[..., :half_dim]
    second_half = values[..., half_dim:]
    return jnp.concatenate(
        [
            first_half * cosine - second_half * sine_table,
            second_half * cosine + first_half * sine_table,
        ],
        axis=-1,
    )


def rotate_back(incoming, cosine, sine_table):
    return rotate(incoming, cosine, -sine_table)


def deal_matrices(token_order, ep_index, rows_dev, ep_count):
    per_pair = rows_dev // ep_count
    rows = jnp.arange(rows_dev, dtype=jnp.int32)
    home = ep_index * rows_dev + rows
    at = jnp.arange(token_order.shape[0], dtype=jnp.int32)
    place = jnp.sum(jnp.where(token_order[None, :] == home[:, None], at[None, :], 0), axis=1)
    dest = place // rows_dev
    rank = jnp.sum(
        ((dest[:, None] == dest[None, :]) & (place[None, :] < place[:, None])).astype(jnp.int32),
        axis=1,
    )
    send_slot = dest * per_pair + rank
    send = (send_slot[None, :] == rows[:, None]).astype(BF16)
    mine = lax.dynamic_slice_in_dim(token_order, ep_index * rows_dev, rows_dev, 0)
    source = mine // rows_dev
    my_rank = jnp.sum(
        ((source[:, None] == source[None, :]) & (rows[None, :] < rows[:, None])).astype(jnp.int32),
        axis=1,
    )
    recv_slot = source * per_pair + my_rank
    recv = (recv_slot[:, None] == rows[None, :]).astype(BF16)
    return (send, recv)


def inverse_rms(values):
    return lax.rsqrt(jnp.mean(values * values, axis=-1, keepdims=True) + epsilon)


def norm_back(grad_unit, unit_values, inverse):
    return inverse * (
        grad_unit - unit_values * jnp.mean(grad_unit * unit_values, axis=-1, keepdims=True)
    )


def dot_nn(left, right):
    return jnp.dot(left, right, preferred_element_type=F32)


def dot_tn(left_rows, right_rows):
    return lax.dot_general(
        left_rows, right_rows, (((0,), (0,)), ((), ())), preferred_element_type=F32
    )


def dot_nt(left_rows, right_matrix):
    return lax.dot_general(
        left_rows, right_matrix, (((1,), (1,)), ((), ())), preferred_element_type=F32
    )


def permute_rows(matrix, rows):
    return dot_nn(matrix, rows).astype(BF16)


def exchange(rows, ep_count):
    split = rows.reshape(ep_count, rows.shape[0] // ep_count, rows.shape[1])
    moved = lax.all_to_all(split, "ep", split_axis=0, concat_axis=0, tiled=True)
    return moved.reshape(rows.shape)


def on_device(
    layer_in,
    token_order,
    seq_lengths,
    routes,
    route_weights,
    w_query,
    w_key,
    w_value,
    w_out,
    norm_attn,
    norm_moe,
    query_gain,
    key_gain,
    w_gate,
    w_up,
    w_down,
    grad_out,
):
    ep_count = lax.axis_size("ep")
    tp_count = lax.axis_size("tp")
    tp_index = lax.axis_index("tp")
    ep_index = lax.axis_index("ep")
    local_experts, hidden_here, model_width = w_gate.shape
    experts = local_experts * ep_count
    rows_dev = layer_in.shape[0]
    micro_rows = rows_dev // MICRO
    share_width = layer_in.shape[1]
    score_scale = HEAD_DIM ** (-0.5)

    send, recv = deal_matrices(token_order, ep_index, rows_dev, ep_count)
    both = jnp.concatenate([layer_in, grad_out], axis=1)
    got = permute_rows(recv, exchange(permute_rows(send, both), ep_count))
    layer_full = lax.all_gather(got[:, :share_width], "tp", axis=1, tiled=True)
    grad_full = lax.all_gather(got[:, share_width:], "tp", axis=1, tiled=True)

    q_width, kv_width = w_query.shape[1], w_key.shape[1]
    packed = jnp.concatenate([w_query, w_out, w_key, w_value], axis=1)
    packed = lax.all_gather(packed, "ep", axis=0, tiled=True)
    full_query = packed[:, :q_width]
    full_out = packed[:, q_width : 2 * q_width]
    full_kv = packed[:, 2 * q_width :]
    gains = jnp.concatenate([norm_attn, norm_moe, query_gain, key_gain]).reshape(1, -1)
    gains = lax.all_gather(gains, "ep", axis=0, tiled=True).astype(F32)
    part = norm_attn.shape[0]
    head_part = query_gain.shape[0]
    gain_attn = gains[:, :part].reshape(-1)
    gain_moe = gains[:, part : 2 * part].reshape(-1)
    gain_query = gains[:, 2 * part : 2 * part + head_part].reshape(-1)
    gain_key = gains[:, 2 * part + head_part :].reshape(-1)

    expert_ids = jnp.arange(experts, dtype=jnp.int32)
    dense = jnp.sum(
        jnp.where(routes[:, :, None] == expert_ids[None, None, :], route_weights[:, :, None], 0.0),
        axis=1,
    )
    scale_all = lax.all_gather(dense, "ep", axis=0, tiled=True)
    scale = lax.dynamic_slice_in_dim(scale_all, ep_index * local_experts, local_experts, 1)
    all_grad = lax.all_gather(grad_full, "ep", axis=0, tiled=True)

    heads_here = q_width // HEAD_DIM
    kv_here = kv_width // HEAD_DIM
    group_size = heads_here // kv_here
    segment, position = jax.vmap(positions_of, in_axes=(0, None))(seq_lengths, micro_rows)
    cosine, sine_table = rope_tables(position.reshape(-1), HEAD_DIM // 2)
    layer_float = layer_full.astype(F32)
    inverse_one = inverse_rms(layer_float)
    unit_one = layer_float * inverse_one
    normed = (unit_one * gain_attn).astype(BF16)
    query_proj = dot_nn(normed, full_query).reshape(rows_dev, heads_here, HEAD_DIM)
    kv_proj = dot_nn(normed, full_kv)
    key_proj = kv_proj[:, :kv_width].reshape(rows_dev, kv_here, HEAD_DIM)
    value_proj = kv_proj[:, kv_width:].reshape(rows_dev, kv_here, HEAD_DIM)
    inverse_query = inverse_rms(query_proj)
    unit_query = query_proj * inverse_query
    inverse_key = inverse_rms(key_proj)
    unit_key = key_proj * inverse_key
    queries = (
        rotate(unit_query * gain_query, cosine, sine_table)
        .astype(BF16)
        .reshape(MICRO, micro_rows, kv_here, group_size, HEAD_DIM)
    )
    key_rows = (
        rotate(unit_key * gain_key, cosine, sine_table)
        .astype(BF16)
        .reshape(MICRO, micro_rows, kv_here, HEAD_DIM)
    )
    values = value_proj.astype(BF16).reshape(MICRO, micro_rows, kv_here, HEAD_DIM)
    scores = (
        jnp.einsum("mqkgd,mtkd->mkgqt", queries, key_rows, preferred_element_type=F32)
        * score_scale
    )
    offsets = jnp.arange(micro_rows, dtype=jnp.int32)
    allowed = (segment[:, :, None] == segment[:, None, :]) & (
        offsets[None, None, :] <= offsets[None, :, None]
    )
    scores = jnp.where(allowed[:, None, None], scores, -1e30)
    row_peak = jnp.max(scores, axis=-1, keepdims=True)
    exponent = jnp.exp(scores - row_peak)
    attn_probs = exponent / jnp.sum(exponent, axis=-1, keepdims=True)
    probs_low = attn_probs.astype(BF16)
    context = jnp.einsum("mkgqt,mtkd->mqkgd", probs_low, values, preferred_element_type=F32)
    context_low = context.reshape(rows_dev, heads_here * HEAD_DIM).astype(BF16)
    attn_part = dot_nt(context_low, full_out)
    attn_out = lax.psum(attn_part.astype(BF16), "tp").astype(F32)
    hidden = layer_float + attn_out
    inverse_two = inverse_rms(hidden)
    unit_two = hidden * inverse_two
    moe_in = (unit_two * gain_moe).astype(BF16)

    all_in = lax.all_gather(moe_in, "ep", axis=0, tiled=True)
    flat = local_experts * hidden_here
    gate_matrix = w_gate.reshape(flat, model_width)
    up_matrix = w_up.reshape(flat, model_width)
    down_matrix = w_down.reshape(flat, model_width)
    row_scale = jnp.repeat(scale, hidden_here, axis=1)
    gate_pre = dot_nt(all_in, gate_matrix)
    up_pre = dot_nt(all_in, up_matrix)
    grad_active = dot_nt(all_grad, down_matrix) * row_scale
    sigmoid_gate = jax.nn.sigmoid(gate_pre)
    silu_gate = gate_pre * sigmoid_gate
    active = (silu_gate * up_pre * row_scale).astype(BF16)
    grad_up_pre = (grad_active * silu_gate).astype(BF16)
    grad_gate_pre = (
        grad_active * up_pre * sigmoid_gate * (1.0 + gate_pre * (1.0 - sigmoid_gate))
    ).astype(BF16)
    grad_partial = dot_nn(grad_gate_pre, gate_matrix) + dot_nn(grad_up_pre, up_matrix)
    grad_partial = lax.psum_scatter(
        grad_partial.astype(BF16), "ep", scatter_dimension=0, tiled=True
    )
    grad_share = lax.psum_scatter(grad_partial, "tp", scatter_dimension=1, tiled=True)
    out_partial = dot_nn(active, down_matrix)
    out_partial = lax.psum_scatter(out_partial.astype(BF16), "ep", scatter_dimension=0, tiled=True)
    mixed = lax.psum_scatter(out_partial, "tp", scatter_dimension=1, tiled=True)
    hidden_share = lax.dynamic_slice_in_dim(hidden, tp_index * share_width, share_width, 1)
    layer_dealt = (hidden_share + mixed.astype(F32)).astype(BF16)
    grad_w_down = dot_tn(active, all_grad).reshape(w_down.shape)
    grad_w_gate = dot_tn(grad_gate_pre, all_in).reshape(w_gate.shape)
    grad_w_up = dot_tn(grad_up_pre, all_in).reshape(w_up.shape)

    grad_float = grad_full.astype(F32)
    grad_moe_in = lax.all_gather(grad_share, "tp", axis=1, tiled=True).astype(F32)
    norm_moe_part = jnp.sum(grad_moe_in * unit_two, axis=0)
    grad_hidden = grad_float + norm_back(grad_moe_in * gain_moe, unit_two, inverse_two)
    grad_attn = grad_hidden.astype(BF16)
    grad_w_out = dot_tn(grad_attn, context_low)
    grad_context = (
        dot_nn(grad_attn, full_out)
        .astype(BF16)
        .reshape(MICRO, micro_rows, kv_here, group_size, HEAD_DIM)
    )
    grad_probs = jnp.einsum("mqkgd,mtkd->mkgqt", grad_context, values, preferred_element_type=F32)
    prob_delta = jnp.sum(attn_probs * grad_probs, axis=-1, keepdims=True)
    grad_scores = (attn_probs * (grad_probs - prob_delta)).astype(BF16)
    grad_queries = (
        jnp.einsum("mkgqt,mtkd->mqkgd", grad_scores, key_rows, preferred_element_type=F32).reshape(
            rows_dev, heads_here, HEAD_DIM
        )
        * score_scale
    )
    grad_keys = (
        jnp.einsum("mkgqt,mqkgd->mtkd", grad_scores, queries, preferred_element_type=F32).reshape(
            rows_dev, kv_here, HEAD_DIM
        )
        * score_scale
    )
    grad_values = jnp.einsum(
        "mkgqt,mqkgd->mtkd", probs_low, grad_context, preferred_element_type=F32
    )
    grad_unit_query = rotate_back(grad_queries, cosine, sine_table)
    grad_unit_key = rotate_back(grad_keys, cosine, sine_table)
    query_gain_part = jnp.sum(grad_unit_query * unit_query, axis=(0, 1))
    key_gain_part = jnp.sum(grad_unit_key * unit_key, axis=(0, 1))
    grad_query_proj = (
        norm_back(grad_unit_query * gain_query, unit_query, inverse_query)
        .reshape(rows_dev, heads_here * HEAD_DIM)
        .astype(BF16)
    )
    grad_key_proj = (
        norm_back(grad_unit_key * gain_key, unit_key, inverse_key)
        .reshape(rows_dev, kv_width)
        .astype(BF16)
    )
    grad_value_proj = grad_values.reshape(rows_dev, kv_width).astype(BF16)
    grad_kv_proj = jnp.concatenate([grad_key_proj, grad_value_proj], axis=1)
    normed_part = dot_nt(grad_query_proj, full_query) + dot_nt(grad_kv_proj, full_kv)
    grad_normed = lax.psum_scatter(
        normed_part.astype(BF16), "tp", scatter_dimension=1, tiled=True
    ).astype(F32)
    grad_packed = jnp.concatenate(
        [
            dot_tn(normed, grad_query_proj).astype(BF16),
            grad_w_out.astype(BF16),
            dot_tn(normed, grad_kv_proj).astype(BF16),
        ],
        axis=1,
    )
    grad_packed = lax.psum_scatter(grad_packed, "ep", scatter_dimension=0, tiled=True).astype(F32)

    start = tp_index * share_width
    gain_share = lax.dynamic_slice_in_dim(gain_attn, start, share_width, 0)
    unit_share = lax.dynamic_slice_in_dim(unit_one, start, share_width, 1)
    hidden_grad_share = lax.dynamic_slice_in_dim(grad_hidden, start, share_width, 1)
    scaled = grad_normed * gain_share
    row_mean = lax.psum(jnp.sum(scaled * unit_share, axis=1), "tp") / model_width
    grad_layer = hidden_grad_share + inverse_one * (scaled - unit_share * row_mean[:, None])
    norm_attn_part = lax.dynamic_update_slice_in_dim(
        jnp.zeros((model_width,), F32), jnp.sum(grad_normed * unit_share, axis=0), start, 0
    )
    small = jnp.concatenate(
        [norm_attn_part, norm_moe_part / tp_count, query_gain_part, key_gain_part]
    )
    small = lax.psum(small, ("ep", "tp"))
    grad_norm_attn = lax.dynamic_slice_in_dim(small, ep_index * part, part, 0)
    grad_norm_moe = lax.dynamic_slice_in_dim(small, model_width + ep_index * part, part, 0)
    grad_query_gain = lax.dynamic_slice_in_dim(
        small, 2 * model_width + ep_index * head_part, head_part, 0
    )
    grad_key_gain = lax.dynamic_slice_in_dim(
        small, 2 * model_width + HEAD_DIM + ep_index * head_part, head_part, 0
    )

    back = jnp.concatenate([layer_dealt, grad_layer.astype(BF16)], axis=1)
    home = exchange(dot_tn(recv, back).astype(BF16), ep_count)
    home = dot_tn(send, home)
    return (
        home[:, :share_width].astype(BF16),
        home[:, share_width:],
        grad_packed[:, :q_width],
        grad_packed[:, 2 * q_width : 2 * q_width + kv_width],
        grad_packed[:, 2 * q_width + kv_width :],
        grad_packed[:, q_width : 2 * q_width],
        grad_norm_attn,
        grad_norm_moe,
        grad_query_gain,
        grad_key_gain,
        grad_w_gate,
        grad_w_up,
        grad_w_down,
    )


def solution(mesh):
    return jax.shard_map(
        on_device,
        mesh=mesh,
        in_specs=(
            P("ep", "tp"),
            P(),
            P("ep", None),
            P("ep", None),
            P("ep", None),
            P("ep", "tp"),
            P("ep", "tp"),
            P("ep", "tp"),
            P("ep", "tp"),
            P("ep"),
            P("ep"),
            P("ep"),
            P("ep"),
            P("ep", "tp", None),
            P("ep", "tp", None),
            P("ep", "tp", None),
            P("ep", "tp"),
        ),
        out_specs=(
            P("ep", "tp"),
            P("ep", "tp"),
            P("ep", "tp"),
            P("ep", "tp"),
            P("ep", "tp"),
            P("ep", "tp"),
            P("ep"),
            P("ep"),
            P("ep"),
            P("ep"),
            P("ep", "tp", None),
            P("ep", "tp", None),
            P("ep", "tp", None),
        ),
        check_vma=False,
    )
```

```python
import functools

import jax
import jax.numpy as jnp
from jax import lax
from jax.experimental import pallas as pl
from jax.experimental.pallas import tpu as pltpu
from jax.sharding import PartitionSpec as P

HEAD_DIM = 128
MICRO = 2
F32 = jnp.float32
BF16 = jnp.bfloat16
SCALE_TERMS = 3
VMEM_LIMIT = 66 * 1000 * 1000

epsilon = 1e-06
rope_base = 1000000.0


def positions_of(lengths, row_count):
    offsets = jnp.arange(row_count, dtype=jnp.int32)
    seq_ends = jnp.cumsum(lengths)
    segment = jnp.sum((offsets[:, None] >= seq_ends[None, :]).astype(jnp.int32), axis=1)
    starts = seq_ends - lengths
    in_segment = segment[:, None] == jnp.arange(lengths.shape[0], dtype=jnp.int32)[None, :]
    position = offsets - jnp.sum(jnp.where(in_segment, starts[None, :], 0), axis=1)
    return (segment, position)


def rope_tables(position, half_dim):
    frequency = rope_base ** (-jnp.arange(half_dim, dtype=F32) / half_dim)
    angles = position.astype(F32)[:, None] * frequency[None, :]
    return (jnp.cos(angles)[:, None, :], jnp.sin(angles)[:, None, :])


def rotate(values, cosine, sine_table):
    half_dim = values.shape[-1] // 2
    first_half = values[..., :half_dim]
    second_half = values[..., half_dim:]
    return jnp.concatenate(
        [
            first_half * cosine - second_half * sine_table,
            second_half * cosine + first_half * sine_table,
        ],
        axis=-1,
    )


def rotate_back(incoming, cosine, sine_table):
    return rotate(incoming, cosine, -sine_table)


def deal_matrices(token_order, ep_index, rows_dev, ep_count):
    per_pair = rows_dev // ep_count
    rows = jnp.arange(rows_dev, dtype=jnp.int32)
    home = ep_index * rows_dev + rows
    at = jnp.arange(token_order.shape[0], dtype=jnp.int32)
    place = jnp.sum(jnp.where(token_order[None, :] == home[:, None], at[None, :], 0), axis=1)
    dest = place // rows_dev
    rank = jnp.sum(
        ((dest[:, None] == dest[None, :]) & (place[None, :] < place[:, None])).astype(jnp.int32),
        axis=1,
    )
    send_slot = dest * per_pair + rank
    send = (send_slot[None, :] == rows[:, None]).astype(BF16)
    mine = lax.dynamic_slice_in_dim(token_order, ep_index * rows_dev, rows_dev, 0)
    source = mine // rows_dev
    my_rank = jnp.sum(
        ((source[:, None] == source[None, :]) & (rows[None, :] < rows[:, None])).astype(jnp.int32),
        axis=1,
    )
    recv_slot = source * per_pair + my_rank
    recv = (recv_slot[:, None] == rows[None, :]).astype(BF16)
    return (send, recv)


def inverse_rms(values):
    return lax.rsqrt(jnp.mean(values * values, axis=-1, keepdims=True) + epsilon)


def norm_back(grad_unit, unit_values, inverse):
    return inverse * (
        grad_unit - unit_values * jnp.mean(grad_unit * unit_values, axis=-1, keepdims=True)
    )


def dot_nn(left, right):
    return jnp.dot(left, right, preferred_element_type=F32)


def dot_tn(left_rows, right_rows):
    return lax.dot_general(
        left_rows, right_rows, (((0,), (0,)), ((), ())), preferred_element_type=F32
    )


def dot_nt(left_rows, right_matrix):
    return lax.dot_general(
        left_rows, right_matrix, (((1,), (1,)), ((), ())), preferred_element_type=F32
    )


def permute_rows(matrix, rows):
    return dot_nn(matrix, rows).astype(BF16)


def exchange(rows, ep_count):
    split = rows.reshape(ep_count, rows.shape[0] // ep_count, rows.shape[1])
    moved = lax.all_to_all(split, "ep", split_axis=0, concat_axis=0, tiled=True)
    return moved.reshape(rows.shape)


MESH_ID = pl.DeviceIdType.MESH
HALF = 2
E0, E1, P0, P1, A0, B0, PA0, PB0, A1, B1, PA1, PB1, D0, PD0, D1, PD1 = range(16)
SLOT_E, SLOT_P, SLOT_A, SLOT_B = (E0, E1), (P0, P1), (A0, A1), (B0, B1)
SLOT_D, SLOT_PA, SLOT_PB, SLOT_PD = (D0, D1), (PA0, PA1), (PB0, PB1), (PD0, PD1)
FOR_PARTNER = (P0, P1, PB0, PB1, PA0, PA1, PD0, PD1)


def roles():
    e = lax.axis_index("ep")
    core, x, y = e % 2, (e // 2) % 2, e // 4
    other = 1 - 2 * core
    over_x, over_y = e + 2 - 4 * x, e + 4 - 8 * y
    a = over_x * (1 - core) + over_y * core
    b = over_y * (1 - core) + over_x * core
    d = over_x + over_y - e
    return dict(e=e, p=e + other, a=a, b=b, d=d, pa=a + other, pb=b + other, pd=d + other)


def slot_owner(r):
    names = ("e", "e", "p", "p", "a", "b", "pa", "pb", "a", "b", "pa", "pb", "d", "pd", "d", "pd")
    halves = (0, 1, 0, 1, 0, 0, 0, 0, 1, 1, 1, 1, 0, 0, 1, 1)
    return [(r[name], half) for name, half in zip(names, halves)]


def greet(plane, line):
    barrier = pltpu.get_barrier_semaphore()
    for device in plane:
        pl.semaphore_signal(barrier, inc=1, device_id={"ep": device}, device_id_type=MESH_ID)
    for device in line:
        pl.semaphore_signal(barrier, inc=1, device_id={"tp": device}, device_id_type=MESH_ID)
    pl.semaphore_wait(barrier, len(plane) + len(line))


def send_to(src, dst, send_sem, recv_sem, **device):
    return pltpu.make_async_remote_copy(
        src_ref=src,
        dst_ref=dst,
        send_sem=send_sem,
        recv_sem=recv_sem,
        device_id=device,
        device_id_type=MESH_ID,
    )


class PlaneGather:
    kinds = 7

    def __init__(self, r, held, half, send, recv):
        self.r, self.held, self.half, self.send, self.recv = r, held, half, send, recv

    def slot(self, index):
        return self.held.at[pl.ds(index * self.half, self.half)]

    def copy(self, kind, k):
        source, target, device = (
            (SLOT_E, SLOT_A, "a"),
            (SLOT_E, SLOT_B, "b"),
            (SLOT_E, SLOT_P, "p"),
            (SLOT_A, SLOT_D, "b"),
            (SLOT_A, SLOT_PB, "p"),
            (SLOT_B, SLOT_PA, "p"),
            (SLOT_D, SLOT_PD, "p"),
        )[kind]
        return send_to(
            self.slot(source[k]),
            self.slot(target[k]),
            self.send.at[kind, k],
            self.recv.at[kind, k],
            ep=self.r[device],
        )

    def begin(self):
        for k in range(HALF):
            for kind in range(3):
                self.copy(kind, k).start()

    def arrived(self, kind, k):
        self.copy(kind, k).wait_recv()

    def pass_near(self, k):
        self.arrived(0, k)
        self.copy(3, k).start()
        self.copy(4, k).start()
        self.arrived(1, k)
        self.copy(5, k).start()

    def pass_far(self, k):
        self.arrived(3, k)
        self.copy(6, k).start()

    def sent(self):
        for k in range(HALF):
            for kind in range(self.kinds):
                self.copy(kind, k).wait_send()


class PlaneSum:
    def __init__(self, r, part, near, far, first, second, half, sems):
        self.r, self.part, self.half = r, part, half
        self.near, self.far, self.first, self.second = near, far, first, second
        self.near_send, self.near_recv, self.send, self.recv = sems

    def slot(self, index):
        return self.part.at[pl.ds(index * self.half, self.half)]

    def rows(self, buffer, index):
        return buffer.at[pl.ds(index * self.half, self.half)]

    def near_copy(self, index):
        return send_to(
            self.slot(FOR_PARTNER[index]),
            self.rows(self.near, index),
            self.near_send.at[index],
            self.near_recv.at[index],
            ep=self.r["p"],
        )

    def far_copy(self, kind, k):
        source, target, device = (
            (SLOT_D, self.far, "b"),
            (SLOT_A, self.first, "a"),
            (SLOT_B, self.second, "b"),
        )[kind]
        return send_to(
            self.slot(source[k]),
            self.rows(target, k),
            self.send.at[kind, k],
            self.recv.at[kind, k],
            ep=self.r[device],
        )

    def add_up(self, slot, others):
        total = self.slot(slot)[...].astype(F32)
        for other in others:
            total = total + other[...].astype(F32)
        return total

    def near_sum(self, name, k):
        index = 2 * name + k
        slot = (SLOT_E, SLOT_A, SLOT_B, SLOT_D)[name][k]
        self.near_copy(index).wait_recv()
        return slot, [self.rows(self.near, index)]

    def pass_far(self, k):
        slot, others = self.near_sum(3, k)
        self.slot(slot)[...] = self.add_up(slot, others).astype(BF16)
        self.far_copy(0, k).start()

    def pass_second(self, k):
        slot, others = self.near_sum(2, k)
        self.slot(slot)[...] = self.add_up(slot, others).astype(BF16)
        self.far_copy(2, k).start()

    def pass_first(self, k):
        slot, others = self.near_sum(1, k)
        self.far_copy(0, k).wait_recv()
        self.slot(slot)[...] = self.add_up(slot, others + [self.rows(self.far, k)]).astype(BF16)
        self.far_copy(1, k).start()

    def total(self, k):
        slot, others = self.near_sum(0, k)
        self.far_copy(1, k).wait_recv()
        self.far_copy(2, k).wait_recv()
        return self.add_up(slot, others + [self.rows(self.first, k), self.rows(self.second, k)])

    def sent(self):
        for index in range(4 * HALF):
            self.near_copy(index).wait_send()
        for kind in range(3):
            for k in range(HALF):
                self.far_copy(kind, k).wait_send()


def plane_sum_scratch(half, width, kinds=3):
    return [
        pltpu.VMEM((8 * half, width), BF16),
        pltpu.VMEM((2 * half, width), BF16),
        pltpu.VMEM((2 * half, width), BF16),
        pltpu.VMEM((2 * half, width), BF16),
        pltpu.SemaphoreType.DMA((4 * HALF,)),
        pltpu.SemaphoreType.DMA((4 * HALF,)),
        pltpu.SemaphoreType.DMA((kinds, HALF)),
        pltpu.SemaphoreType.DMA((kinds, HALF)),
    ]


def any_spec():
    return pl.BlockSpec(memory_space=pl.ANY)


def vmem_spec():
    return pl.BlockSpec(memory_space=pltpu.VMEM)


def comm_params(collective_id):
    return pltpu.CompilerParams(
        collective_id=collective_id, has_side_effects=True, vmem_limit_bytes=VMEM_LIMIT
    )


def expert_body(
    flat,
    rows,
    parts,
    own_hbm,
    grad_hbm,
    scale_hbm,
    pick_ref,
    gate_hbm,
    up_hbm,
    down_hbm,
    total_ref,
    active_hbm,
    d_gate_hbm,
    d_up_hbm,
    d_down_hbm,
    held,
    grads,
    scales,
    both,
    down,
    grad_act,
    grad_both,
    active,
    d_weights,
    part,
    near,
    far,
    first,
    second,
    near_send,
    near_recv,
    sum_send,
    sum_recv,
    gather_send,
    gather_recv,
    local_sem,
    grad_sem,
    out_sem,
):
    r = roles()
    half = rows // HALF
    unit = 2 * half
    owners = slot_owner(r)
    loads = [
        pltpu.make_async_copy(own_hbm, held.at[pl.ds(0, rows)], local_sem.at[0]),
        pltpu.make_async_copy(gate_hbm, both.at[pl.ds(0, flat)], local_sem.at[1]),
        pltpu.make_async_copy(up_hbm, both.at[pl.ds(flat, flat)], local_sem.at[2]),
        pltpu.make_async_copy(down_hbm, down, local_sem.at[3]),
    ]
    for load in loads:
        load.start()
    slots = []
    for index, (owner, k) in enumerate(owners):
        slots.append(
            (
                pltpu.make_async_copy(
                    scale_hbm.at[pl.ds(owner * parts, parts), pl.ds(k * half, half)],
                    scales.at[index],
                    grad_sem.at[0, index],
                ),
                pltpu.make_async_copy(
                    grad_hbm.at[pl.ds(owner * rows + k * half, half)],
                    grads.at[pl.ds(index * half, half)],
                    grad_sem.at[1, index],
                ),
            )
        )
        for load in slots[-1]:
            load.start()
    greet([r["p"], r["a"], r["b"]], [])
    gather = PlaneGather(r, held, half, gather_send, gather_recv)
    loads[0].wait()
    gather.begin()
    for load in loads[1:]:
        load.wait()
    for pair in slots:
        for load in pair:
            load.wait()
    psum = PlaneSum(
        r, part, near, far, first, second, half, (near_send, near_recv, sum_send, sum_recv)
    )

    def expand(index):
        return jnp.concatenate(
            [dot_tn(scales[2 * index], pick_ref[...]), dot_tn(scales[2 * index + 1], pick_ref[...])],
            axis=0,
        )

    @pl.loop(0, 8)
    def _(index):
        at = pl.ds(pl.multiple_of(index * unit, unit), unit)
        grad_act[at, :] = dot_nt(grads[at, :], down[...]) * expand(index)

    @pl.loop(0, 8)
    def _(index):
        @pl.when(index == 1)
        def _():
            gather.arrived(2, 0)
            gather.arrived(2, 1)

        for k, first_unit in ((0, 2), (1, 4)):

            @pl.when(index == first_unit)
            def _():
                gather.pass_near(k)

            @pl.when(index == first_unit + 1)
            def _():
                gather.arrived(4, k)
                gather.arrived(5, k)

            @pl.when(index == 6 + k)
            def _():
                gather.pass_far(k)
                gather.arrived(6, k)

        at = pl.ds(pl.multiple_of(index * unit, unit), unit)
        pre = dot_nt(held[at, :], both[...])
        gate_pre, up_pre = pre[:, :flat], pre[:, flat:]
        grad_active = grad_act[at, :]
        sigmoid_gate = jax.nn.sigmoid(gate_pre)
        silu_gate = gate_pre * sigmoid_gate
        active[at, :] = (silu_gate * up_pre * expand(index)).astype(BF16)
        grad_both[at, flat:] = (grad_active * silu_gate).astype(BF16)
        grad_both[at, :flat] = (
            grad_active * up_pre * sigmoid_gate * (1.0 + gate_pre * (1.0 - sigmoid_gate))
        ).astype(BF16)
        part[at, :] = dot_nn(grad_both[at, :], both[...]).astype(BF16)

        @pl.when(index == 1)
        def _():
            psum.near_copy(0).start()
            psum.near_copy(1).start()

        for k, last_unit in ((0, 3), (1, 5)):

            @pl.when(index == last_unit)
            def _():
                psum.near_copy(2 + k).start()
                psum.near_copy(4 + k).start()

            @pl.when(index == last_unit + 1)
            def _():
                psum.pass_second(k)

            @pl.when(index == 6 + k)
            def _():
                psum.near_copy(6 + k).start()

    active_out = pltpu.make_async_copy(active, active_hbm, local_sem.at[0])
    active_out.start()
    psum.pass_far(0)
    psum.pass_far(1)
    group = 128
    pieces = flat // group

    def weight_piece(which, index):
        source, other, column = (
            (active, grads, 0),
            (grad_both, held, 0),
            (grad_both, held, flat),
        )[which]
        lanes = pl.ds(pl.multiple_of(column + index * group, group), group)
        place = pl.ds(pl.multiple_of(which * flat + index * group, group), group)
        d_weights[place, :] = dot_tn(source[:, lanes], other[...])

    def weight_out(which):
        target = (d_down_hbm, d_gate_hbm, d_up_hbm)[which]
        return pltpu.make_async_copy(
            d_weights.at[pl.ds(which * flat, flat)], target, out_sem.at[which]
        )

    @pl.loop(0, pieces)
    def _(index):
        weight_piece(0, index)

    weight_out(0).start()
    psum.pass_first(0)
    psum.pass_first(1)

    @pl.loop(0, 2 * pieces)
    def _(index):
        lanes = pl.ds(pl.multiple_of(index * group, group), group)
        place = pl.ds(pl.multiple_of(flat + index * group, group), group)
        d_weights[place, :] = dot_tn(grad_both[:, lanes], held[...])

    weight_out(1).start()
    weight_out(2).start()
    for k in range(HALF):
        total_ref[pl.ds(k * half, half), :] = psum.total(k).astype(BF16)
    active_out.wait()
    for which in range(3):
        weight_out(which).wait()
    gather.sent()
    psum.sent()


def expert_call(own, all_grad, scale_parts, pick, gate_matrix, up_matrix, down_matrix):
    rows, width = own.shape
    flat = gate_matrix.shape[0]
    everything = all_grad.shape[0]
    parts = pick.shape[0]
    half = rows // HALF
    f32_weight = jax.ShapeDtypeStruct((flat, width), F32)
    return pl.pallas_call(
        functools.partial(expert_body, flat, rows, parts),
        out_shape=(
            jax.ShapeDtypeStruct((rows, width), BF16),
            jax.ShapeDtypeStruct((everything, flat), BF16),
            f32_weight,
            f32_weight,
            f32_weight,
        ),
        in_specs=[any_spec(), any_spec(), any_spec(), vmem_spec()] + [any_spec()] * 3,
        out_specs=(vmem_spec(), any_spec(), any_spec(), any_spec(), any_spec()),
        scratch_shapes=[
            pltpu.VMEM((everything, width), BF16),
            pltpu.VMEM((everything, width), BF16),
            pltpu.VMEM((16, parts, half), BF16),
            pltpu.VMEM((2 * flat, width), BF16),
            pltpu.VMEM((flat, width), BF16),
            pltpu.VMEM((everything, flat), F32),
            pltpu.VMEM((everything, 2 * flat), BF16),
            pltpu.VMEM((everything, flat), BF16),
            pltpu.VMEM((3 * flat, width), F32),
            pltpu.VMEM((everything, width), BF16),
        ]
        + plane_sum_scratch(half, width)
        + [
            pltpu.SemaphoreType.DMA((PlaneGather.kinds, HALF)),
            pltpu.SemaphoreType.DMA((PlaneGather.kinds, HALF)),
            pltpu.SemaphoreType.DMA((4,)),
            pltpu.SemaphoreType.DMA((2, 16)),
            pltpu.SemaphoreType.DMA((3,)),
        ],
        compiler_params=comm_params(1),
        name="experts",
    )(own, all_grad, scale_parts, pick, gate_matrix, up_matrix, down_matrix)


class LineSum:
    def __init__(self, count, source, arrived, send, recv):
        self.count, self.source, self.arrived, self.send, self.recv = (
            count,
            source,
            arrived,
            send,
            recv,
        )
        self.z = lax.axis_index("tp")
        self.share = source.shape[1] // count

    def columns(self, z):
        return pl.ds(pl.multiple_of(z * self.share, self.share), self.share)

    def copy(self, j):
        target = (self.z + j) % self.count
        return send_to(
            self.source.at[:, self.columns(target)],
            self.arrived.at[j - 1],
            self.send.at[j - 1],
            self.recv.at[j - 1],
            tp=target,
        )

    def begin(self):
        for j in range(1, self.count):
            self.copy(j).start()

    def total(self):
        total = self.source[:, self.columns(self.z)].astype(F32)
        for j in range(1, self.count):
            self.copy(j).wait_recv()
            total = total + self.arrived[j - 1].astype(F32)
        return total

    def sent(self):
        for j in range(1, self.count):
            self.copy(j).wait_send()


class LineGather:
    def __init__(self, count, whole, send, recv):
        self.count, self.whole, self.send, self.recv = count, whole, send, recv
        self.z = lax.axis_index("tp")
        self.share = whole.shape[1] // count

    def columns(self, z):
        return pl.ds(pl.multiple_of(z * self.share, self.share), self.share)

    def copy(self, j):
        mine = self.whole.at[:, self.columns(self.z)]
        return send_to(
            mine, mine, self.send.at[j - 1], self.recv.at[j - 1], tp=(self.z + j) % self.count
        )

    def arrival(self, j):
        theirs = self.whole.at[:, self.columns((self.z + self.count - j) % self.count)]
        return send_to(
            theirs, theirs, self.send.at[j - 1], self.recv.at[j - 1], tp=(self.z + j) % self.count
        )

    def begin(self):
        for j in range(1, self.count):
            self.copy(j).start()

    def wait(self):
        for j in range(1, self.count):
            self.arrival(j).wait_recv()

    def sent(self):
        for j in range(1, self.count):
            self.copy(j).wait_send()


def line_peers(count):
    z = lax.axis_index("tp")
    return [(z + j) % count for j in range(1, count)]


def mix_body(
    tp_count,
    rows,
    partial_ref,
    active_ref,
    down_ref,
    grad_ref,
    mixed_ref,
    part,
    line,
    near,
    far,
    first,
    second,
    near_send,
    near_recv,
    sum_send,
    sum_recv,
    line_send,
    line_recv,
    back_send,
    back_recv,
):
    r = roles()
    half = rows // HALF
    unit = 2 * half
    greet([r["p"], r["a"], r["b"]], line_peers(tp_count))
    over_line = LineSum(tp_count, partial_ref, line, line_send, line_recv)
    over_line.begin()
    psum = PlaneSum(
        r, part, near, far, first, second, half, (near_send, near_recv, sum_send, sum_recv)
    )

    @pl.loop(0, 8)
    def _(step):
        index = (step + 6) % 8
        at = pl.ds(pl.multiple_of(index * unit, unit), unit)
        part[at, :] = dot_nn(active_ref[at, :], down_ref[...]).astype(BF16)
        for unit_done, copies in ((6, (6,)), (7, (7,)), (1, (0, 1)), (3, (2, 4)), (5, (3, 5))):

            @pl.when(index == unit_done)
            def _():
                for copy in copies:
                    psum.near_copy(copy).start()

    for k in range(HALF):
        psum.pass_far(k)
    for k in range(HALF):
        psum.pass_second(k)
    for k in range(HALF):
        psum.pass_first(k)
    back = LineGather(tp_count, grad_ref, back_send, back_recv)
    grad_ref[:, back.columns(back.z)] = over_line.total().astype(BF16)
    back.begin()
    for k in range(HALF):
        mixed_ref[pl.ds(k * half, half), :] = psum.total(k).astype(BF16)
    back.wait()
    over_line.sent()
    back.sent()
    psum.sent()


def mix_call(partial, active, down_matrix, tp_count):
    rows, width = partial.shape
    everything = active.shape[0]
    half = rows // HALF
    whole = jax.ShapeDtypeStruct((rows, width), BF16)
    line_sems = pltpu.SemaphoreType.DMA((tp_count - 1,))
    return pl.pallas_call(
        functools.partial(mix_body, tp_count, rows),
        out_shape=(whole, whole),
        in_specs=[vmem_spec()] * 3,
        out_specs=(vmem_spec(), vmem_spec()),
        scratch_shapes=[
            pltpu.VMEM((everything, width), BF16),
            pltpu.VMEM((tp_count - 1, rows, width // tp_count), BF16),
        ]
        + plane_sum_scratch(half, width)
        + [line_sems] * 4,
        compiler_params=comm_params(2),
        name="mix",
    )(partial, active, down_matrix)


def on_device(
    layer_in,
    token_order,
    seq_lengths,
    routes,
    route_weights,
    w_query,
    w_key,
    w_value,
    w_out,
    norm_attn,
    norm_moe,
    query_gain,
    key_gain,
    w_gate,
    w_up,
    w_down,
    grad_out,
):
    ep_count = lax.axis_size("ep")
    tp_count = lax.axis_size("tp")
    tp_index = lax.axis_index("tp")
    ep_index = lax.axis_index("ep")
    local_experts, hidden_here, model_width = w_gate.shape
    experts = local_experts * ep_count
    rows_dev = layer_in.shape[0]
    micro_rows = rows_dev // MICRO
    share_width = layer_in.shape[1]
    score_scale = HEAD_DIM ** (-0.5)
    planes = ep_count == 8 and tp_count == 4

    send, recv = deal_matrices(token_order, ep_index, rows_dev, ep_count)
    both = jnp.concatenate([layer_in, grad_out], axis=1)
    got = permute_rows(recv, exchange(permute_rows(send, both), ep_count))
    layer_full = lax.all_gather(got[:, :share_width], "tp", axis=1, tiled=True)
    grad_full = lax.all_gather(got[:, share_width:], "tp", axis=1, tiled=True)

    q_width, kv_width = w_query.shape[1], w_key.shape[1]
    packed = jnp.concatenate([w_query, w_out, w_key, w_value], axis=1)
    packed = lax.all_gather(packed, "ep", axis=0, tiled=True)
    full_query = packed[:, :q_width]
    full_out = packed[:, q_width : 2 * q_width]
    full_kv = packed[:, 2 * q_width :]
    gains = jnp.concatenate([norm_attn, norm_moe, query_gain, key_gain]).reshape(1, -1)
    gains = lax.all_gather(gains, "ep", axis=0, tiled=True).astype(F32)
    part = norm_attn.shape[0]
    head_part = query_gain.shape[0]
    gain_attn = gains[:, :part].reshape(-1)
    gain_moe = gains[:, part : 2 * part].reshape(-1)
    gain_query = gains[:, 2 * part : 2 * part + head_part].reshape(-1)
    gain_key = gains[:, 2 * part + head_part :].reshape(-1)

    expert_ids = jnp.arange(experts, dtype=jnp.int32)
    dense = jnp.sum(
        jnp.where(
            routes.T[None, :, :] == expert_ids[:, None, None], route_weights.T[None, :, :], 0.0
        ),
        axis=1,
    )
    terms = []
    for _ in range(SCALE_TERMS):
        terms.append(lax.reduce_precision(dense, 8, 7))
        dense = dense - terms[-1]
    scale_parts = jnp.concatenate(terms, axis=0).astype(BF16)
    scale_all = lax.all_gather(scale_parts, "ep", axis=0, tiled=True)
    flat_expert = ep_index * local_experts + jnp.repeat(
        jnp.arange(local_experts, dtype=jnp.int32), hidden_here
    )
    part_expert = jnp.arange(scale_parts.shape[0], dtype=jnp.int32) % experts
    pick = (part_expert[:, None] == flat_expert[None, :]).astype(BF16)
    all_grad = lax.all_gather(grad_full, "ep", axis=0, tiled=True)

    heads_here = q_width // HEAD_DIM
    kv_here = kv_width // HEAD_DIM
    group_size = heads_here // kv_here
    segment, position = jax.vmap(positions_of, in_axes=(0, None))(seq_lengths, micro_rows)
    cosine, sine_table = rope_tables(position.reshape(-1), HEAD_DIM // 2)
    layer_float = layer_full.astype(F32)
    inverse_one = inverse_rms(layer_float)
    unit_one = layer_float * inverse_one
    normed = (unit_one * gain_attn).astype(BF16)
    query_proj = dot_nn(normed, full_query).reshape(rows_dev, heads_here, HEAD_DIM)
    kv_proj = dot_nn(normed, full_kv)
    key_proj = kv_proj[:, :kv_width].reshape(rows_dev, kv_here, HEAD_DIM)
    value_proj = kv_proj[:, kv_width:].reshape(rows_dev, kv_here, HEAD_DIM)
    inverse_query = inverse_rms(query_proj)
    unit_query = query_proj * inverse_query
    inverse_key = inverse_rms(key_proj)
    unit_key = key_proj * inverse_key
    queries = (
        rotate(unit_query * gain_query, cosine, sine_table)
        .astype(BF16)
        .reshape(MICRO, micro_rows, kv_here, group_size, HEAD_DIM)
    )
    key_rows = (
        rotate(unit_key * gain_key, cosine, sine_table)
        .astype(BF16)
        .reshape(MICRO, micro_rows, kv_here, HEAD_DIM)
    )
    values = value_proj.astype(BF16).reshape(MICRO, micro_rows, kv_here, HEAD_DIM)
    scores = (
        jnp.einsum("mqkgd,mtkd->mkgqt", queries, key_rows, preferred_element_type=F32)
        * score_scale
    )
    offsets = jnp.arange(micro_rows, dtype=jnp.int32)
    allowed = (segment[:, :, None] == segment[:, None, :]) & (
        offsets[None, None, :] <= offsets[None, :, None]
    )
    scores = jnp.where(allowed[:, None, None], scores, -1e30)
    row_peak = jnp.max(scores, axis=-1, keepdims=True)
    exponent = jnp.exp(scores - row_peak)
    attn_probs = exponent / jnp.sum(exponent, axis=-1, keepdims=True)
    probs_low = attn_probs.astype(BF16)
    context = jnp.einsum("mkgqt,mtkd->mqkgd", probs_low, values, preferred_element_type=F32)
    context_low = context.reshape(rows_dev, heads_here * HEAD_DIM).astype(BF16)
    attn_part = dot_nt(context_low, full_out)
    attn_out = lax.psum(attn_part.astype(BF16), "tp").astype(F32)
    hidden = layer_float + attn_out
    inverse_two = inverse_rms(hidden)
    unit_two = hidden * inverse_two
    moe_in = (unit_two * gain_moe).astype(BF16)

    flat = local_experts * hidden_here
    gate_matrix = w_gate.reshape(flat, model_width)
    up_matrix = w_up.reshape(flat, model_width)
    down_matrix = w_down.reshape(flat, model_width)
    if planes:
        grad_partial, active, grad_w_gate, grad_w_up, grad_w_down = expert_call(
            moe_in, all_grad, scale_all, pick, gate_matrix, up_matrix, down_matrix
        )
        grad_moe_in, mixed_plane = mix_call(grad_partial, active, down_matrix, tp_count)
        mixed = lax.psum_scatter(mixed_plane, "tp", scatter_dimension=1, tiled=True)
    else:
        all_in = lax.all_gather(moe_in, "ep", axis=0, tiled=True)
        parts_all = scale_all.reshape(ep_count, pick.shape[0], rows_dev)
        row_scale = lax.dot_general(
            parts_all, pick, (((1,), (0,)), ((), ())), preferred_element_type=F32
        ).reshape(ep_count * rows_dev, flat)
        gate_pre = dot_nt(all_in, gate_matrix)
        up_pre = dot_nt(all_in, up_matrix)
        grad_active = dot_nt(all_grad, down_matrix) * row_scale
        sigmoid_gate = jax.nn.sigmoid(gate_pre)
        silu_gate = gate_pre * sigmoid_gate
        active = (silu_gate * up_pre * row_scale).astype(BF16)
        grad_up_pre = (grad_active * silu_gate).astype(BF16)
        grad_gate_pre = (
            grad_active * up_pre * sigmoid_gate * (1.0 + gate_pre * (1.0 - sigmoid_gate))
        ).astype(BF16)
        grad_partial = dot_nn(grad_gate_pre, gate_matrix) + dot_nn(grad_up_pre, up_matrix)
        grad_partial = lax.psum_scatter(
            grad_partial.astype(BF16), "ep", scatter_dimension=0, tiled=True
        )
        grad_share = lax.psum_scatter(grad_partial, "tp", scatter_dimension=1, tiled=True)
        grad_moe_in = lax.all_gather(grad_share, "tp", axis=1, tiled=True)
        out_partial = dot_nn(active, down_matrix)
        out_partial = lax.psum_scatter(
            out_partial.astype(BF16), "ep", scatter_dimension=0, tiled=True
        )
        mixed = lax.psum_scatter(out_partial, "tp", scatter_dimension=1, tiled=True)
        grad_w_down = dot_tn(active, all_grad)
        grad_w_gate = dot_tn(grad_gate_pre, all_in)
        grad_w_up = dot_tn(grad_up_pre, all_in)
    hidden_share = lax.dynamic_slice_in_dim(hidden, tp_index * share_width, share_width, 1)
    layer_dealt = (hidden_share + mixed.astype(F32)).astype(BF16)

    grad_float = grad_full.astype(F32)
    grad_moe_in = grad_moe_in.astype(F32)
    norm_moe_part = jnp.sum(grad_moe_in * unit_two, axis=0)
    grad_hidden = grad_float + norm_back(grad_moe_in * gain_moe, unit_two, inverse_two)
    grad_attn = grad_hidden.astype(BF16)
    grad_w_out = dot_tn(grad_attn, context_low)
    grad_context = (
        dot_nn(grad_attn, full_out)
        .astype(BF16)
        .reshape(MICRO, micro_rows, kv_here, group_size, HEAD_DIM)
    )
    grad_probs = jnp.einsum("mqkgd,mtkd->mkgqt", grad_context, values, preferred_element_type=F32)
    prob_delta = jnp.sum(attn_probs * grad_probs, axis=-1, keepdims=True)
    grad_scores = (attn_probs * (grad_probs - prob_delta)).astype(BF16)
    grad_queries = (
        jnp.einsum("mkgqt,mtkd->mqkgd", grad_scores, key_rows, preferred_element_type=F32).reshape(
            rows_dev, heads_here, HEAD_DIM
        )
        * score_scale
    )
    grad_keys = (
        jnp.einsum("mkgqt,mqkgd->mtkd", grad_scores, queries, preferred_element_type=F32).reshape(
            rows_dev, kv_here, HEAD_DIM
        )
        * score_scale
    )
    grad_values = jnp.einsum(
        "mkgqt,mqkgd->mtkd", probs_low, grad_context, preferred_element_type=F32
    )
    grad_unit_query = rotate_back(grad_queries, cosine, sine_table)
    grad_unit_key = rotate_back(grad_keys, cosine, sine_table)
    query_gain_part = jnp.sum(grad_unit_query * unit_query, axis=(0, 1))
    key_gain_part = jnp.sum(grad_unit_key * unit_key, axis=(0, 1))
    grad_query_proj = (
        norm_back(grad_unit_query * gain_query, unit_query, inverse_query)
        .reshape(rows_dev, heads_here * HEAD_DIM)
        .astype(BF16)
    )
    grad_key_proj = (
        norm_back(grad_unit_key * gain_key, unit_key, inverse_key)
        .reshape(rows_dev, kv_width)
        .astype(BF16)
    )
    grad_value_proj = grad_values.reshape(rows_dev, kv_width).astype(BF16)
    grad_kv_proj = jnp.concatenate([grad_key_proj, grad_value_proj], axis=1)
    normed_part = dot_nt(grad_query_proj, full_query) + dot_nt(grad_kv_proj, full_kv)
    grad_normed = lax.psum_scatter(
        normed_part.astype(BF16), "tp", scatter_dimension=1, tiled=True
    ).astype(F32)
    grad_packed = jnp.concatenate(
        [
            dot_tn(normed, grad_query_proj).astype(BF16),
            grad_w_out.astype(BF16),
            dot_tn(normed, grad_kv_proj).astype(BF16),
        ],
        axis=1,
    )
    grad_packed = lax.psum_scatter(grad_packed, "ep", scatter_dimension=0, tiled=True).astype(F32)

    start = tp_index * share_width
    gain_share = lax.dynamic_slice_in_dim(gain_attn, start, share_width, 0)
    unit_share = lax.dynamic_slice_in_dim(unit_one, start, share_width, 1)
    hidden_grad_share = lax.dynamic_slice_in_dim(grad_hidden, start, share_width, 1)
    scaled = grad_normed * gain_share
    row_mean = lax.psum(jnp.sum(scaled * unit_share, axis=1), "tp") / model_width
    grad_layer = hidden_grad_share + inverse_one * (scaled - unit_share * row_mean[:, None])
    norm_attn_part = lax.dynamic_update_slice_in_dim(
        jnp.zeros((model_width,), F32), jnp.sum(grad_normed * unit_share, axis=0), start, 0
    )
    small = jnp.concatenate(
        [norm_attn_part, norm_moe_part / tp_count, query_gain_part, key_gain_part]
    )
    small = lax.psum(small, ("ep", "tp"))
    grad_norm_attn = lax.dynamic_slice_in_dim(small, ep_index * part, part, 0)
    grad_norm_moe = lax.dynamic_slice_in_dim(small, model_width + ep_index * part, part, 0)
    grad_query_gain = lax.dynamic_slice_in_dim(
        small, 2 * model_width + ep_index * head_part, head_part, 0
    )
    grad_key_gain = lax.dynamic_slice_in_dim(
        small, 2 * model_width + HEAD_DIM + ep_index * head_part, head_part, 0
    )

    back = jnp.concatenate([layer_dealt, grad_layer.astype(BF16)], axis=1)
    home = exchange(dot_tn(recv, back).astype(BF16), ep_count)
    home = dot_tn(send, home)
    return (
        home[:, :share_width].astype(BF16),
        home[:, share_width:],
        grad_packed[:, :q_width],
        grad_packed[:, 2 * q_width : 2 * q_width + kv_width],
        grad_packed[:, 2 * q_width + kv_width :],
        grad_packed[:, q_width : 2 * q_width],
        grad_norm_attn,
        grad_norm_moe,
        grad_query_gain,
        grad_key_gain,
        grad_w_gate.reshape(w_gate.shape),
        grad_w_up.reshape(w_up.shape),
        grad_w_down.reshape(w_down.shape),
    )


def solution(mesh):
    return jax.shard_map(
        on_device,
        mesh=mesh,
        in_specs=(
            P("ep", "tp"),
            P(),
            P("ep", None),
            P("ep", None),
            P("ep", None),
            P("ep", "tp"),
            P("ep", "tp"),
            P("ep", "tp"),
            P("ep", "tp"),
            P("ep"),
            P("ep"),
            P("ep"),
            P("ep"),
            P("ep", "tp", None),
            P("ep", "tp", None),
            P("ep", "tp", None),
            P("ep", "tp"),
        ),
        out_specs=(
            P("ep", "tp"),
            P("ep", "tp"),
            P("ep", "tp"),
            P("ep", "tp"),
            P("ep", "tp"),
            P("ep", "tp"),
            P("ep"),
            P("ep"),
            P("ep"),
            P("ep"),
            P("ep", "tp", None),
            P("ep", "tp", None),
            P("ep", "tp", None),
        ),
        check_vma=False,
    )
```

```python
import functools

import jax
import jax.numpy as jnp
from jax import lax
from jax.experimental import pallas as pl
from jax.experimental.pallas import tpu as pltpu
from jax.sharding import PartitionSpec as P

HEAD_DIM = 128
MICRO = 2
F32 = jnp.float32
BF16 = jnp.bfloat16
SCALE_TERMS = 3
VMEM_LIMIT = 66 * 1000 * 1000

epsilon = 1e-06
rope_base = 1000000.0


def positions_of(lengths, row_count):
    offsets = jnp.arange(row_count, dtype=jnp.int32)
    seq_ends = jnp.cumsum(lengths)
    segment = jnp.sum((offsets[:, None] >= seq_ends[None, :]).astype(jnp.int32), axis=1)
    starts = seq_ends - lengths
    in_segment = segment[:, None] == jnp.arange(lengths.shape[0], dtype=jnp.int32)[None, :]
    position = offsets - jnp.sum(jnp.where(in_segment, starts[None, :], 0), axis=1)
    return (segment, position)


def rope_tables(position, half_dim):
    frequency = rope_base ** (-jnp.arange(half_dim, dtype=F32) / half_dim)
    angles = position.astype(F32)[:, None] * frequency[None, :]
    return (jnp.cos(angles)[:, None, :], jnp.sin(angles)[:, None, :])


def rotate(values, cosine, sine_table):
    half_dim = values.shape[-1] // 2
    first_half = values[..., :half_dim]
    second_half = values[..., half_dim:]
    return jnp.concatenate(
        [
            first_half * cosine - second_half * sine_table,
            second_half * cosine + first_half * sine_table,
        ],
        axis=-1,
    )


def rotate_back(incoming, cosine, sine_table):
    return rotate(incoming, cosine, -sine_table)


def deal_matrices(token_order, ep_index, rows_dev, ep_count):
    per_pair = rows_dev // ep_count
    rows = jnp.arange(rows_dev, dtype=jnp.int32)
    home = ep_index * rows_dev + rows
    at = jnp.arange(token_order.shape[0], dtype=jnp.int32)
    place = jnp.sum(jnp.where(token_order[None, :] == home[:, None], at[None, :], 0), axis=1)
    dest = place // rows_dev
    rank = jnp.sum(
        ((dest[:, None] == dest[None, :]) & (place[None, :] < place[:, None])).astype(jnp.int32),
        axis=1,
    )
    send_slot = dest * per_pair + rank
    send = (send_slot[None, :] == rows[:, None]).astype(BF16)
    mine = lax.dynamic_slice_in_dim(token_order, ep_index * rows_dev, rows_dev, 0)
    source = mine // rows_dev
    my_rank = jnp.sum(
        ((source[:, None] == source[None, :]) & (rows[None, :] < rows[:, None])).astype(jnp.int32),
        axis=1,
    )
    recv_slot = source * per_pair + my_rank
    recv = (recv_slot[:, None] == rows[None, :]).astype(BF16)
    return (send, recv)


def inverse_rms(values):
    return lax.rsqrt(jnp.mean(values * values, axis=-1, keepdims=True) + epsilon)


def norm_back(grad_unit, unit_values, inverse):
    return inverse * (
        grad_unit - unit_values * jnp.mean(grad_unit * unit_values, axis=-1, keepdims=True)
    )


def dot_nn(left, right):
    return jnp.dot(left, right, preferred_element_type=F32)


def dot_tn(left_rows, right_rows):
    return lax.dot_general(
        left_rows, right_rows, (((0,), (0,)), ((), ())), preferred_element_type=F32
    )


def dot_nt(left_rows, right_matrix):
    return lax.dot_general(
        left_rows, right_matrix, (((1,), (1,)), ((), ())), preferred_element_type=F32
    )


def permute_rows(matrix, rows):
    return dot_nn(matrix, rows).astype(BF16)


def exchange(rows, ep_count):
    split = rows.reshape(ep_count, rows.shape[0] // ep_count, rows.shape[1])
    moved = lax.all_to_all(split, "ep", split_axis=0, concat_axis=0, tiled=True)
    return moved.reshape(rows.shape)


MESH_ID = pl.DeviceIdType.MESH
HALF = 2
E0, E1, P0, P1, A0, B0, PA0, PB0, A1, B1, PA1, PB1, D0, PD0, D1, PD1 = range(16)
SLOT_E, SLOT_P, SLOT_A, SLOT_B = (E0, E1), (P0, P1), (A0, A1), (B0, B1)
SLOT_D, SLOT_PA, SLOT_PB, SLOT_PD = (D0, D1), (PA0, PA1), (PB0, PB1), (PD0, PD1)
FOR_PARTNER = (P0, P1, PB0, PB1, PA0, PA1, PD0, PD1)


def roles():
    e = lax.axis_index("ep")
    core, x, y = e % 2, (e // 2) % 2, e // 4
    other = 1 - 2 * core
    over_x, over_y = e + 2 - 4 * x, e + 4 - 8 * y
    a = over_x * (1 - core) + over_y * core
    b = over_y * (1 - core) + over_x * core
    d = over_x + over_y - e
    return dict(e=e, p=e + other, a=a, b=b, d=d, pa=a + other, pb=b + other, pd=d + other)


def slot_owner(r):
    names = ("e", "e", "p", "p", "a", "b", "pa", "pb", "a", "b", "pa", "pb", "d", "pd", "d", "pd")
    halves = (0, 1, 0, 1, 0, 0, 0, 0, 1, 1, 1, 1, 0, 0, 1, 1)
    return [(r[name], half) for name, half in zip(names, halves)]


def greet(plane, line):
    barrier = pltpu.get_barrier_semaphore()
    for device in plane:
        pl.semaphore_signal(barrier, inc=1, device_id={"ep": device}, device_id_type=MESH_ID)
    for device in line:
        pl.semaphore_signal(barrier, inc=1, device_id={"tp": device}, device_id_type=MESH_ID)
    pl.semaphore_wait(barrier, len(plane) + len(line))


def send_to(src, dst, send_sem, recv_sem, **device):
    return pltpu.make_async_remote_copy(
        src_ref=src,
        dst_ref=dst,
        send_sem=send_sem,
        recv_sem=recv_sem,
        device_id=device,
        device_id_type=MESH_ID,
    )


class PlaneGather:
    kinds = 7

    def __init__(self, r, held, half, send, recv):
        self.r, self.held, self.half, self.send, self.recv = r, held, half, send, recv

    def slot(self, index):
        return self.held.at[pl.ds(index * self.half, self.half)]

    def copy(self, kind, k):
        source, target, device = (
            (SLOT_E, SLOT_A, "a"),
            (SLOT_E, SLOT_B, "b"),
            (SLOT_E, SLOT_P, "p"),
            (SLOT_A, SLOT_D, "b"),
            (SLOT_A, SLOT_PB, "p"),
            (SLOT_B, SLOT_PA, "p"),
            (SLOT_D, SLOT_PD, "p"),
        )[kind]
        return send_to(
            self.slot(source[k]),
            self.slot(target[k]),
            self.send.at[kind, k],
            self.recv.at[kind, k],
            ep=self.r[device],
        )

    def begin(self):
        for k in range(HALF):
            for kind in range(3):
                self.copy(kind, k).start()

    def arrived(self, kind, k):
        self.copy(kind, k).wait_recv()

    def pass_near(self, k):
        self.arrived(0, k)
        self.copy(3, k).start()
        self.copy(4, k).start()
        self.arrived(1, k)
        self.copy(5, k).start()

    def pass_far(self, k):
        self.arrived(3, k)
        self.copy(6, k).start()

    def sent(self):
        for k in range(HALF):
            for kind in range(self.kinds):
                self.copy(kind, k).wait_send()


class PlaneSum:
    def __init__(self, r, part, near, far, first, second, half, sems):
        self.r, self.part, self.half = r, part, half
        self.near, self.far, self.first, self.second = near, far, first, second
        self.near_send, self.near_recv, self.send, self.recv = sems

    def slot(self, index):
        return self.part.at[pl.ds(index * self.half, self.half)]

    def rows(self, buffer, index):
        return buffer.at[pl.ds(index * self.half, self.half)]

    def near_copy(self, index):
        return send_to(
            self.slot(FOR_PARTNER[index]),
            self.rows(self.near, index),
            self.near_send.at[index],
            self.near_recv.at[index],
            ep=self.r["p"],
        )

    def far_copy(self, kind, k):
        source, target, device = (
            (SLOT_D, self.far, "b"),
            (SLOT_A, self.first, "a"),
            (SLOT_B, self.second, "b"),
        )[kind]
        return send_to(
            self.slot(source[k]),
            self.rows(target, k),
            self.send.at[kind, k],
            self.recv.at[kind, k],
            ep=self.r[device],
        )

    def add_up(self, slot, others):
        total = self.slot(slot)[...].astype(F32)
        for other in others:
            total = total + other[...].astype(F32)
        return total

    def near_sum(self, name, k):
        index = 2 * name + k
        slot = (SLOT_E, SLOT_A, SLOT_B, SLOT_D)[name][k]
        self.near_copy(index).wait_recv()
        return slot, [self.rows(self.near, index)]

    def pass_far(self, k):
        slot, others = self.near_sum(3, k)
        self.slot(slot)[...] = self.add_up(slot, others).astype(BF16)
        self.far_copy(0, k).start()

    def pass_second(self, k):
        slot, others = self.near_sum(2, k)
        self.slot(slot)[...] = self.add_up(slot, others).astype(BF16)
        self.far_copy(2, k).start()

    def pass_first(self, k):
        slot, others = self.near_sum(1, k)
        self.far_copy(0, k).wait_recv()
        self.slot(slot)[...] = self.add_up(slot, others + [self.rows(self.far, k)]).astype(BF16)
        self.far_copy(1, k).start()

    def total(self, k):
        slot, others = self.near_sum(0, k)
        self.far_copy(1, k).wait_recv()
        self.far_copy(2, k).wait_recv()
        return self.add_up(slot, others + [self.rows(self.first, k), self.rows(self.second, k)])

    def sent(self):
        for index in range(4 * HALF):
            self.near_copy(index).wait_send()
        for kind in range(3):
            for k in range(HALF):
                self.far_copy(kind, k).wait_send()


def plane_sum_scratch(half, width, kinds=3):
    return [
        pltpu.VMEM((8 * half, width), BF16),
        pltpu.VMEM((2 * half, width), BF16),
        pltpu.VMEM((2 * half, width), BF16),
        pltpu.VMEM((2 * half, width), BF16),
        pltpu.SemaphoreType.DMA((4 * HALF,)),
        pltpu.SemaphoreType.DMA((4 * HALF,)),
        pltpu.SemaphoreType.DMA((kinds, HALF)),
        pltpu.SemaphoreType.DMA((kinds, HALF)),
    ]


def any_spec():
    return pl.BlockSpec(memory_space=pl.ANY)


def vmem_spec():
    return pl.BlockSpec(memory_space=pltpu.VMEM)


def comm_params(collective_id):
    return pltpu.CompilerParams(
        collective_id=collective_id, has_side_effects=True, vmem_limit_bytes=VMEM_LIMIT
    )


def expert_body(
    flat,
    rows,
    parts,
    own_hbm,
    grad_hbm,
    scale_hbm,
    pick_ref,
    gate_hbm,
    up_hbm,
    down_hbm,
    total_ref,
    active_hbm,
    d_gate_hbm,
    d_up_hbm,
    d_down_hbm,
    held,
    grads,
    scales,
    both,
    down,
    grad_act,
    grad_both,
    active,
    d_weights,
    part,
    near,
    far,
    first,
    second,
    near_send,
    near_recv,
    sum_send,
    sum_recv,
    gather_send,
    gather_recv,
    local_sem,
    grad_sem,
    out_sem,
):
    r = roles()
    half = rows // HALF
    unit = 2 * half
    owners = slot_owner(r)
    loads = [
        pltpu.make_async_copy(own_hbm, held.at[pl.ds(0, rows)], local_sem.at[0]),
        pltpu.make_async_copy(gate_hbm, both.at[pl.ds(0, flat)], local_sem.at[1]),
        pltpu.make_async_copy(up_hbm, both.at[pl.ds(flat, flat)], local_sem.at[2]),
        pltpu.make_async_copy(down_hbm, down, local_sem.at[3]),
    ]
    for load in loads:
        load.start()
    stride = scale_hbm.shape[0] // 8
    slots = []
    for index, (owner, k) in enumerate(owners):
        slots.append(
            (
                pltpu.make_async_copy(
                    scale_hbm.at[pl.ds(owner * stride, parts), pl.ds(k * half, half)],
                    scales.at[index],
                    grad_sem.at[0, index],
                ),
                pltpu.make_async_copy(
                    grad_hbm.at[pl.ds(owner * rows + k * half, half)],
                    grads.at[pl.ds(index * half, half)],
                    grad_sem.at[1, index],
                ),
            )
        )
        for load in slots[-1]:
            load.start()
    greet([r["p"], r["a"], r["b"]], [])
    gather = PlaneGather(r, held, half, gather_send, gather_recv)
    loads[0].wait()
    gather.begin()
    for load in loads[1:]:
        load.wait()
    for pair in slots:
        for load in pair:
            load.wait()
    psum = PlaneSum(
        r, part, near, far, first, second, half, (near_send, near_recv, sum_send, sum_recv)
    )

    def expand(index):
        return jnp.concatenate(
            [dot_tn(scales[2 * index], pick_ref[...]), dot_tn(scales[2 * index + 1], pick_ref[...])],
            axis=0,
        )

    @pl.loop(0, 8)
    def _(index):
        at = pl.ds(pl.multiple_of(index * unit, unit), unit)
        grad_act[at, :] = dot_nt(grads[at, :], down[...]) * expand(index)

    @pl.loop(0, 8)
    def _(index):
        @pl.when(index == 1)
        def _():
            gather.arrived(2, 0)
            gather.arrived(2, 1)

        for k, first_unit in ((0, 2), (1, 4)):

            @pl.when(index == first_unit)
            def _():
                gather.pass_near(k)

            @pl.when(index == first_unit + 1)
            def _():
                gather.arrived(4, k)
                gather.arrived(5, k)

            @pl.when(index == 6 + k)
            def _():
                gather.pass_far(k)
                gather.arrived(6, k)

        at = pl.ds(pl.multiple_of(index * unit, unit), unit)
        pre = dot_nt(held[at, :], both[...])
        gate_pre, up_pre = pre[:, :flat], pre[:, flat:]
        grad_active = grad_act[at, :]
        sigmoid_gate = jax.nn.sigmoid(gate_pre)
        silu_gate = gate_pre * sigmoid_gate
        active[at, :] = (silu_gate * up_pre * expand(index)).astype(BF16)
        grad_both[at, flat:] = (grad_active * silu_gate).astype(BF16)
        grad_both[at, :flat] = (
            grad_active * up_pre * sigmoid_gate * (1.0 + gate_pre * (1.0 - sigmoid_gate))
        ).astype(BF16)
        part[at, :] = dot_nn(grad_both[at, :], both[...]).astype(BF16)

        @pl.when(index == 1)
        def _():
            psum.near_copy(0).start()
            psum.near_copy(1).start()

        for k, last_unit in ((0, 3), (1, 5)):

            @pl.when(index == last_unit)
            def _():
                psum.near_copy(2 + k).start()
                psum.near_copy(4 + k).start()

            @pl.when(index == last_unit + 1)
            def _():
                psum.pass_second(k)

            @pl.when(index == 6 + k)
            def _():
                psum.near_copy(6 + k).start()

    active_out = pltpu.make_async_copy(active, active_hbm, local_sem.at[0])
    active_out.start()
    psum.pass_far(0)
    psum.pass_far(1)
    group = 128
    pieces = flat // group

    def weight_piece(which, index):
        source, other, column = (
            (active, grads, 0),
            (grad_both, held, 0),
            (grad_both, held, flat),
        )[which]
        lanes = pl.ds(pl.multiple_of(column + index * group, group), group)
        place = pl.ds(pl.multiple_of(which * flat + index * group, group), group)
        d_weights[place, :] = dot_tn(source[:, lanes], other[...])

    def weight_out(which):
        target = (d_down_hbm, d_gate_hbm, d_up_hbm)[which]
        return pltpu.make_async_copy(
            d_weights.at[pl.ds(which * flat, flat)], target, out_sem.at[which]
        )

    @pl.loop(0, pieces)
    def _(index):
        weight_piece(0, index)

    weight_out(0).start()
    psum.pass_first(0)
    psum.pass_first(1)

    @pl.loop(0, 2 * pieces)
    def _(index):
        lanes = pl.ds(pl.multiple_of(index * group, group), group)
        place = pl.ds(pl.multiple_of(flat + index * group, group), group)
        d_weights[place, :] = dot_tn(grad_both[:, lanes], held[...])

    weight_out(1).start()
    weight_out(2).start()
    for k in range(HALF):
        total_ref[pl.ds(k * half, half), :] = psum.total(k).astype(BF16)
    active_out.wait()
    for which in range(3):
        weight_out(which).wait()
    gather.sent()
    psum.sent()


def expert_call(own, all_grad, scale_parts, pick, gate_matrix, up_matrix, down_matrix):
    rows, width = own.shape
    flat = gate_matrix.shape[0]
    everything = all_grad.shape[0]
    parts = pick.shape[0]
    half = rows // HALF
    f32_weight = jax.ShapeDtypeStruct((flat, width), F32)
    return pl.pallas_call(
        functools.partial(expert_body, flat, rows, parts),
        out_shape=(
            jax.ShapeDtypeStruct((rows, width), BF16),
            jax.ShapeDtypeStruct((everything, flat), BF16),
            f32_weight,
            f32_weight,
            f32_weight,
        ),
        in_specs=[any_spec(), any_spec(), any_spec(), vmem_spec()] + [any_spec()] * 3,
        out_specs=(vmem_spec(), any_spec(), any_spec(), any_spec(), any_spec()),
        scratch_shapes=[
            pltpu.VMEM((everything, width), BF16),
            pltpu.VMEM((everything, width), BF16),
            pltpu.VMEM((16, parts, half), BF16),
            pltpu.VMEM((2 * flat, width), BF16),
            pltpu.VMEM((flat, width), BF16),
            pltpu.VMEM((everything, flat), F32),
            pltpu.VMEM((everything, 2 * flat), BF16),
            pltpu.VMEM((everything, flat), BF16),
            pltpu.VMEM((3 * flat, width), F32),
            pltpu.VMEM((everything, width), BF16),
        ]
        + plane_sum_scratch(half, width)
        + [
            pltpu.SemaphoreType.DMA((PlaneGather.kinds, HALF)),
            pltpu.SemaphoreType.DMA((PlaneGather.kinds, HALF)),
            pltpu.SemaphoreType.DMA((4,)),
            pltpu.SemaphoreType.DMA((2, 16)),
            pltpu.SemaphoreType.DMA((3,)),
        ],
        compiler_params=comm_params(1),
        name="experts",
    )(own, all_grad, scale_parts, pick, gate_matrix, up_matrix, down_matrix)


class LineSum:
    def __init__(self, count, source, arrived, send, recv):
        self.count, self.source, self.arrived, self.send, self.recv = (
            count,
            source,
            arrived,
            send,
            recv,
        )
        self.z = lax.axis_index("tp")
        self.share = source.shape[1] // count

    def columns(self, z):
        return pl.ds(pl.multiple_of(z * self.share, self.share), self.share)

    def copy(self, j):
        target = (self.z + j) % self.count
        return send_to(
            self.source.at[:, self.columns(target)],
            self.arrived.at[j - 1],
            self.send.at[j - 1],
            self.recv.at[j - 1],
            tp=target,
        )

    def begin(self):
        for j in range(1, self.count):
            self.copy(j).start()

    def total(self):
        total = self.source[:, self.columns(self.z)].astype(F32)
        for j in range(1, self.count):
            self.copy(j).wait_recv()
            total = total + self.arrived[j - 1].astype(F32)
        return total

    def sent(self):
        for j in range(1, self.count):
            self.copy(j).wait_send()


class OrderedGather(PlaneGather):
    def place(self, name, k):
        return self.held.at[pl.ds((self.r[name] * HALF + k) * self.half, self.half)]

    def copy(self, kind, k):
        source, device = (
            ("e", "a"),
            ("e", "b"),
            ("e", "p"),
            ("a", "b"),
            ("a", "p"),
            ("b", "p"),
            ("d", "p"),
        )[kind]
        block = self.place(source, k)
        return send_to(
            block, block, self.send.at[kind, k], self.recv.at[kind, k], ep=self.r[device]
        )

    def arrived(self, kind, k):
        source, device = (
            ("a", "a"),
            ("b", "b"),
            ("p", "p"),
            ("d", "b"),
            ("pb", "p"),
            ("pa", "p"),
            ("pd", "p"),
        )[kind]
        block = self.place(source, k)
        send_to(
            block, block, self.send.at[kind, k], self.recv.at[kind, k], ep=self.r[device]
        ).wait_recv()

    def finish(self):
        for k in range(HALF):
            for kind in (2, 4, 5, 6):
                self.arrived(kind, k)


class LineGather:
    def __init__(self, count, whole, up_send, up_recv, down_send, down_recv):
        self.count, self.whole = count, whole
        self.up_sems, self.down_sems = (up_send, up_recv), (down_send, down_recv)
        self.z = lax.axis_index("tp")
        self.share = whole.shape[1] // count

    def columns(self, z):
        return pl.ds(pl.multiple_of(z * self.share, self.share), self.share)

    def move(self, share, j, sems, target):
        block = self.whole.at[:, self.columns(share)]
        return send_to(block, block, sems[0].at[j - 1], sems[1].at[j - 1], tp=target)

    def up(self, j):
        return self.move(self.z - j + 1, j, self.up_sems, self.z + 1)

    def down(self, j):
        return self.move(self.z + j - 1, j, self.down_sems, self.z - 1)

    def sends(self, j, act):
        @pl.when((self.z < self.count - 1) & (self.z >= j - 1))
        def _():
            act(self.up(j))

        @pl.when((self.z > 0) & (self.z + j <= self.count))
        def _():
            act(self.down(j))

    def begin(self):
        self.sends(1, lambda copy: copy.start())

    def step(self, j):
        @pl.when(self.z >= j)
        def _():
            self.move(self.z - j, j, self.up_sems, self.z - 1).wait_recv()

        @pl.when(self.z + j < self.count)
        def _():
            self.move(self.z + j, j, self.down_sems, self.z + 1).wait_recv()

        if j + 1 < self.count:
            self.sends(j + 1, lambda copy: copy.start())

    def wait(self):
        for j in range(1, self.count):
            self.step(j)

    def sent(self):
        for j in range(1, self.count):
            self.sends(j, lambda copy: copy.wait_send())


def line_peers(count):
    z = lax.axis_index("tp")
    return [(z + j) % count for j in range(1, count)]


def mix_body(
    tp_count,
    rows,
    partial_ref,
    active_ref,
    down_ref,
    grad_ref,
    mixed_ref,
    part,
    line,
    near,
    far,
    first,
    second,
    near_send,
    near_recv,
    sum_send,
    sum_recv,
    line_send,
    line_recv,
    back_line,
):
    r = roles()
    half = rows // HALF
    unit = 2 * half
    greet([r["p"], r["a"], r["b"]], line_peers(tp_count))
    over_line = LineSum(tp_count, partial_ref, line, line_send, line_recv)
    over_line.begin()
    psum = PlaneSum(
        r, part, near, far, first, second, half, (near_send, near_recv, sum_send, sum_recv)
    )

    @pl.loop(0, 8)
    def _(step):
        index = (step + 6) % 8
        at = pl.ds(pl.multiple_of(index * unit, unit), unit)
        part[at, :] = dot_nn(active_ref[at, :], down_ref[...]).astype(BF16)
        for unit_done, copies in ((6, (6,)), (7, (7,)), (1, (0, 1)), (3, (2, 4)), (5, (3, 5))):

            @pl.when(index == unit_done)
            def _():
                for copy in copies:
                    psum.near_copy(copy).start()

    for k in range(HALF):
        psum.pass_far(k)
    for k in range(HALF):
        psum.pass_second(k)
    for k in range(HALF):
        psum.pass_first(k)
    back = LineGather(tp_count, grad_ref, *[back_line.at[i] for i in range(4)])
    grad_ref[:, back.columns(back.z)] = over_line.total().astype(BF16)
    back.begin()
    back.step(1)
    back.step(2)
    for k in range(HALF):
        mixed_ref[pl.ds(k * half, half), :] = psum.total(k).astype(BF16)
    back.step(3)
    over_line.sent()
    back.sent()
    psum.sent()


def mix_call(partial, active, down_matrix, tp_count):
    rows, width = partial.shape
    everything = active.shape[0]
    half = rows // HALF
    whole = jax.ShapeDtypeStruct((rows, width), BF16)
    line_sems = pltpu.SemaphoreType.DMA((tp_count - 1,))
    return pl.pallas_call(
        functools.partial(mix_body, tp_count, rows),
        out_shape=(whole, whole),
        in_specs=[vmem_spec()] * 3,
        out_specs=(vmem_spec(), vmem_spec()),
        scratch_shapes=[
            pltpu.VMEM((everything, width), BF16),
            pltpu.VMEM((tp_count - 1, rows, width // tp_count), BF16),
        ]
        + plane_sum_scratch(half, width)
        + [line_sems] * 2
        + [pltpu.SemaphoreType.DMA((4, tp_count - 1))],
        compiler_params=comm_params(2),
        name="mix",
    )(partial, active, down_matrix)


def turn(values, cosine, sine_table):
    return values * cosine + pltpu.roll(values, HEAD_DIM // 2, 1) * sine_table


def unit_of(values):
    return values * lax.rsqrt(jnp.mean(values * values, axis=-1, keepdims=True) + epsilon)


def front_body(
    gain_at,
    ep_count,
    tp_count,
    rows,
    heads,
    send_ref,
    recv_ref,
    small_ref,
    cosine_ref,
    sine_ref,
    mask_ref,
    query_hbm,
    key_hbm,
    value_hbm,
    out_hbm,
    x_ref,
    grad_ref,
    hidden_ref,
    moe_ref,
    proj_ref,
    turned_ref,
    keys_ref,
    values_ref,
    probs_ref,
    context_ref,
    small_all,
    normed,
    all_grad,
    w_in_hbm,
    w_out_hbm,
    w_in,
    w_out,
    dealt,
    x_wire,
    grad_wire,
    back_wire,
    attn,
    line,
    deal_send,
    deal_recv,
    small_send,
    small_recv,
    in_send,
    in_recv,
    out_send,
    out_recv,
    grad_send,
    grad_recv,
    x_line,
    grad_line,
    back_line,
    line_send,
    line_recv,
    local_sem,
):
    r = roles()
    e = r["e"]
    z = lax.axis_index("tp")
    half = rows // HALF
    q_width = heads * HEAD_DIM
    share = x_wire.shape[1] // tp_count
    per_pair = rows // ep_count
    micro_rows = rows // MICRO
    own = pl.ds(e * rows, rows)
    loads = [
        pltpu.make_async_copy(query_hbm, w_in.at[own, pl.ds(0, q_width)], local_sem.at[0]),
        pltpu.make_async_copy(key_hbm, w_in.at[own, pl.ds(q_width, HEAD_DIM)], local_sem.at[1]),
        pltpu.make_async_copy(
            value_hbm, w_in.at[own, pl.ds(q_width + HEAD_DIM, HEAD_DIM)], local_sem.at[2]
        ),
        pltpu.make_async_copy(out_hbm, w_out.at[own], local_sem.at[3]),
    ]
    for load in loads:
        load.start()
    small_rows = small_ref.shape[0]
    small_all[pl.ds(e * small_rows, small_rows), :] = small_ref[...]
    others = [(e + j) % ep_count for j in range(1, ep_count)]
    greet(others, line_peers(tp_count))

    def deal(j, source, target):
        return send_to(
            send_ref.at[pl.ds(target * per_pair, per_pair)],
            dealt.at[pl.ds(source * per_pair, per_pair)],
            deal_send.at[j - 1],
            deal_recv.at[j - 1],
            ep=target,
        )

    for j in range(1, ep_count):
        deal(j, e, (e + j) % ep_count).start()
    mine = pl.ds(pl.multiple_of(e * per_pair, per_pair), per_pair)
    dealt[mine, :] = send_ref[mine, :]
    gather_small = OrderedGather(r, small_all, small_rows // HALF, small_send, small_recv)
    gather_in = OrderedGather(r, w_in, half, in_send, in_recv)
    gather_out = OrderedGather(r, w_out, half, out_send, out_recv)
    gather_grad = OrderedGather(r, all_grad, half, grad_send, grad_recv)
    gather_small.begin()
    for load in loads:
        load.wait()
    gather_in.begin()
    for j in range(1, ep_count):
        deal(j, (e + ep_count - j) % ep_count, (e + j) % ep_count).wait_recv()
    x_gather = LineGather(tp_count, x_wire, *[x_line.at[i] for i in range(4)])
    grad_gather = LineGather(tp_count, grad_wire, *[grad_line.at[i] for i in range(4)])
    x_wire[:, x_gather.columns(z)] = dealt[:, :share]
    grad_wire[:, x_gather.columns(z)] = dealt[:, share:]
    x_gather.begin()
    for k in range(HALF):
        gather_small.pass_near(k)
    x_gather.step(1)
    gather_in.pass_near(0)
    x_gather.step(2)
    grad_gather.begin()
    gather_in.pass_near(1)
    gather_out.begin()
    x_gather.step(3)
    for k in range(HALF):
        gather_small.pass_far(k)
    gather_small.finish()

    def gain_row(place, column, width):
        at = place * small_rows + gain_at
        return small_all[at : at + 1, column : column + width].astype(F32)

    x_rows = dot_nn(recv_ref[...], x_wire[...])
    x_ref[...] = x_rows.astype(BF16)
    unit_one = unit_of(x_rows)
    for place in range(ep_count):
        at = slice(place * rows, (place + 1) * rows)
        normed[:, at] = (unit_one[:, at] * gain_row(place, 0, rows)).astype(BF16)
    for k in range(HALF):
        gather_in.pass_far(k)
    grad_gather.step(1)
    gather_in.finish()
    gather_out.pass_near(0)

    proj_ref[...] = dot_nn(normed[...], w_in[...])
    grad_gather.step(2)
    gather_out.pass_near(1)
    column = 2 * rows
    gain_query = sum(gain_row(place, column, HEAD_DIM) for place in range(ep_count))
    gain_key = sum(gain_row(place, column + HEAD_DIM, HEAD_DIM) for place in range(ep_count))
    cosine, sine_table = cosine_ref[...], sine_ref[...]
    keys_ref[...] = turn(
        unit_of(proj_ref[:, q_width : q_width + HEAD_DIM]) * gain_key, cosine, sine_table
    ).astype(BF16)
    values_ref[...] = proj_ref[:, q_width + HEAD_DIM :].astype(BF16)

    @pl.loop(0, heads)
    def _(head):
        lanes = pl.ds(pl.multiple_of(head * HEAD_DIM, HEAD_DIM), HEAD_DIM)
        queries = turn(unit_of(proj_ref[:, lanes]) * gain_query, cosine, sine_table).astype(BF16)
        for micro in range(MICRO):
            at = pl.ds(
                pl.multiple_of((micro * heads + head) * micro_rows, micro_rows), micro_rows
            )
            turned_ref[at, :] = queries[micro * micro_rows : (micro + 1) * micro_rows]

    grad_gather.step(3)
    for micro in range(MICRO):
        within = slice(micro * micro_rows, (micro + 1) * micro_rows)
        stacked = slice(micro * heads * micro_rows, (micro + 1) * heads * micro_rows)
        scores = dot_nt(turned_ref[stacked, :], keys_ref[within, :]) * HEAD_DIM ** (-0.5)
        mask = mask_ref[within, :]
        scores = scores.reshape(heads, micro_rows, micro_rows)
        scores = jnp.where(mask[None] > 0.0, scores, -1e30)
        exponent = jnp.exp(scores - jnp.max(scores, axis=-1, keepdims=True))
        probs = exponent / jnp.sum(exponent, axis=-1, keepdims=True)
        probs = probs.reshape(heads * micro_rows, micro_rows)
        probs_ref[stacked, :] = probs
        context = dot_nn(probs.astype(BF16), values_ref[within, :]).astype(BF16)
        for head in range(heads):
            context_ref[within, head * HEAD_DIM : (head + 1) * HEAD_DIM] = context[
                head * micro_rows : (head + 1) * micro_rows
            ]

    grad_ref[...] = dot_nn(recv_ref[...], grad_wire[...]).astype(BF16)
    grad_here = pltpu.make_async_copy(grad_ref, all_grad.at[own], local_sem.at[4])
    grad_here.start()
    for k in range(HALF):
        gather_out.pass_far(k)
    grad_here.wait()
    gather_grad.begin()
    gather_out.finish()

    attn[...] = dot_nt(context_ref[...], w_out[...]).astype(BF16)
    over_line = LineSum(tp_count, attn, line, line_send, line_recv)
    over_line.begin()
    w_in_out = pltpu.make_async_copy(w_in, w_in_hbm, local_sem.at[0])
    w_out_out = pltpu.make_async_copy(w_out, w_out_hbm, local_sem.at[1])
    w_in_out.start()
    w_out_out.start()
    gather_grad.pass_near(0)
    total = over_line.total()
    back = LineGather(tp_count, back_wire, *[back_line.at[i] for i in range(4)])
    back_wire[:, back.columns(z)] = total.astype(BF16)
    back.begin()
    back.step(1)
    gather_grad.pass_near(1)
    back.step(2)
    gather_grad.pass_far(0)
    back.step(3)
    hidden = x_ref[...].astype(F32) + back_wire[...].astype(F32)
    hidden_ref[...] = hidden
    unit_two = unit_of(hidden)
    for place in range(ep_count):
        at = slice(place * rows, (place + 1) * rows)
        moe_ref[:, at] = (unit_two[:, at] * gain_row(place, rows, rows)).astype(BF16)
    gather_grad.pass_far(1)
    gather_grad.finish()
    for j in range(1, ep_count):
        deal(j, e, (e + j) % ep_count).wait_send()
    x_gather.sent()
    grad_gather.sent()
    back.sent()
    over_line.sent()
    for gather in (gather_small, gather_in, gather_out, gather_grad):
        gather.sent()
    w_in_out.wait()
    w_out_out.wait()


def front_call(
    gain_at, ep_count, tp_count, send_rows, recv, small, cosine, sine_table, mask, query, key, value, out
):
    rows = send_rows.shape[0]
    share = send_rows.shape[1] // 2
    width = share * tp_count
    q_width = query.shape[1]
    heads = q_width // HEAD_DIM
    everything = rows * ep_count
    in_width = q_width + 2 * HEAD_DIM
    micro_rows = rows // MICRO
    shape = jax.ShapeDtypeStruct
    gather_sems = pltpu.SemaphoreType.DMA((PlaneGather.kinds, HALF))
    line_sems = pltpu.SemaphoreType.DMA((4, tp_count - 1))
    return pl.pallas_call(
        functools.partial(front_body, gain_at, ep_count, tp_count, rows, heads),
        out_shape=(
            shape((rows, width), BF16),
            shape((rows, width), BF16),
            shape((rows, width), F32),
            shape((rows, width), BF16),
            shape((rows, in_width), F32),
            shape((heads * rows, HEAD_DIM), BF16),
            shape((rows, HEAD_DIM), BF16),
            shape((rows, HEAD_DIM), BF16),
            shape((heads * rows, micro_rows), F32),
            shape((rows, q_width), BF16),
            shape((ep_count * small.shape[0], small.shape[1]), BF16),
            shape((rows, width), BF16),
            shape((everything, width), BF16),
            shape((everything, in_width), BF16),
            shape((everything, q_width), BF16),
        ),
        in_specs=[vmem_spec()] * 6 + [any_spec()] * 4,
        out_specs=tuple([vmem_spec()] * 12 + [any_spec()] * 3),
        scratch_shapes=[
            pltpu.VMEM((everything, in_width), BF16),
            pltpu.VMEM((everything, q_width), BF16),
            pltpu.VMEM(send_rows.shape, BF16),
            pltpu.VMEM((rows, width), BF16),
            pltpu.VMEM((rows, width), BF16),
            pltpu.VMEM((rows, width), BF16),
            pltpu.VMEM((rows, width), BF16),
            pltpu.VMEM((tp_count - 1, rows, share), BF16),
            pltpu.SemaphoreType.DMA((ep_count - 1,)),
            pltpu.SemaphoreType.DMA((ep_count - 1,)),
        ]
        + [gather_sems] * 8
        + [line_sems] * 3
        + [pltpu.SemaphoreType.DMA((tp_count - 1,))] * 2
        + [pltpu.SemaphoreType.DMA((5,))],
        compiler_params=comm_params(3),
        name="front",
    )(send_rows, recv, small, cosine, sine_table, mask, query, key, value, out)


def plain_layer(
    layer_in,
    token_order,
    seq_lengths,
    routes,
    route_weights,
    w_query,
    w_key,
    w_value,
    w_out,
    norm_attn,
    norm_moe,
    query_gain,
    key_gain,
    w_gate,
    w_up,
    w_down,
    grad_out,
):
    ep_count = lax.axis_size("ep")
    tp_count = lax.axis_size("tp")
    tp_index = lax.axis_index("tp")
    ep_index = lax.axis_index("ep")
    local_experts, hidden_here, model_width = w_gate.shape
    experts = local_experts * ep_count
    rows_dev = layer_in.shape[0]
    micro_rows = rows_dev // MICRO
    share_width = layer_in.shape[1]
    score_scale = HEAD_DIM ** (-0.5)

    send, recv = deal_matrices(token_order, ep_index, rows_dev, ep_count)
    both = jnp.concatenate([layer_in, grad_out], axis=1)
    got = permute_rows(recv, exchange(permute_rows(send, both), ep_count))
    layer_full = lax.all_gather(got[:, :share_width], "tp", axis=1, tiled=True)
    grad_full = lax.all_gather(got[:, share_width:], "tp", axis=1, tiled=True)

    q_width, kv_width = w_query.shape[1], w_key.shape[1]
    packed = jnp.concatenate([w_query, w_out, w_key, w_value], axis=1)
    packed = lax.all_gather(packed, "ep", axis=0, tiled=True)
    full_query = packed[:, :q_width]
    full_out = packed[:, q_width : 2 * q_width]
    full_kv = packed[:, 2 * q_width :]
    gains = jnp.concatenate([norm_attn, norm_moe, query_gain, key_gain]).reshape(1, -1)
    gains = lax.all_gather(gains, "ep", axis=0, tiled=True).astype(F32)
    part = norm_attn.shape[0]
    head_part = query_gain.shape[0]
    gain_attn = gains[:, :part].reshape(-1)
    gain_moe = gains[:, part : 2 * part].reshape(-1)
    gain_query = gains[:, 2 * part : 2 * part + head_part].reshape(-1)
    gain_key = gains[:, 2 * part + head_part :].reshape(-1)

    expert_ids = jnp.arange(experts, dtype=jnp.int32)
    dense = jnp.sum(
        jnp.where(routes[:, :, None] == expert_ids[None, None, :], route_weights[:, :, None], 0.0),
        axis=1,
    )
    scale_all = lax.all_gather(dense, "ep", axis=0, tiled=True)
    scale = lax.dynamic_slice_in_dim(scale_all, ep_index * local_experts, local_experts, 1)
    all_grad = lax.all_gather(grad_full, "ep", axis=0, tiled=True)

    heads_here = q_width // HEAD_DIM
    kv_here = kv_width // HEAD_DIM
    group_size = heads_here // kv_here
    segment, position = jax.vmap(positions_of, in_axes=(0, None))(seq_lengths, micro_rows)
    cosine, sine_table = rope_tables(position.reshape(-1), HEAD_DIM // 2)
    layer_float = layer_full.astype(F32)
    inverse_one = inverse_rms(layer_float)
    unit_one = layer_float * inverse_one
    normed = (unit_one * gain_attn).astype(BF16)
    query_proj = dot_nn(normed, full_query).reshape(rows_dev, heads_here, HEAD_DIM)
    kv_proj = dot_nn(normed, full_kv)
    key_proj = kv_proj[:, :kv_width].reshape(rows_dev, kv_here, HEAD_DIM)
    value_proj = kv_proj[:, kv_width:].reshape(rows_dev, kv_here, HEAD_DIM)
    inverse_query = inverse_rms(query_proj)
    unit_query = query_proj * inverse_query
    inverse_key = inverse_rms(key_proj)
    unit_key = key_proj * inverse_key
    queries = (
        rotate(unit_query * gain_query, cosine, sine_table)
        .astype(BF16)
        .reshape(MICRO, micro_rows, kv_here, group_size, HEAD_DIM)
    )
    key_rows = (
        rotate(unit_key * gain_key, cosine, sine_table)
        .astype(BF16)
        .reshape(MICRO, micro_rows, kv_here, HEAD_DIM)
    )
    values = value_proj.astype(BF16).reshape(MICRO, micro_rows, kv_here, HEAD_DIM)
    scores = (
        jnp.einsum("mqkgd,mtkd->mkgqt", queries, key_rows, preferred_element_type=F32)
        * score_scale
    )
    offsets = jnp.arange(micro_rows, dtype=jnp.int32)
    allowed = (segment[:, :, None] == segment[:, None, :]) & (
        offsets[None, None, :] <= offsets[None, :, None]
    )
    scores = jnp.where(allowed[:, None, None], scores, -1e30)
    row_peak = jnp.max(scores, axis=-1, keepdims=True)
    exponent = jnp.exp(scores - row_peak)
    attn_probs = exponent / jnp.sum(exponent, axis=-1, keepdims=True)
    probs_low = attn_probs.astype(BF16)
    context = jnp.einsum("mkgqt,mtkd->mqkgd", probs_low, values, preferred_element_type=F32)
    context_low = context.reshape(rows_dev, heads_here * HEAD_DIM).astype(BF16)
    attn_part = dot_nt(context_low, full_out)
    attn_out = lax.psum(attn_part.astype(BF16), "tp").astype(F32)
    hidden = layer_float + attn_out
    inverse_two = inverse_rms(hidden)
    unit_two = hidden * inverse_two
    moe_in = (unit_two * gain_moe).astype(BF16)

    all_in = lax.all_gather(moe_in, "ep", axis=0, tiled=True)
    flat = local_experts * hidden_here
    gate_matrix = w_gate.reshape(flat, model_width)
    up_matrix = w_up.reshape(flat, model_width)
    down_matrix = w_down.reshape(flat, model_width)
    row_scale = jnp.repeat(scale, hidden_here, axis=1)
    gate_pre = dot_nt(all_in, gate_matrix)
    up_pre = dot_nt(all_in, up_matrix)
    grad_active = dot_nt(all_grad, down_matrix) * row_scale
    sigmoid_gate = jax.nn.sigmoid(gate_pre)
    silu_gate = gate_pre * sigmoid_gate
    active = (silu_gate * up_pre * row_scale).astype(BF16)
    grad_up_pre = (grad_active * silu_gate).astype(BF16)
    grad_gate_pre = (
        grad_active * up_pre * sigmoid_gate * (1.0 + gate_pre * (1.0 - sigmoid_gate))
    ).astype(BF16)
    grad_partial = dot_nn(grad_gate_pre, gate_matrix) + dot_nn(grad_up_pre, up_matrix)
    grad_partial = lax.psum_scatter(
        grad_partial.astype(BF16), "ep", scatter_dimension=0, tiled=True
    )
    grad_share = lax.psum_scatter(grad_partial, "tp", scatter_dimension=1, tiled=True)
    out_partial = dot_nn(active, down_matrix)
    out_partial = lax.psum_scatter(out_partial.astype(BF16), "ep", scatter_dimension=0, tiled=True)
    mixed = lax.psum_scatter(out_partial, "tp", scatter_dimension=1, tiled=True)
    hidden_share = lax.dynamic_slice_in_dim(hidden, tp_index * share_width, share_width, 1)
    layer_dealt = (hidden_share + mixed.astype(F32)).astype(BF16)
    grad_w_down = dot_tn(active, all_grad).reshape(w_down.shape)
    grad_w_gate = dot_tn(grad_gate_pre, all_in).reshape(w_gate.shape)
    grad_w_up = dot_tn(grad_up_pre, all_in).reshape(w_up.shape)

    grad_float = grad_full.astype(F32)
    grad_moe_in = lax.all_gather(grad_share, "tp", axis=1, tiled=True).astype(F32)
    norm_moe_part = jnp.sum(grad_moe_in * unit_two, axis=0)
    grad_hidden = grad_float + norm_back(grad_moe_in * gain_moe, unit_two, inverse_two)
    grad_attn = grad_hidden.astype(BF16)
    grad_w_out = dot_tn(grad_attn, context_low)
    grad_context = (
        dot_nn(grad_attn, full_out)
        .astype(BF16)
        .reshape(MICRO, micro_rows, kv_here, group_size, HEAD_DIM)
    )
    grad_probs = jnp.einsum("mqkgd,mtkd->mkgqt", grad_context, values, preferred_element_type=F32)
    prob_delta = jnp.sum(attn_probs * grad_probs, axis=-1, keepdims=True)
    grad_scores = (attn_probs * (grad_probs - prob_delta)).astype(BF16)
    grad_queries = (
        jnp.einsum("mkgqt,mtkd->mqkgd", grad_scores, key_rows, preferred_element_type=F32).reshape(
            rows_dev, heads_here, HEAD_DIM
        )
        * score_scale
    )
    grad_keys = (
        jnp.einsum("mkgqt,mqkgd->mtkd", grad_scores, queries, preferred_element_type=F32).reshape(
            rows_dev, kv_here, HEAD_DIM
        )
        * score_scale
    )
    grad_values = jnp.einsum(
        "mkgqt,mqkgd->mtkd", probs_low, grad_context, preferred_element_type=F32
    )
    grad_unit_query = rotate_back(grad_queries, cosine, sine_table)
    grad_unit_key = rotate_back(grad_keys, cosine, sine_table)
    query_gain_part = jnp.sum(grad_unit_query * unit_query, axis=(0, 1))
    key_gain_part = jnp.sum(grad_unit_key * unit_key, axis=(0, 1))
    grad_query_proj = (
        norm_back(grad_unit_query * gain_query, unit_query, inverse_query)
        .reshape(rows_dev, heads_here * HEAD_DIM)
        .astype(BF16)
    )
    grad_key_proj = (
        norm_back(grad_unit_key * gain_key, unit_key, inverse_key)
        .reshape(rows_dev, kv_width)
        .astype(BF16)
    )
    grad_value_proj = grad_values.reshape(rows_dev, kv_width).astype(BF16)
    grad_kv_proj = jnp.concatenate([grad_key_proj, grad_value_proj], axis=1)
    normed_part = dot_nt(grad_query_proj, full_query) + dot_nt(grad_kv_proj, full_kv)
    grad_normed = lax.psum_scatter(
        normed_part.astype(BF16), "tp", scatter_dimension=1, tiled=True
    ).astype(F32)
    grad_packed = jnp.concatenate(
        [
            dot_tn(normed, grad_query_proj).astype(BF16),
            grad_w_out.astype(BF16),
            dot_tn(normed, grad_kv_proj).astype(BF16),
        ],
        axis=1,
    )
    grad_packed = lax.psum_scatter(grad_packed, "ep", scatter_dimension=0, tiled=True).astype(F32)

    start = tp_index * share_width
    gain_share = lax.dynamic_slice_in_dim(gain_attn, start, share_width, 0)
    unit_share = lax.dynamic_slice_in_dim(unit_one, start, share_width, 1)
    hidden_grad_share = lax.dynamic_slice_in_dim(grad_hidden, start, share_width, 1)
    scaled = grad_normed * gain_share
    row_mean = lax.psum(jnp.sum(scaled * unit_share, axis=1), "tp") / model_width
    grad_layer = hidden_grad_share + inverse_one * (scaled - unit_share * row_mean[:, None])
    norm_attn_part = lax.dynamic_update_slice_in_dim(
        jnp.zeros((model_width,), F32), jnp.sum(grad_normed * unit_share, axis=0), start, 0
    )
    small = jnp.concatenate(
        [norm_attn_part, norm_moe_part / tp_count, query_gain_part, key_gain_part]
    )
    small = lax.psum(small, ("ep", "tp"))
    grad_norm_attn = lax.dynamic_slice_in_dim(small, ep_index * part, part, 0)
    grad_norm_moe = lax.dynamic_slice_in_dim(small, model_width + ep_index * part, part, 0)
    grad_query_gain = lax.dynamic_slice_in_dim(
        small, 2 * model_width + ep_index * head_part, head_part, 0
    )
    grad_key_gain = lax.dynamic_slice_in_dim(
        small, 2 * model_width + HEAD_DIM + ep_index * head_part, head_part, 0
    )

    back = jnp.concatenate([layer_dealt, grad_layer.astype(BF16)], axis=1)
    home = exchange(dot_tn(recv, back).astype(BF16), ep_count)
    home = dot_tn(send, home)
    return (
        home[:, :share_width].astype(BF16),
        home[:, share_width:],
        grad_packed[:, :q_width],
        grad_packed[:, 2 * q_width : 2 * q_width + kv_width],
        grad_packed[:, 2 * q_width + kv_width :],
        grad_packed[:, q_width : 2 * q_width],
        grad_norm_attn,
        grad_norm_moe,
        grad_query_gain,
        grad_key_gain,
        grad_w_gate,
        grad_w_up,
        grad_w_down,
    )


def route_scales(routes, route_weights, experts, local_experts, hidden_here, ep_index):
    expert_ids = jnp.arange(experts, dtype=jnp.int32)
    dense = jnp.sum(
        jnp.where(
            routes.T[None, :, :] == expert_ids[:, None, None], route_weights.T[None, :, :], 0.0
        ),
        axis=1,
    )
    terms = []
    for _ in range(SCALE_TERMS):
        terms.append(lax.reduce_precision(dense, 8, 7))
        dense = dense - terms[-1]
    parts = jnp.concatenate(terms, axis=0).astype(BF16)
    flat_expert = ep_index * local_experts + jnp.repeat(
        jnp.arange(local_experts, dtype=jnp.int32), hidden_here
    )
    part_expert = jnp.arange(parts.shape[0], dtype=jnp.int32) % experts
    return (parts, (part_expert[:, None] == flat_expert[None, :]).astype(BF16))


def plane_layer(
    layer_in,
    token_order,
    seq_lengths,
    routes,
    route_weights,
    w_query,
    w_key,
    w_value,
    w_out,
    norm_attn,
    norm_moe,
    query_gain,
    key_gain,
    w_gate,
    w_up,
    w_down,
    grad_out,
):
    ep_count = lax.axis_size("ep")
    tp_count = lax.axis_size("tp")
    tp_index = lax.axis_index("tp")
    ep_index = lax.axis_index("ep")
    local_experts, hidden_here, model_width = w_gate.shape
    experts = local_experts * ep_count
    rows_dev = layer_in.shape[0]
    micro_rows = rows_dev // MICRO
    share_width = layer_in.shape[1]
    score_scale = HEAD_DIM ** (-0.5)

    q_width, kv_width = w_query.shape[1], w_key.shape[1]
    heads_here = q_width // HEAD_DIM
    kv_here = kv_width // HEAD_DIM
    group_size = heads_here // kv_here
    send, recv = deal_matrices(token_order, ep_index, rows_dev, ep_count)
    send_rows = permute_rows(send, jnp.concatenate([layer_in, grad_out], axis=1))
    part = norm_attn.shape[0]
    head_part = query_gain.shape[0]
    scale_parts, pick = route_scales(
        routes, route_weights, experts, local_experts, hidden_here, ep_index
    )
    gain_at = scale_parts.shape[0]
    gains = jnp.zeros((1, 2 * part + 2 * HEAD_DIM), BF16)
    for vector, at in (
        (norm_attn, 0),
        (norm_moe, part),
        (query_gain, 2 * part + ep_index * head_part),
        (key_gain, 2 * part + HEAD_DIM + ep_index * head_part),
    ):
        gains = lax.dynamic_update_slice(gains, vector[None], (0, at))
    small_rows = -(-(gain_at + 1) // 32) * 32
    small = jnp.pad(scale_parts, ((0, 0), (0, gains.shape[1] - scale_parts.shape[1])))
    small = jnp.pad(
        jnp.concatenate([small, gains], axis=0), ((0, small_rows - gain_at - 1), (0, 0))
    )
    segment, position = jax.vmap(positions_of, in_axes=(0, None))(seq_lengths, micro_rows)
    cosine, sine_table = rope_tables(position.reshape(-1), HEAD_DIM // 2)
    cosine_wide = jnp.concatenate([cosine[:, 0], cosine[:, 0]], axis=1)
    sine_wide = jnp.concatenate([-sine_table[:, 0], sine_table[:, 0]], axis=1)
    offsets = jnp.arange(micro_rows, dtype=jnp.int32)
    allowed = (segment[:, :, None] == segment[:, None, :]) & (
        offsets[None, None, :] <= offsets[None, :, None]
    )
    mask = allowed.astype(F32).reshape(rows_dev, micro_rows)
    (
        layer_full,
        grad_full,
        hidden,
        moe_in,
        proj,
        turned,
        key_flat,
        value_flat,
        probs,
        context_low,
        small_all,
        normed,
        all_grad,
        w_in_all,
        full_out,
    ) = front_call(
        gain_at,
        ep_count,
        tp_count,
        send_rows,
        recv,
        small,
        cosine_wide,
        sine_wide,
        mask,
        w_query,
        w_key,
        w_value,
        w_out,
    )

    flat = local_experts * hidden_here
    gate_matrix = w_gate.reshape(flat, model_width)
    up_matrix = w_up.reshape(flat, model_width)
    down_matrix = w_down.reshape(flat, model_width)
    grad_partial, active, grad_w_gate, grad_w_up, grad_w_down = expert_call(
        moe_in, all_grad, small_all, pick, gate_matrix, up_matrix, down_matrix
    )
    grad_moe_in, mixed_plane = mix_call(grad_partial, active, down_matrix, tp_count)
    mixed = lax.psum_scatter(mixed_plane, "tp", scatter_dimension=1, tiled=True)
    hidden_share = lax.dynamic_slice_in_dim(hidden, tp_index * share_width, share_width, 1)
    layer_dealt = (hidden_share + mixed.astype(F32)).astype(BF16)

    gain_rows = small_all.reshape(ep_count, small_rows, -1)[:, gain_at].astype(F32)
    gain_attn = gain_rows[:, :part].reshape(-1)
    gain_moe = gain_rows[:, part : 2 * part].reshape(-1)
    gain_query = jnp.sum(gain_rows[:, 2 * part : 2 * part + HEAD_DIM], axis=0)
    gain_key = jnp.sum(gain_rows[:, 2 * part + HEAD_DIM :], axis=0)
    full_query, full_kv = w_in_all[:, :q_width], w_in_all[:, q_width:]
    layer_float = layer_full.astype(F32)
    inverse_one = inverse_rms(layer_float)
    unit_one = layer_float * inverse_one
    inverse_two = inverse_rms(hidden)
    unit_two = hidden * inverse_two
    query_proj = proj[:, :q_width].reshape(rows_dev, heads_here, HEAD_DIM)
    key_proj = proj[:, q_width : q_width + kv_width].reshape(rows_dev, kv_here, HEAD_DIM)
    inverse_query = inverse_rms(query_proj)
    unit_query = query_proj * inverse_query
    inverse_key = inverse_rms(key_proj)
    unit_key = key_proj * inverse_key
    attn_probs = probs.reshape(MICRO, kv_here, group_size, micro_rows, micro_rows)
    probs_low = attn_probs.astype(BF16)
    queries = jnp.transpose(
        turned.reshape(MICRO, kv_here, group_size, micro_rows, HEAD_DIM), (0, 3, 1, 2, 4)
    )
    key_rows = key_flat.reshape(MICRO, micro_rows, kv_here, HEAD_DIM)
    values = value_flat.reshape(MICRO, micro_rows, kv_here, HEAD_DIM)

    grad_float = grad_full.astype(F32)
    grad_moe_in = grad_moe_in.astype(F32)
    norm_moe_part = jnp.sum(grad_moe_in * unit_two, axis=0)
    grad_hidden = grad_float + norm_back(grad_moe_in * gain_moe, unit_two, inverse_two)
    grad_attn = grad_hidden.astype(BF16)
    grad_w_out = dot_tn(grad_attn, context_low)
    grad_context = (
        dot_nn(grad_attn, full_out)
        .astype(BF16)
        .reshape(MICRO, micro_rows, kv_here, group_size, HEAD_DIM)
    )
    grad_probs = jnp.einsum("mqkgd,mtkd->mkgqt", grad_context, values, preferred_element_type=F32)
    prob_delta = jnp.sum(attn_probs * grad_probs, axis=-1, keepdims=True)
    grad_scores = (attn_probs * (grad_probs - prob_delta)).astype(BF16)
    grad_queries = (
        jnp.einsum("mkgqt,mtkd->mqkgd", grad_scores, key_rows, preferred_element_type=F32).reshape(
            rows_dev, heads_here, HEAD_DIM
        )
        * score_scale
    )
    grad_keys = (
        jnp.einsum("mkgqt,mqkgd->mtkd", grad_scores, queries, preferred_element_type=F32).reshape(
            rows_dev, kv_here, HEAD_DIM
        )
        * score_scale
    )
    grad_values = jnp.einsum(
        "mkgqt,mqkgd->mtkd", probs_low, grad_context, preferred_element_type=F32
    )
    grad_unit_query = rotate_back(grad_queries, cosine, sine_table)
    grad_unit_key = rotate_back(grad_keys, cosine, sine_table)
    query_gain_part = jnp.sum(grad_unit_query * unit_query, axis=(0, 1))
    key_gain_part = jnp.sum(grad_unit_key * unit_key, axis=(0, 1))
    grad_query_proj = (
        norm_back(grad_unit_query * gain_query, unit_query, inverse_query)
        .reshape(rows_dev, heads_here * HEAD_DIM)
        .astype(BF16)
    )
    grad_key_proj = (
        norm_back(grad_unit_key * gain_key, unit_key, inverse_key)
        .reshape(rows_dev, kv_width)
        .astype(BF16)
    )
    grad_value_proj = grad_values.reshape(rows_dev, kv_width).astype(BF16)
    grad_kv_proj = jnp.concatenate([grad_key_proj, grad_value_proj], axis=1)
    normed_part = dot_nt(grad_query_proj, full_query) + dot_nt(grad_kv_proj, full_kv)
    grad_normed = lax.psum_scatter(
        normed_part.astype(BF16), "tp", scatter_dimension=1, tiled=True
    ).astype(F32)
    grad_packed = jnp.concatenate(
        [
            dot_tn(normed, grad_query_proj).astype(BF16),
            grad_w_out.astype(BF16),
            dot_tn(normed, grad_kv_proj).astype(BF16),
        ],
        axis=1,
    )
    grad_packed = lax.psum_scatter(grad_packed, "ep", scatter_dimension=0, tiled=True).astype(F32)

    start = tp_index * share_width
    gain_share = lax.dynamic_slice_in_dim(gain_attn, start, share_width, 0)
    unit_share = lax.dynamic_slice_in_dim(unit_one, start, share_width, 1)
    hidden_grad_share = lax.dynamic_slice_in_dim(grad_hidden, start, share_width, 1)
    scaled = grad_normed * gain_share
    row_mean = lax.psum(jnp.sum(scaled * unit_share, axis=1), "tp") / model_width
    grad_layer = hidden_grad_share + inverse_one * (scaled - unit_share * row_mean[:, None])
    norm_attn_part = lax.dynamic_update_slice_in_dim(
        jnp.zeros((model_width,), F32), jnp.sum(grad_normed * unit_share, axis=0), start, 0
    )
    small = jnp.concatenate(
        [norm_attn_part, norm_moe_part / tp_count, query_gain_part, key_gain_part]
    )
    small = lax.psum(small, ("ep", "tp"))
    grad_norm_attn = lax.dynamic_slice_in_dim(small, ep_index * part, part, 0)
    grad_norm_moe = lax.dynamic_slice_in_dim(small, model_width + ep_index * part, part, 0)
    grad_query_gain = lax.dynamic_slice_in_dim(
        small, 2 * model_width + ep_index * head_part, head_part, 0
    )
    grad_key_gain = lax.dynamic_slice_in_dim(
        small, 2 * model_width + HEAD_DIM + ep_index * head_part, head_part, 0
    )

    back = jnp.concatenate([layer_dealt, grad_layer.astype(BF16)], axis=1)
    home = exchange(dot_tn(recv, back).astype(BF16), ep_count)
    home = dot_tn(send, home)
    return (
        home[:, :share_width].astype(BF16),
        home[:, share_width:],
        grad_packed[:, :q_width],
        grad_packed[:, 2 * q_width : 2 * q_width + kv_width],
        grad_packed[:, 2 * q_width + kv_width :],
        grad_packed[:, q_width : 2 * q_width],
        grad_norm_attn,
        grad_norm_moe,
        grad_query_gain,
        grad_key_gain,
        grad_w_gate.reshape(w_gate.shape),
        grad_w_up.reshape(w_up.shape),
        grad_w_down.reshape(w_down.shape),
    )


def solution(mesh):
    return jax.shard_map(
        on_device,
        mesh=mesh,
        in_specs=(
            P("ep", "tp"),
            P(),
            P("ep", None),
            P("ep", None),
            P("ep", None),
            P("ep", "tp"),
            P("ep", "tp"),
            P("ep", "tp"),
            P("ep", "tp"),
            P("ep"),
            P("ep"),
            P("ep"),
            P("ep"),
            P("ep", "tp", None),
            P("ep", "tp", None),
            P("ep", "tp", None),
            P("ep", "tp"),
        ),
        out_specs=(
            P("ep", "tp"),
            P("ep", "tp"),
            P("ep", "tp"),
            P("ep", "tp"),
            P("ep", "tp"),
            P("ep", "tp"),
            P("ep"),
            P("ep"),
            P("ep"),
            P("ep"),
            P("ep", "tp", None),
            P("ep", "tp", None),
            P("ep", "tp", None),
        ),
        check_vma=False,
    )


def solution(mesh):
    shape = dict(mesh.shape)
    planes = shape["ep"] == 8 and shape["tp"] == 4
    return jax.shard_map(
        plane_layer if planes else plain_layer,
        mesh=mesh,
        in_specs=(
            P("ep", "tp"),
            P(),
            P("ep", None),
            P("ep", None),
            P("ep", None),
            P("ep", "tp"),
            P("ep", "tp"),
            P("ep", "tp"),
            P("ep", "tp"),
            P("ep"),
            P("ep"),
            P("ep"),
            P("ep"),
            P("ep", "tp", None),
            P("ep", "tp", None),
            P("ep", "tp", None),
            P("ep", "tp"),
        ),
        out_specs=(
            P("ep", "tp"),
            P("ep", "tp"),
            P("ep", "tp"),
            P("ep", "tp"),
            P("ep", "tp"),
            P("ep", "tp"),
            P("ep"),
            P("ep"),
            P("ep"),
            P("ep"),
            P("ep", "tp", None),
            P("ep", "tp", None),
            P("ep", "tp", None),
        ),
        check_vma=False,
    )
```

```python
import functools

import jax
import jax.numpy as jnp
from jax import lax
from jax.experimental import pallas as pl
from jax.experimental.pallas import tpu as pltpu
from jax.sharding import PartitionSpec as P

HEAD_DIM = 128
MICRO = 2
F32 = jnp.float32
BF16 = jnp.bfloat16
SCALE_TERMS = 3
VMEM_LIMIT = 66 * 1000 * 1000

epsilon = 1e-06
rope_base = 1000000.0


def positions_of(lengths, row_count):
    offsets = jnp.arange(row_count, dtype=jnp.int32)
    seq_ends = jnp.cumsum(lengths)
    segment = jnp.sum((offsets[:, None] >= seq_ends[None, :]).astype(jnp.int32), axis=1)
    starts = seq_ends - lengths
    in_segment = segment[:, None] == jnp.arange(lengths.shape[0], dtype=jnp.int32)[None, :]
    position = offsets - jnp.sum(jnp.where(in_segment, starts[None, :], 0), axis=1)
    return (segment, position)


def rope_tables(position, half_dim):
    frequency = rope_base ** (-jnp.arange(half_dim, dtype=F32) / half_dim)
    angles = position.astype(F32)[:, None] * frequency[None, :]
    return (jnp.cos(angles)[:, None, :], jnp.sin(angles)[:, None, :])


def rotate(values, cosine, sine_table):
    half_dim = values.shape[-1] // 2
    first_half = values[..., :half_dim]
    second_half = values[..., half_dim:]
    return jnp.concatenate(
        [
            first_half * cosine - second_half * sine_table,
            second_half * cosine + first_half * sine_table,
        ],
        axis=-1,
    )


def rotate_back(incoming, cosine, sine_table):
    return rotate(incoming, cosine, -sine_table)


def deal_matrices(token_order, ep_index, rows_dev, ep_count):
    per_pair = rows_dev // ep_count
    rows = jnp.arange(rows_dev, dtype=jnp.int32)
    home = ep_index * rows_dev + rows
    at = jnp.arange(token_order.shape[0], dtype=jnp.int32)
    place = jnp.sum(jnp.where(token_order[None, :] == home[:, None], at[None, :], 0), axis=1)
    dest = place // rows_dev
    rank = jnp.sum(
        ((dest[:, None] == dest[None, :]) & (place[None, :] < place[:, None])).astype(jnp.int32),
        axis=1,
    )
    send_slot = dest * per_pair + rank
    send = (send_slot[None, :] == rows[:, None]).astype(BF16)
    mine = lax.dynamic_slice_in_dim(token_order, ep_index * rows_dev, rows_dev, 0)
    source = mine // rows_dev
    my_rank = jnp.sum(
        ((source[:, None] == source[None, :]) & (rows[None, :] < rows[:, None])).astype(jnp.int32),
        axis=1,
    )
    recv_slot = source * per_pair + my_rank
    recv = (recv_slot[:, None] == rows[None, :]).astype(BF16)
    return (send, recv)


def inverse_rms(values):
    return lax.rsqrt(jnp.mean(values * values, axis=-1, keepdims=True) + epsilon)


def norm_back(grad_unit, unit_values, inverse):
    return inverse * (
        grad_unit - unit_values * jnp.mean(grad_unit * unit_values, axis=-1, keepdims=True)
    )


def dot_nn(left, right):
    return jnp.dot(left, right, preferred_element_type=F32)


def dot_tn(left_rows, right_rows):
    return lax.dot_general(
        left_rows, right_rows, (((0,), (0,)), ((), ())), preferred_element_type=F32
    )


def dot_nt(left_rows, right_matrix):
    return lax.dot_general(
        left_rows, right_matrix, (((1,), (1,)), ((), ())), preferred_element_type=F32
    )


def permute_rows(matrix, rows):
    return dot_nn(matrix, rows).astype(BF16)


def exchange(rows, ep_count):
    split = rows.reshape(ep_count, rows.shape[0] // ep_count, rows.shape[1])
    moved = lax.all_to_all(split, "ep", split_axis=0, concat_axis=0, tiled=True)
    return moved.reshape(rows.shape)


MESH_ID = pl.DeviceIdType.MESH
HALF = 2
E0, E1, P0, P1, A0, B0, PA0, PB0, A1, B1, PA1, PB1, D0, PD0, D1, PD1 = range(16)
SLOT_E, SLOT_P, SLOT_A, SLOT_B = (E0, E1), (P0, P1), (A0, A1), (B0, B1)
SLOT_D, SLOT_PA, SLOT_PB, SLOT_PD = (D0, D1), (PA0, PA1), (PB0, PB1), (PD0, PD1)
FOR_PARTNER = (P0, P1, PB0, PB1, PA0, PA1, PD0, PD1)


def roles():
    e = lax.axis_index("ep")
    core, x, y = e % 2, (e // 2) % 2, e // 4
    other = 1 - 2 * core
    over_x, over_y = e + 2 - 4 * x, e + 4 - 8 * y
    a = over_x * (1 - core) + over_y * core
    b = over_y * (1 - core) + over_x * core
    d = over_x + over_y - e
    return dict(e=e, p=e + other, a=a, b=b, d=d, pa=a + other, pb=b + other, pd=d + other)


def slot_owner(r):
    names = ("e", "e", "p", "p", "a", "b", "pa", "pb", "a", "b", "pa", "pb", "d", "pd", "d", "pd")
    halves = (0, 1, 0, 1, 0, 0, 0, 0, 1, 1, 1, 1, 0, 0, 1, 1)
    return [(r[name], half) for name, half in zip(names, halves)]


def greet(plane, line):
    barrier = pltpu.get_barrier_semaphore()
    for device in plane:
        pl.semaphore_signal(barrier, inc=1, device_id={"ep": device}, device_id_type=MESH_ID)
    for device in line:
        pl.semaphore_signal(barrier, inc=1, device_id={"tp": device}, device_id_type=MESH_ID)
    pl.semaphore_wait(barrier, len(plane) + len(line))


def send_to(src, dst, send_sem, recv_sem, **device):
    return pltpu.make_async_remote_copy(
        src_ref=src,
        dst_ref=dst,
        send_sem=send_sem,
        recv_sem=recv_sem,
        device_id=device,
        device_id_type=MESH_ID,
    )


class PlaneGather:
    kinds = 7

    def __init__(self, r, held, half, send, recv):
        self.r, self.held, self.half, self.send, self.recv = r, held, half, send, recv

    def slot(self, index):
        return self.held.at[pl.ds(index * self.half, self.half)]

    def copy(self, kind, k):
        source, target, device = (
            (SLOT_E, SLOT_A, "a"),
            (SLOT_E, SLOT_B, "b"),
            (SLOT_E, SLOT_P, "p"),
            (SLOT_A, SLOT_D, "b"),
            (SLOT_A, SLOT_PB, "p"),
            (SLOT_B, SLOT_PA, "p"),
            (SLOT_D, SLOT_PD, "p"),
        )[kind]
        return send_to(
            self.slot(source[k]),
            self.slot(target[k]),
            self.send.at[kind, k],
            self.recv.at[kind, k],
            ep=self.r[device],
        )

    def begin(self):
        for k in range(HALF):
            for kind in range(3):
                self.copy(kind, k).start()

    def arrived(self, kind, k):
        self.copy(kind, k).wait_recv()

    def pass_near(self, k):
        self.arrived(0, k)
        self.copy(3, k).start()
        self.copy(4, k).start()
        self.arrived(1, k)
        self.copy(5, k).start()

    def pass_far(self, k):
        self.arrived(3, k)
        self.copy(6, k).start()

    def sent(self):
        for k in range(HALF):
            for kind in range(self.kinds):
                self.copy(kind, k).wait_send()


class PlaneSum:
    def __init__(self, r, part, near, far, first, second, half, sems):
        self.r, self.part, self.half = r, part, half
        self.near, self.far, self.first, self.second = near, far, first, second
        self.near_send, self.near_recv, self.send, self.recv = sems

    def slot(self, index):
        return self.part.at[pl.ds(index * self.half, self.half)]

    def rows(self, buffer, index):
        return buffer.at[pl.ds(index * self.half, self.half)]

    def near_copy(self, index):
        return send_to(
            self.slot(FOR_PARTNER[index]),
            self.rows(self.near, index),
            self.near_send.at[index],
            self.near_recv.at[index],
            ep=self.r["p"],
        )

    def far_copy(self, kind, k):
        source, target, device = (
            (SLOT_D, self.far, "b"),
            (SLOT_A, self.first, "a"),
            (SLOT_B, self.second, "b"),
        )[kind]
        return send_to(
            self.slot(source[k]),
            self.rows(target, k),
            self.send.at[kind, k],
            self.recv.at[kind, k],
            ep=self.r[device],
        )

    def add_up(self, slot, others):
        total = self.slot(slot)[...].astype(F32)
        for other in others:
            total = total + other[...].astype(F32)
        return total

    def near_sum(self, name, k):
        index = 2 * name + k
        slot = (SLOT_E, SLOT_A, SLOT_B, SLOT_D)[name][k]
        self.near_copy(index).wait_recv()
        return slot, [self.rows(self.near, index)]

    def pass_far(self, k):
        slot, others = self.near_sum(3, k)
        self.slot(slot)[...] = self.add_up(slot, others).astype(BF16)
        self.far_copy(0, k).start()

    def pass_second(self, k):
        slot, others = self.near_sum(2, k)
        self.slot(slot)[...] = self.add_up(slot, others).astype(BF16)
        self.far_copy(2, k).start()

    def pass_first(self, k):
        slot, others = self.near_sum(1, k)
        self.far_copy(0, k).wait_recv()
        self.slot(slot)[...] = self.add_up(slot, others + [self.rows(self.far, k)]).astype(BF16)
        self.far_copy(1, k).start()

    def total(self, k):
        slot, others = self.near_sum(0, k)
        self.far_copy(1, k).wait_recv()
        self.far_copy(2, k).wait_recv()
        return self.add_up(slot, others + [self.rows(self.first, k), self.rows(self.second, k)])

    def sent(self):
        for index in range(4 * HALF):
            self.near_copy(index).wait_send()
        for kind in range(3):
            for k in range(HALF):
                self.far_copy(kind, k).wait_send()


def plane_sum_scratch(half, width, kinds=3):
    return [
        pltpu.VMEM((8 * half, width), BF16),
        pltpu.VMEM((2 * half, width), BF16),
        pltpu.VMEM((2 * half, width), BF16),
        pltpu.VMEM((2 * half, width), BF16),
        pltpu.SemaphoreType.DMA((4 * HALF,)),
        pltpu.SemaphoreType.DMA((4 * HALF,)),
        pltpu.SemaphoreType.DMA((kinds, HALF)),
        pltpu.SemaphoreType.DMA((kinds, HALF)),
    ]


def any_spec():
    return pl.BlockSpec(memory_space=pl.ANY)


def vmem_spec():
    return pl.BlockSpec(memory_space=pltpu.VMEM)


def comm_params(collective_id):
    return pltpu.CompilerParams(
        collective_id=collective_id, has_side_effects=True, vmem_limit_bytes=VMEM_LIMIT
    )


def expert_body(
    flat,
    rows,
    parts,
    own_hbm,
    grad_hbm,
    scale_hbm,
    pick_ref,
    gate_hbm,
    up_hbm,
    down_hbm,
    total_ref,
    active_hbm,
    d_gate_hbm,
    d_up_hbm,
    d_down_hbm,
    held,
    grads,
    scales,
    both,
    down,
    grad_act,
    grad_both,
    active,
    d_weights,
    part,
    near,
    far,
    first,
    second,
    near_send,
    near_recv,
    sum_send,
    sum_recv,
    gather_send,
    gather_recv,
    local_sem,
    grad_sem,
    out_sem,
):
    r = roles()
    half = rows // HALF
    unit = 2 * half
    owners = slot_owner(r)
    loads = [
        pltpu.make_async_copy(own_hbm, held.at[pl.ds(0, rows)], local_sem.at[0]),
        pltpu.make_async_copy(gate_hbm, both.at[pl.ds(0, flat)], local_sem.at[1]),
        pltpu.make_async_copy(up_hbm, both.at[pl.ds(flat, flat)], local_sem.at[2]),
        pltpu.make_async_copy(down_hbm, down, local_sem.at[3]),
    ]
    for load in loads:
        load.start()
    stride = scale_hbm.shape[0] // 8
    slots = []
    for index, (owner, k) in enumerate(owners):
        slots.append(
            (
                pltpu.make_async_copy(
                    scale_hbm.at[pl.ds(owner * stride, parts), pl.ds(k * half, half)],
                    scales.at[index],
                    grad_sem.at[0, index],
                ),
                pltpu.make_async_copy(
                    grad_hbm.at[pl.ds(owner * rows + k * half, half)],
                    grads.at[pl.ds(index * half, half)],
                    grad_sem.at[1, index],
                ),
            )
        )
        for load in slots[-1]:
            load.start()
    greet([r["p"], r["a"], r["b"]], [])
    gather = PlaneGather(r, held, half, gather_send, gather_recv)
    loads[0].wait()
    gather.begin()
    for load in loads[1:]:
        load.wait()
    for pair in slots:
        for load in pair:
            load.wait()
    psum = PlaneSum(
        r, part, near, far, first, second, half, (near_send, near_recv, sum_send, sum_recv)
    )

    def expand(index):
        return jnp.concatenate(
            [dot_tn(scales[2 * index], pick_ref[...]), dot_tn(scales[2 * index + 1], pick_ref[...])],
            axis=0,
        )

    @pl.loop(0, 8)
    def _(index):
        at = pl.ds(pl.multiple_of(index * unit, unit), unit)
        grad_act[at, :] = dot_nt(grads[at, :], down[...]) * expand(index)

    @pl.loop(0, 8)
    def _(index):
        @pl.when(index == 1)
        def _():
            gather.arrived(2, 0)
            gather.arrived(2, 1)

        for k, first_unit in ((0, 2), (1, 4)):

            @pl.when(index == first_unit)
            def _():
                gather.pass_near(k)

            @pl.when(index == first_unit + 1)
            def _():
                gather.arrived(4, k)
                gather.arrived(5, k)

            @pl.when(index == 6 + k)
            def _():
                gather.pass_far(k)
                gather.arrived(6, k)

        at = pl.ds(pl.multiple_of(index * unit, unit), unit)
        pre = dot_nt(held[at, :], both[...])
        gate_pre, up_pre = pre[:, :flat], pre[:, flat:]
        grad_active = grad_act[at, :]
        sigmoid_gate = jax.nn.sigmoid(gate_pre)
        silu_gate = gate_pre * sigmoid_gate
        active[at, :] = (silu_gate * up_pre * expand(index)).astype(BF16)
        grad_both[at, flat:] = (grad_active * silu_gate).astype(BF16)
        grad_both[at, :flat] = (
            grad_active * up_pre * sigmoid_gate * (1.0 + gate_pre * (1.0 - sigmoid_gate))
        ).astype(BF16)
        part[at, :] = dot_nn(grad_both[at, :], both[...]).astype(BF16)

        @pl.when(index == 1)
        def _():
            psum.near_copy(0).start()
            psum.near_copy(1).start()

        for k, last_unit in ((0, 3), (1, 5)):

            @pl.when(index == last_unit)
            def _():
                psum.near_copy(2 + k).start()
                psum.near_copy(4 + k).start()

            @pl.when(index == last_unit + 1)
            def _():
                psum.pass_second(k)

            @pl.when(index == 6 + k)
            def _():
                psum.near_copy(6 + k).start()

    active_out = pltpu.make_async_copy(active, active_hbm, local_sem.at[0])
    active_out.start()
    psum.pass_far(0)
    psum.pass_far(1)
    group = 128
    pieces = flat // group

    def weight_piece(which, index):
        source, other, column = (
            (active, grads, 0),
            (grad_both, held, 0),
            (grad_both, held, flat),
        )[which]
        lanes = pl.ds(pl.multiple_of(column + index * group, group), group)
        place = pl.ds(pl.multiple_of(which * flat + index * group, group), group)
        d_weights[place, :] = dot_tn(source[:, lanes], other[...])

    def weight_out(which):
        target = (d_down_hbm, d_gate_hbm, d_up_hbm)[which]
        return pltpu.make_async_copy(
            d_weights.at[pl.ds(which * flat, flat)], target, out_sem.at[which]
        )

    @pl.loop(0, pieces)
    def _(index):
        weight_piece(0, index)

    weight_out(0).start()
    psum.pass_first(0)
    psum.pass_first(1)

    @pl.loop(0, 2 * pieces)
    def _(index):
        lanes = pl.ds(pl.multiple_of(index * group, group), group)
        place = pl.ds(pl.multiple_of(flat + index * group, group), group)
        d_weights[place, :] = dot_tn(grad_both[:, lanes], held[...])

    weight_out(1).start()
    weight_out(2).start()
    for k in range(HALF):
        total_ref[pl.ds(k * half, half), :] = psum.total(k).astype(BF16)
    active_out.wait()
    for which in range(3):
        weight_out(which).wait()
    gather.sent()
    psum.sent()


def expert_call(own, all_grad, scale_parts, pick, gate_matrix, up_matrix, down_matrix):
    rows, width = own.shape
    flat = gate_matrix.shape[0]
    everything = all_grad.shape[0]
    parts = pick.shape[0]
    half = rows // HALF
    f32_weight = jax.ShapeDtypeStruct((flat, width), F32)
    return pl.pallas_call(
        functools.partial(expert_body, flat, rows, parts),
        out_shape=(
            jax.ShapeDtypeStruct((rows, width), BF16),
            jax.ShapeDtypeStruct((everything, flat), BF16),
            f32_weight,
            f32_weight,
            f32_weight,
        ),
        in_specs=[any_spec(), any_spec(), any_spec(), vmem_spec()] + [any_spec()] * 3,
        out_specs=(vmem_spec(), any_spec(), any_spec(), any_spec(), any_spec()),
        scratch_shapes=[
            pltpu.VMEM((everything, width), BF16),
            pltpu.VMEM((everything, width), BF16),
            pltpu.VMEM((16, parts, half), BF16),
            pltpu.VMEM((2 * flat, width), BF16),
            pltpu.VMEM((flat, width), BF16),
            pltpu.VMEM((everything, flat), F32),
            pltpu.VMEM((everything, 2 * flat), BF16),
            pltpu.VMEM((everything, flat), BF16),
            pltpu.VMEM((3 * flat, width), F32),
            pltpu.VMEM((everything, width), BF16),
        ]
        + plane_sum_scratch(half, width)
        + [
            pltpu.SemaphoreType.DMA((PlaneGather.kinds, HALF)),
            pltpu.SemaphoreType.DMA((PlaneGather.kinds, HALF)),
            pltpu.SemaphoreType.DMA((4,)),
            pltpu.SemaphoreType.DMA((2, 16)),
            pltpu.SemaphoreType.DMA((3,)),
        ],
        compiler_params=comm_params(1),
        name="experts",
    )(own, all_grad, scale_parts, pick, gate_matrix, up_matrix, down_matrix)


class LineSum:
    def __init__(self, count, source, arrived, send, recv):
        self.count, self.source, self.arrived, self.send, self.recv = (
            count,
            source,
            arrived,
            send,
            recv,
        )
        self.z = lax.axis_index("tp")
        self.share = source.shape[1] // count

    def columns(self, z):
        return pl.ds(pl.multiple_of(z * self.share, self.share), self.share)

    def copy(self, j):
        target = (self.z + j) % self.count
        return send_to(
            self.source.at[:, self.columns(target)],
            self.arrived.at[j - 1],
            self.send.at[j - 1],
            self.recv.at[j - 1],
            tp=target,
        )

    def begin(self):
        for j in range(1, self.count):
            self.copy(j).start()

    def total(self):
        total = self.source[:, self.columns(self.z)].astype(F32)
        for j in range(1, self.count):
            self.copy(j).wait_recv()
            total = total + self.arrived[j - 1].astype(F32)
        return total

    def sent(self):
        for j in range(1, self.count):
            self.copy(j).wait_send()


class OrderedGather(PlaneGather):
    def place(self, name, k):
        return self.held.at[pl.ds((self.r[name] * HALF + k) * self.half, self.half)]

    def copy(self, kind, k):
        source, device = (
            ("e", "a"),
            ("e", "b"),
            ("e", "p"),
            ("a", "b"),
            ("a", "p"),
            ("b", "p"),
            ("d", "p"),
        )[kind]
        block = self.place(source, k)
        return send_to(
            block, block, self.send.at[kind, k], self.recv.at[kind, k], ep=self.r[device]
        )

    def arrived(self, kind, k):
        source, device = (
            ("a", "a"),
            ("b", "b"),
            ("p", "p"),
            ("d", "b"),
            ("pb", "p"),
            ("pa", "p"),
            ("pd", "p"),
        )[kind]
        block = self.place(source, k)
        send_to(
            block, block, self.send.at[kind, k], self.recv.at[kind, k], ep=self.r[device]
        ).wait_recv()

    def finish(self):
        for k in range(HALF):
            for kind in (2, 4, 5, 6):
                self.arrived(kind, k)


class LineGather:
    def __init__(self, count, whole, up_send, up_recv, down_send, down_recv):
        self.count, self.whole = count, whole
        self.up_sems, self.down_sems = (up_send, up_recv), (down_send, down_recv)
        self.z = lax.axis_index("tp")
        self.share = whole.shape[1] // count

    def columns(self, z):
        return pl.ds(pl.multiple_of(z * self.share, self.share), self.share)

    def move(self, share, j, sems, target):
        block = self.whole.at[:, self.columns(share)]
        return send_to(block, block, sems[0].at[j - 1], sems[1].at[j - 1], tp=target)

    def up(self, j):
        return self.move(self.z - j + 1, j, self.up_sems, self.z + 1)

    def down(self, j):
        return self.move(self.z + j - 1, j, self.down_sems, self.z - 1)

    def sends(self, j, act):
        @pl.when((self.z < self.count - 1) & (self.z >= j - 1))
        def _():
            act(self.up(j))

        @pl.when((self.z > 0) & (self.z + j <= self.count))
        def _():
            act(self.down(j))

    def begin(self):
        self.sends(1, lambda copy: copy.start())

    def step(self, j):
        @pl.when(self.z >= j)
        def _():
            self.move(self.z - j, j, self.up_sems, self.z - 1).wait_recv()

        @pl.when(self.z + j < self.count)
        def _():
            self.move(self.z + j, j, self.down_sems, self.z + 1).wait_recv()

        if j + 1 < self.count:
            self.sends(j + 1, lambda copy: copy.start())

    def wait(self):
        for j in range(1, self.count):
            self.step(j)

    def sent(self):
        for j in range(1, self.count):
            self.sends(j, lambda copy: copy.wait_send())


def line_peers(count):
    z = lax.axis_index("tp")
    return [(z + j) % count for j in range(1, count)]


def mix_body(
    tp_count,
    rows,
    partial_ref,
    active_ref,
    down_ref,
    grad_ref,
    mixed_ref,
    part,
    line,
    near,
    far,
    first,
    second,
    near_send,
    near_recv,
    sum_send,
    sum_recv,
    line_send,
    line_recv,
    back_line,
):
    r = roles()
    half = rows // HALF
    unit = 2 * half
    greet([r["p"], r["a"], r["b"]], line_peers(tp_count))
    over_line = LineSum(tp_count, partial_ref, line, line_send, line_recv)
    over_line.begin()
    psum = PlaneSum(
        r, part, near, far, first, second, half, (near_send, near_recv, sum_send, sum_recv)
    )

    @pl.loop(0, 8)
    def _(step):
        index = (step + 6) % 8
        at = pl.ds(pl.multiple_of(index * unit, unit), unit)
        part[at, :] = dot_nn(active_ref[at, :], down_ref[...]).astype(BF16)
        for unit_done, copies in ((6, (6,)), (7, (7,)), (1, (0, 1)), (3, (2, 4)), (5, (3, 5))):

            @pl.when(index == unit_done)
            def _():
                for copy in copies:
                    psum.near_copy(copy).start()

    for k in range(HALF):
        psum.pass_far(k)
    for k in range(HALF):
        psum.pass_second(k)
    for k in range(HALF):
        psum.pass_first(k)
    back = LineGather(tp_count, grad_ref, *[back_line.at[i] for i in range(4)])
    grad_ref[:, back.columns(back.z)] = over_line.total().astype(BF16)
    back.begin()
    back.step(1)
    back.step(2)
    for k in range(HALF):
        mixed_ref[pl.ds(k * half, half), :] = psum.total(k).astype(BF16)
    back.step(3)
    over_line.sent()
    back.sent()
    psum.sent()


def mix_call(partial, active, down_matrix, tp_count):
    rows, width = partial.shape
    everything = active.shape[0]
    half = rows // HALF
    whole = jax.ShapeDtypeStruct((rows, width), BF16)
    line_sems = pltpu.SemaphoreType.DMA((tp_count - 1,))
    return pl.pallas_call(
        functools.partial(mix_body, tp_count, rows),
        out_shape=(whole, whole),
        in_specs=[vmem_spec()] * 3,
        out_specs=(vmem_spec(), vmem_spec()),
        scratch_shapes=[
            pltpu.VMEM((everything, width), BF16),
            pltpu.VMEM((tp_count - 1, rows, width // tp_count), BF16),
        ]
        + plane_sum_scratch(half, width)
        + [line_sems] * 2
        + [pltpu.SemaphoreType.DMA((4, tp_count - 1))],
        compiler_params=comm_params(2),
        name="mix",
    )(partial, active, down_matrix)


def turn(values, cosine, sine_table):
    return values * cosine + pltpu.roll(values, HEAD_DIM // 2, 1) * sine_table


def unit_of(values):
    return values * lax.rsqrt(jnp.mean(values * values, axis=-1, keepdims=True) + epsilon)


def front_body(
    gain_at,
    ep_count,
    tp_count,
    rows,
    heads,
    send_ref,
    recv_ref,
    small_ref,
    cosine_ref,
    sine_ref,
    mask_ref,
    query_hbm,
    key_hbm,
    value_hbm,
    out_hbm,
    x_ref,
    grad_ref,
    hidden_ref,
    moe_ref,
    proj_ref,
    turned_ref,
    keys_ref,
    values_ref,
    probs_ref,
    context_ref,
    small_all,
    normed,
    all_grad,
    w_in_hbm,
    w_out_hbm,
    w_in,
    w_out,
    dealt,
    x_wire,
    grad_wire,
    back_wire,
    attn,
    line,
    deal_send,
    deal_recv,
    small_send,
    small_recv,
    in_send,
    in_recv,
    out_send,
    out_recv,
    grad_send,
    grad_recv,
    x_line,
    grad_line,
    back_line,
    line_send,
    line_recv,
    local_sem,
):
    r = roles()
    e = r["e"]
    z = lax.axis_index("tp")
    half = rows // HALF
    q_width = heads * HEAD_DIM
    share = x_wire.shape[1] // tp_count
    per_pair = rows // ep_count
    micro_rows = rows // MICRO
    own = pl.ds(e * rows, rows)
    loads = [
        pltpu.make_async_copy(query_hbm, w_in.at[own, pl.ds(0, q_width)], local_sem.at[0]),
        pltpu.make_async_copy(key_hbm, w_in.at[own, pl.ds(q_width, HEAD_DIM)], local_sem.at[1]),
        pltpu.make_async_copy(
            value_hbm, w_in.at[own, pl.ds(q_width + HEAD_DIM, HEAD_DIM)], local_sem.at[2]
        ),
        pltpu.make_async_copy(out_hbm, w_out.at[own], local_sem.at[3]),
    ]
    for load in loads:
        load.start()
    small_rows = small_ref.shape[0]
    small_all[pl.ds(e * small_rows, small_rows), :] = small_ref[...]
    others = [(e + j) % ep_count for j in range(1, ep_count)]
    greet(others, line_peers(tp_count))

    def deal(j, source, target):
        return send_to(
            send_ref.at[pl.ds(target * per_pair, per_pair)],
            dealt.at[pl.ds(source * per_pair, per_pair)],
            deal_send.at[j - 1],
            deal_recv.at[j - 1],
            ep=target,
        )

    for j in range(1, ep_count):
        deal(j, e, (e + j) % ep_count).start()
    mine = pl.ds(pl.multiple_of(e * per_pair, per_pair), per_pair)
    dealt[mine, :] = send_ref[mine, :]
    gather_small = OrderedGather(r, small_all, small_rows // HALF, small_send, small_recv)
    gather_in = OrderedGather(r, w_in, half, in_send, in_recv)
    gather_out = OrderedGather(r, w_out, half, out_send, out_recv)
    gather_grad = OrderedGather(r, all_grad, half, grad_send, grad_recv)
    gather_small.begin()
    for load in loads:
        load.wait()
    gather_in.begin()
    for j in range(1, ep_count):
        deal(j, (e + ep_count - j) % ep_count, (e + j) % ep_count).wait_recv()
    x_gather = LineGather(tp_count, x_wire, *[x_line.at[i] for i in range(4)])
    grad_gather = LineGather(tp_count, grad_wire, *[grad_line.at[i] for i in range(4)])
    x_wire[:, x_gather.columns(z)] = dealt[:, :share]
    grad_wire[:, x_gather.columns(z)] = dealt[:, share:]
    x_gather.begin()
    for k in range(HALF):
        gather_small.pass_near(k)
    x_gather.step(1)
    gather_in.pass_near(0)
    x_gather.step(2)
    grad_gather.begin()
    gather_in.pass_near(1)
    gather_out.begin()
    x_gather.step(3)
    for k in range(HALF):
        gather_small.pass_far(k)
    gather_small.finish()

    def gain_row(place, column, width):
        at = place * small_rows + gain_at
        return small_all[at : at + 1, column : column + width].astype(F32)

    x_rows = dot_nn(recv_ref[...], x_wire[...])
    x_ref[...] = x_rows.astype(BF16)
    unit_one = unit_of(x_rows)
    for place in range(ep_count):
        at = slice(place * rows, (place + 1) * rows)
        normed[:, at] = (unit_one[:, at] * gain_row(place, 0, rows)).astype(BF16)
    for k in range(HALF):
        gather_in.pass_far(k)
    grad_gather.step(1)
    gather_in.finish()
    gather_out.pass_near(0)

    proj_ref[...] = dot_nn(normed[...], w_in[...])
    grad_gather.step(2)
    gather_out.pass_near(1)
    column = 2 * rows
    gain_query = sum(gain_row(place, column, HEAD_DIM) for place in range(ep_count))
    gain_key = sum(gain_row(place, column + HEAD_DIM, HEAD_DIM) for place in range(ep_count))
    cosine, sine_table = cosine_ref[...], sine_ref[...]
    keys_ref[...] = turn(
        unit_of(proj_ref[:, q_width : q_width + HEAD_DIM]) * gain_key, cosine, sine_table
    ).astype(BF16)
    values_ref[...] = proj_ref[:, q_width + HEAD_DIM :].astype(BF16)

    @pl.loop(0, heads)
    def _(head):
        lanes = pl.ds(pl.multiple_of(head * HEAD_DIM, HEAD_DIM), HEAD_DIM)
        queries = turn(unit_of(proj_ref[:, lanes]) * gain_query, cosine, sine_table).astype(BF16)
        for micro in range(MICRO):
            at = pl.ds(
                pl.multiple_of((micro * heads + head) * micro_rows, micro_rows), micro_rows
            )
            turned_ref[at, :] = queries[micro * micro_rows : (micro + 1) * micro_rows]

    grad_gather.step(3)
    for micro in range(MICRO):
        within = slice(micro * micro_rows, (micro + 1) * micro_rows)
        stacked = slice(micro * heads * micro_rows, (micro + 1) * heads * micro_rows)
        scores = dot_nt(turned_ref[stacked, :], keys_ref[within, :]) * HEAD_DIM ** (-0.5)
        mask = mask_ref[within, :]
        scores = scores.reshape(heads, micro_rows, micro_rows)
        scores = jnp.where(mask[None] > 0.0, scores, -1e30)
        exponent = jnp.exp(scores - jnp.max(scores, axis=-1, keepdims=True))
        probs = exponent / jnp.sum(exponent, axis=-1, keepdims=True)
        probs = probs.reshape(heads * micro_rows, micro_rows)
        probs_ref[stacked, :] = probs
        context = dot_nn(probs.astype(BF16), values_ref[within, :]).astype(BF16)
        for head in range(heads):
            context_ref[within, head * HEAD_DIM : (head + 1) * HEAD_DIM] = context[
                head * micro_rows : (head + 1) * micro_rows
            ]

    grad_ref[...] = dot_nn(recv_ref[...], grad_wire[...]).astype(BF16)
    grad_here = pltpu.make_async_copy(grad_ref, all_grad.at[own], local_sem.at[4])
    grad_here.start()
    for k in range(HALF):
        gather_out.pass_far(k)
    grad_here.wait()
    gather_grad.begin()
    gather_out.finish()

    attn[...] = dot_nt(context_ref[...], w_out[...]).astype(BF16)
    over_line = LineSum(tp_count, attn, line, line_send, line_recv)
    over_line.begin()
    w_in_out = pltpu.make_async_copy(w_in, w_in_hbm, local_sem.at[0])
    w_out_out = pltpu.make_async_copy(w_out, w_out_hbm, local_sem.at[1])
    w_in_out.start()
    w_out_out.start()
    gather_grad.pass_near(0)
    total = over_line.total()
    back = LineGather(tp_count, back_wire, *[back_line.at[i] for i in range(4)])
    back_wire[:, back.columns(z)] = total.astype(BF16)
    back.begin()
    back.step(1)
    gather_grad.pass_near(1)
    back.step(2)
    gather_grad.pass_far(0)
    back.step(3)
    hidden = x_ref[...].astype(F32) + back_wire[...].astype(F32)
    hidden_ref[...] = hidden
    unit_two = unit_of(hidden)
    for place in range(ep_count):
        at = slice(place * rows, (place + 1) * rows)
        moe_ref[:, at] = (unit_two[:, at] * gain_row(place, rows, rows)).astype(BF16)
    gather_grad.pass_far(1)
    gather_grad.finish()
    for j in range(1, ep_count):
        deal(j, e, (e + j) % ep_count).wait_send()
    x_gather.sent()
    grad_gather.sent()
    back.sent()
    over_line.sent()
    for gather in (gather_small, gather_in, gather_out, gather_grad):
        gather.sent()
    w_in_out.wait()
    w_out_out.wait()


def front_call(
    gain_at, ep_count, tp_count, send_rows, recv, small, cosine, sine_table, mask, query, key, value, out
):
    rows = send_rows.shape[0]
    share = send_rows.shape[1] // 2
    width = share * tp_count
    q_width = query.shape[1]
    heads = q_width // HEAD_DIM
    everything = rows * ep_count
    in_width = q_width + 2 * HEAD_DIM
    micro_rows = rows // MICRO
    shape = jax.ShapeDtypeStruct
    gather_sems = pltpu.SemaphoreType.DMA((PlaneGather.kinds, HALF))
    line_sems = pltpu.SemaphoreType.DMA((4, tp_count - 1))
    return pl.pallas_call(
        functools.partial(front_body, gain_at, ep_count, tp_count, rows, heads),
        out_shape=(
            shape((rows, width), BF16),
            shape((rows, width), BF16),
            shape((rows, width), F32),
            shape((rows, width), BF16),
            shape((rows, in_width), F32),
            shape((heads * rows, HEAD_DIM), BF16),
            shape((rows, HEAD_DIM), BF16),
            shape((rows, HEAD_DIM), BF16),
            shape((heads * rows, micro_rows), F32),
            shape((rows, q_width), BF16),
            shape((ep_count * small.shape[0], small.shape[1]), BF16),
            shape((rows, width), BF16),
            shape((everything, width), BF16),
            shape((everything, in_width), BF16),
            shape((everything, q_width), BF16),
        ),
        in_specs=[vmem_spec()] * 6 + [any_spec()] * 4,
        out_specs=tuple([vmem_spec()] * 12 + [any_spec()] * 3),
        scratch_shapes=[
            pltpu.VMEM((everything, in_width), BF16),
            pltpu.VMEM((everything, q_width), BF16),
            pltpu.VMEM(send_rows.shape, BF16),
            pltpu.VMEM((rows, width), BF16),
            pltpu.VMEM((rows, width), BF16),
            pltpu.VMEM((rows, width), BF16),
            pltpu.VMEM((rows, width), BF16),
            pltpu.VMEM((tp_count - 1, rows, share), BF16),
            pltpu.SemaphoreType.DMA((ep_count - 1,)),
            pltpu.SemaphoreType.DMA((ep_count - 1,)),
        ]
        + [gather_sems] * 8
        + [line_sems] * 3
        + [pltpu.SemaphoreType.DMA((tp_count - 1,))] * 2
        + [pltpu.SemaphoreType.DMA((5,))],
        compiler_params=comm_params(3),
        name="front",
    )(send_rows, recv, small, cosine, sine_table, mask, query, key, value, out)


def fold(values):
    rows, width = values.shape
    return jnp.sum(values.reshape(rows // 8, 8, width), axis=0)


class Straight:
    def __init__(self, axis, count, source, landed, send, recv):
        self.axis, self.count, self.source, self.landed = axis, count, source, landed
        self.send, self.recv = send, recv
        self.me = lax.axis_index(axis)

    def copy(self, j):
        target = (self.me + j) % self.count
        return send_to(
            self.source(target),
            self.landed(j),
            self.send.at[j - 1],
            self.recv.at[j - 1],
            **{self.axis: target},
        )

    def begin(self):
        for j in range(1, self.count):
            self.copy(j).start()

    def wait(self):
        for j in range(1, self.count):
            self.copy(j).wait_recv()

    def sent(self):
        for j in range(1, self.count):
            self.copy(j).wait_send()


def back_body(
    gain_at,
    ep_count,
    tp_count,
    rows,
    heads,
    grad_moe_ref,
    mixed_ref,
    x_ref,
    hidden_ref,
    grad_ref,
    normed_ref,
    proj_ref,
    turned_ref,
    keys_ref,
    values_ref,
    probs_ref,
    context_ref,
    small_all,
    cosine_ref,
    sine_ref,
    send_ref,
    recv_ref,
    w_in_hbm,
    w_out_hbm,
    layer_out,
    layer_grad,
    d_query,
    d_key,
    d_value,
    d_out,
    sums_out,
    w_in,
    w_out,
    grad_hidden,
    grad_attn,
    stacked_grad,
    grad_turned,
    grad_proj,
    normed_part,
    mixed_line,
    normed_line,
    row_sums,
    row_line,
    sums,
    sums_near,
    sums_line,
    home_send,
    home_recv,
    out_part,
    in_part,
    *rest,
):
    out_bufs, out_sems = rest[0:4], rest[4:8]
    in_bufs, in_sems = rest[8:12], rest[12:16]
    mixed_sems, normed_sems, row_sems, sum_sems, sum_line_sems, home_sems = (
        rest[16:18],
        rest[18:20],
        rest[20:22],
        rest[22:24],
        rest[24:26],
        rest[26:28],
    )
    local_sem = rest[28]
    r = roles()
    e = r["e"]
    z = lax.axis_index("tp")
    half = rows // HALF
    width = x_ref.shape[1]
    share = width // tp_count
    q_width = heads * HEAD_DIM
    micro_rows = rows // MICRO
    per_pair = rows // ep_count
    small_rows = small_all.shape[0] // ep_count
    loads = [
        pltpu.make_async_copy(w_out_hbm, w_out, local_sem.at[0]),
        pltpu.make_async_copy(w_in_hbm, w_in, local_sem.at[1]),
    ]
    for load in loads:
        load.start()
    greet([(e + j) % ep_count for j in range(1, ep_count)], line_peers(tp_count))
    mixed_sum = LineSum(tp_count, mixed_ref, mixed_line, *mixed_sems)
    mixed_sum.begin()
    out_sum = PlaneSum(r, out_part, *out_bufs, half, out_sems)
    in_sum = PlaneSum(r, in_part, *in_bufs, half, in_sems)

    def gain_row(place, column, wide):
        at = place * small_rows + gain_at
        return small_all[at : at + 1, column : column + wide].astype(F32)

    hidden = hidden_ref[...]
    inverse_two = lax.rsqrt(jnp.mean(hidden * hidden, axis=-1, keepdims=True) + epsilon)
    unit_two = hidden * inverse_two
    grad_moe = grad_moe_ref[...].astype(F32)
    moe_sums = fold(grad_moe * unit_two)
    gain_moe = jnp.concatenate([gain_row(place, rows, rows) for place in range(ep_count)], axis=1)
    scaled = grad_moe * gain_moe
    grad_hidden[...] = grad_ref[...].astype(F32) + inverse_two * (
        scaled - unit_two * jnp.mean(scaled * unit_two, axis=-1, keepdims=True)
    )
    grad_attn[...] = grad_hidden[...].astype(BF16)
    sums[...] = jnp.zeros_like(sums)
    for place in range(ep_count):
        sums[place * 8 : place * 8 + 8, rows : 2 * rows] = moe_sums[
            :, place * rows : (place + 1) * rows
        ]

    near_of = {"pd": (6, 7), "pb": (2, 3), "pa": (4, 5), "p": (0, 1)}
    slots_of = {
        "pd": SLOT_PD,
        "d": SLOT_D,
        "pb": SLOT_PB,
        "b": SLOT_B,
        "pa": SLOT_PA,
        "a": SLOT_A,
        "p": SLOT_P,
        "e": SLOT_E,
    }

    def weight_blocks(plane, left, right):
        for name, slots in slots_of.items():
            lanes = pl.ds(pl.multiple_of(r[name] * rows, rows), rows)
            block = dot_tn(left[:, lanes], right[...]).astype(BF16)
            for k in range(HALF):
                plane.slot(slots[k])[...] = block[k * half : (k + 1) * half]
                if name in near_of:
                    plane.near_copy(near_of[name][k]).start()

    weight_blocks(out_sum, grad_attn, context_ref)
    loads[0].wait()
    grad_context = dot_nn(grad_attn[...], w_out[...]).astype(BF16)
    for micro in range(MICRO):
        for head in range(heads):
            at = (micro * heads + head) * micro_rows
            stacked_grad[at : at + micro_rows, :] = grad_context[
                micro * micro_rows : (micro + 1) * micro_rows,
                head * HEAD_DIM : (head + 1) * HEAD_DIM,
            ]
    for k in range(HALF):
        out_sum.pass_far(k)
    for k in range(HALF):
        out_sum.pass_second(k)

    cosine, sine_table = cosine_ref[...], -sine_ref[...]
    column = 2 * rows
    gain_query = sum(gain_row(place, column, HEAD_DIM) for place in range(ep_count))
    gain_key = sum(gain_row(place, column + HEAD_DIM, HEAD_DIM) for place in range(ep_count))
    scale = HEAD_DIM ** (-0.5)
    grad_keys = []
    for micro in range(MICRO):
        within = slice(micro * micro_rows, (micro + 1) * micro_rows)
        stacked = slice(micro * heads * micro_rows, (micro + 1) * heads * micro_rows)
        probs = probs_ref[stacked, :]
        grad_probs = dot_nt(stacked_grad[stacked, :], values_ref[within, :])
        delta = jnp.sum(probs * grad_probs, axis=-1, keepdims=True)
        grad_scores = (probs * (grad_probs - delta)).astype(BF16)
        grad_turned[stacked, :] = dot_nn(grad_scores, keys_ref[within, :]) * scale
        grad_keys.append(dot_tn(grad_scores, turned_ref[stacked, :]) * scale)
        grad_proj[within, q_width + HEAD_DIM :] = dot_tn(
            probs.astype(BF16), stacked_grad[stacked, :]
        ).astype(BF16)

    def unturn(grad, values, gain):
        unturned = turn(grad, cosine, sine_table)
        inverse = lax.rsqrt(jnp.mean(values * values, axis=-1, keepdims=True) + epsilon)
        unit = values * inverse
        scaled = unturned * gain
        result = inverse * (scaled - unit * jnp.mean(scaled * unit, axis=-1, keepdims=True))
        return fold(unturned * unit), result.astype(BF16)

    key_sums, grad_key = unturn(
        jnp.concatenate(grad_keys, axis=0), proj_ref[:, q_width : q_width + HEAD_DIM], gain_key
    )
    grad_proj[:, q_width : q_width + HEAD_DIM] = grad_key
    for k in range(HALF):
        out_sum.pass_first(k)

    def one_head(head, total):
        lanes = pl.ds(pl.multiple_of(head * HEAD_DIM, HEAD_DIM), HEAD_DIM)
        grads = [
            grad_turned[
                pl.ds(pl.multiple_of((micro * heads + head) * micro_rows, micro_rows), micro_rows),
                :,
            ]
            for micro in range(MICRO)
        ]
        part, grad = unturn(jnp.concatenate(grads, axis=0), proj_ref[:, lanes], gain_query)
        grad_proj[:, lanes] = grad
        return total + part

    query_sums = lax.fori_loop(0, heads, one_head, jnp.zeros((8, HEAD_DIM), F32))
    for place in range(ep_count):
        at = slice(place * 8, place * 8 + 8)
        sums[at, column : column + HEAD_DIM] = query_sums
        sums[at, column + HEAD_DIM :] = key_sums

    x_rows = x_ref[...].astype(F32)
    inverse_one = lax.rsqrt(jnp.mean(x_rows * x_rows, axis=-1, keepdims=True) + epsilon)
    gain_attn = jnp.concatenate([gain_row(place, 0, rows) for place in range(ep_count)], axis=1)
    loads[1].wait()
    partial = dot_nt(grad_proj[...], w_in[...])
    normed_part[...] = partial.astype(BF16)
    normed_sum = LineSum(tp_count, normed_part, normed_line, *normed_sems)
    normed_sum.begin()
    weight_blocks(in_sum, normed_ref, grad_proj)
    along = jnp.sum(partial * gain_attn * (x_rows * inverse_one), axis=-1, keepdims=True)
    row_sums[...] = jnp.transpose(jnp.broadcast_to(along, (rows, HEAD_DIM)))[:8]
    over_rows = Straight("tp", tp_count, lambda _: row_sums, lambda j: row_line.at[j - 1], *row_sems)
    over_rows.begin()
    for k in range(HALF):
        in_sum.pass_far(k)
    for k in range(HALF):
        in_sum.pass_second(k)
    for k in range(HALF):
        d_out[pl.ds(k * half, half), :] = out_sum.total(k)
    for k in range(HALF):
        in_sum.pass_first(k)

    lanes = pl.ds(pl.multiple_of(z * share, share), share)
    layer_rows = (hidden_ref[:, lanes] + mixed_sum.total()).astype(BF16)
    over_rows.wait()
    all_rows = row_sums[...]
    for j in range(1, tp_count):
        all_rows = all_rows + row_line[j - 1]
    mean = jnp.transpose(jnp.broadcast_to(all_rows[:1], (HEAD_DIM, rows)))[:, :1] / width
    grad_normed = normed_sum.total()
    unit_share = x_ref[:, lanes].astype(F32) * inverse_one
    places = share // rows
    gain_share = []
    for place in range(places):
        at = pl.multiple_of((z * places + place) * small_rows + gain_at, 16)
        gain_share.append(small_all[pl.ds(at, 16), :rows][:1].astype(F32))
    scaled = grad_normed * jnp.concatenate(gain_share, axis=1)
    grad_rows = grad_hidden[:, lanes] + inverse_one * (scaled - unit_share * mean)
    both = jnp.concatenate([layer_rows, grad_rows.astype(BF16)], axis=1)
    home_send[...] = dot_tn(recv_ref[...], both).astype(BF16)
    home = Straight(
        "ep",
        ep_count,
        lambda target: home_send.at[pl.ds(pl.multiple_of(target * per_pair, per_pair), per_pair)],
        lambda j: home_recv.at[pl.ds(pl.multiple_of(e * per_pair, per_pair), per_pair)],
        *home_sems,
    )
    home.begin()
    norm_sums = fold(grad_normed * unit_share)
    for place in range(places):
        at = pl.multiple_of((z * places + place) * 8, 8)
        sums[pl.ds(at, 8), :rows] = norm_sums[:, place * rows : (place + 1) * rows]
    over_plane = Straight(
        "ep",
        ep_count,
        lambda target: sums.at[pl.ds(pl.multiple_of(target * 8, 8), 8)],
        lambda j: sums_near.at[j - 1],
        *sum_sems,
    )
    over_plane.begin()
    mine = pl.ds(pl.multiple_of(e * per_pair, per_pair), per_pair)
    home_recv[mine, :] = home_send[mine, :]
    over_plane.wait()
    plane_sums = sums[pl.ds(pl.multiple_of(e * 8, 8), 8), :]
    for j in range(1, ep_count):
        plane_sums = plane_sums + sums_near[j - 1]
    sums_line[0] = plane_sums
    over_line = Straight(
        "tp", tp_count, lambda _: sums_line.at[0], lambda j: sums_line.at[j], *sum_line_sems
    )
    over_line.begin()
    for j in range(1, ep_count):
        source = (e + ep_count - j) % ep_count
        block = home_recv.at[pl.ds(pl.multiple_of(source * per_pair, per_pair), per_pair)]
        send_to(block, block, home_sems[0].at[j - 1], home_sems[1].at[j - 1], ep=source).wait_recv()
    arrived = dot_tn(send_ref[...], home_recv[...])
    layer_out[...] = arrived[:, :share].astype(BF16)
    layer_grad[...] = arrived[:, share:]
    over_line.wait()
    line_sums = plane_sums
    for j in range(1, tp_count):
        line_sums = line_sums + sums_line[j]
    sums_out[:, :rows] = line_sums[:, :rows]
    sums_out[:, rows : 2 * rows] = plane_sums[:, rows : 2 * rows]
    sums_out[:, 2 * rows :] = line_sums[:, 2 * rows :]
    for k in range(HALF):
        total = in_sum.total(k)
        at = pl.ds(k * half, half)
        d_query[at, :] = total[:, :q_width]
        d_key[at, :] = total[:, q_width : q_width + HEAD_DIM]
        d_value[at, :] = total[:, q_width + HEAD_DIM :]
    for op in (
        mixed_sum,
        normed_sum,
        over_rows,
        home,
        over_plane,
        over_line,
        out_sum,
        in_sum,
    ):
        op.sent()


def back_call(gain_at, ep_count, tp_count, operands, w_in_all, w_out_all):
    grad_moe, x = operands[0], operands[2]
    rows, width = x.shape
    share = width // tp_count
    in_width = w_in_all.shape[1]
    q_width = w_out_all.shape[1]
    heads = q_width // HEAD_DIM
    half = rows // HALF
    everything = rows * ep_count
    sums_width = 2 * rows + 2 * HEAD_DIM
    shape = jax.ShapeDtypeStruct

    def pair(count):
        return [pltpu.SemaphoreType.DMA((count,))] * 2

    return pl.pallas_call(
        functools.partial(back_body, gain_at, ep_count, tp_count, rows, heads),
        out_shape=(
            shape((rows, share), BF16),
            shape((rows, share), F32),
            shape((rows, q_width), F32),
            shape((rows, HEAD_DIM), F32),
            shape((rows, HEAD_DIM), F32),
            shape((rows, q_width), F32),
            shape((8, sums_width), F32),
        ),
        in_specs=[vmem_spec()] * len(operands) + [any_spec()] * 2,
        out_specs=tuple([vmem_spec()] * 7),
        scratch_shapes=[
            pltpu.VMEM((everything, in_width), BF16),
            pltpu.VMEM((everything, q_width), BF16),
            pltpu.VMEM((rows, width), F32),
            pltpu.VMEM((rows, width), BF16),
            pltpu.VMEM((heads * rows, HEAD_DIM), BF16),
            pltpu.VMEM((heads * rows, HEAD_DIM), F32),
            pltpu.VMEM((rows, in_width), BF16),
            pltpu.VMEM((rows, width), BF16),
            pltpu.VMEM((tp_count - 1, rows, share), BF16),
            pltpu.VMEM((tp_count - 1, rows, share), BF16),
            pltpu.VMEM((8, rows), F32),
            pltpu.VMEM((tp_count - 1, 8, rows), F32),
            pltpu.VMEM((8 * ep_count, sums_width), F32),
            pltpu.VMEM((ep_count - 1, 8, sums_width), F32),
            pltpu.VMEM((tp_count, 8, sums_width), F32),
            pltpu.VMEM((rows, 2 * share), BF16),
            pltpu.VMEM((rows, 2 * share), BF16),
            pltpu.VMEM((everything, q_width), BF16),
            pltpu.VMEM((everything, in_width), BF16),
        ]
        + plane_sum_scratch(half, q_width)
        + plane_sum_scratch(half, in_width)
        + pair(tp_count - 1) * 3
        + pair(ep_count - 1)
        + pair(tp_count - 1)
        + pair(ep_count - 1)
        + [pltpu.SemaphoreType.DMA((2,))],
        compiler_params=comm_params(4),
        name="back",
    )(*operands, w_in_all, w_out_all)


def plain_layer(
    layer_in,
    token_order,
    seq_lengths,
    routes,
    route_weights,
    w_query,
    w_key,
    w_value,
    w_out,
    norm_attn,
    norm_moe,
    query_gain,
    key_gain,
    w_gate,
    w_up,
    w_down,
    grad_out,
):
    ep_count = lax.axis_size("ep")
    tp_count = lax.axis_size("tp")
    tp_index = lax.axis_index("tp")
    ep_index = lax.axis_index("ep")
    local_experts, hidden_here, model_width = w_gate.shape
    experts = local_experts * ep_count
    rows_dev = layer_in.shape[0]
    micro_rows = rows_dev // MICRO
    share_width = layer_in.shape[1]
    score_scale = HEAD_DIM ** (-0.5)

    send, recv = deal_matrices(token_order, ep_index, rows_dev, ep_count)
    both = jnp.concatenate([layer_in, grad_out], axis=1)
    got = permute_rows(recv, exchange(permute_rows(send, both), ep_count))
    layer_full = lax.all_gather(got[:, :share_width], "tp", axis=1, tiled=True)
    grad_full = lax.all_gather(got[:, share_width:], "tp", axis=1, tiled=True)

    q_width, kv_width = w_query.shape[1], w_key.shape[1]
    packed = jnp.concatenate([w_query, w_out, w_key, w_value], axis=1)
    packed = lax.all_gather(packed, "ep", axis=0, tiled=True)
    full_query = packed[:, :q_width]
    full_out = packed[:, q_width : 2 * q_width]
    full_kv = packed[:, 2 * q_width :]
    gains = jnp.concatenate([norm_attn, norm_moe, query_gain, key_gain]).reshape(1, -1)
    gains = lax.all_gather(gains, "ep", axis=0, tiled=True).astype(F32)
    part = norm_attn.shape[0]
    head_part = query_gain.shape[0]
    gain_attn = gains[:, :part].reshape(-1)
    gain_moe = gains[:, part : 2 * part].reshape(-1)
    gain_query = gains[:, 2 * part : 2 * part + head_part].reshape(-1)
    gain_key = gains[:, 2 * part + head_part :].reshape(-1)

    expert_ids = jnp.arange(experts, dtype=jnp.int32)
    dense = jnp.sum(
        jnp.where(routes[:, :, None] == expert_ids[None, None, :], route_weights[:, :, None], 0.0),
        axis=1,
    )
    scale_all = lax.all_gather(dense, "ep", axis=0, tiled=True)
    scale = lax.dynamic_slice_in_dim(scale_all, ep_index * local_experts, local_experts, 1)
    all_grad = lax.all_gather(grad_full, "ep", axis=0, tiled=True)

    heads_here = q_width // HEAD_DIM
    kv_here = kv_width // HEAD_DIM
    group_size = heads_here // kv_here
    segment, position = jax.vmap(positions_of, in_axes=(0, None))(seq_lengths, micro_rows)
    cosine, sine_table = rope_tables(position.reshape(-1), HEAD_DIM // 2)
    layer_float = layer_full.astype(F32)
    inverse_one = inverse_rms(layer_float)
    unit_one = layer_float * inverse_one
    normed = (unit_one * gain_attn).astype(BF16)
    query_proj = dot_nn(normed, full_query).reshape(rows_dev, heads_here, HEAD_DIM)
    kv_proj = dot_nn(normed, full_kv)
    key_proj = kv_proj[:, :kv_width].reshape(rows_dev, kv_here, HEAD_DIM)
    value_proj = kv_proj[:, kv_width:].reshape(rows_dev, kv_here, HEAD_DIM)
    inverse_query = inverse_rms(query_proj)
    unit_query = query_proj * inverse_query
    inverse_key = inverse_rms(key_proj)
    unit_key = key_proj * inverse_key
    queries = (
        rotate(unit_query * gain_query, cosine, sine_table)
        .astype(BF16)
        .reshape(MICRO, micro_rows, kv_here, group_size, HEAD_DIM)
    )
    key_rows = (
        rotate(unit_key * gain_key, cosine, sine_table)
        .astype(BF16)
        .reshape(MICRO, micro_rows, kv_here, HEAD_DIM)
    )
    values = value_proj.astype(BF16).reshape(MICRO, micro_rows, kv_here, HEAD_DIM)
    scores = (
        jnp.einsum("mqkgd,mtkd->mkgqt", queries, key_rows, preferred_element_type=F32)
        * score_scale
    )
    offsets = jnp.arange(micro_rows, dtype=jnp.int32)
    allowed = (segment[:, :, None] == segment[:, None, :]) & (
        offsets[None, None, :] <= offsets[None, :, None]
    )
    scores = jnp.where(allowed[:, None, None], scores, -1e30)
    row_peak = jnp.max(scores, axis=-1, keepdims=True)
    exponent = jnp.exp(scores - row_peak)
    attn_probs = exponent / jnp.sum(exponent, axis=-1, keepdims=True)
    probs_low = attn_probs.astype(BF16)
    context = jnp.einsum("mkgqt,mtkd->mqkgd", probs_low, values, preferred_element_type=F32)
    context_low = context.reshape(rows_dev, heads_here * HEAD_DIM).astype(BF16)
    attn_part = dot_nt(context_low, full_out)
    attn_out = lax.psum(attn_part.astype(BF16), "tp").astype(F32)
    hidden = layer_float + attn_out
    inverse_two = inverse_rms(hidden)
    unit_two = hidden * inverse_two
    moe_in = (unit_two * gain_moe).astype(BF16)

    all_in = lax.all_gather(moe_in, "ep", axis=0, tiled=True)
    flat = local_experts * hidden_here
    gate_matrix = w_gate.reshape(flat, model_width)
    up_matrix = w_up.reshape(flat, model_width)
    down_matrix = w_down.reshape(flat, model_width)
    row_scale = jnp.repeat(scale, hidden_here, axis=1)
    gate_pre = dot_nt(all_in, gate_matrix)
    up_pre = dot_nt(all_in, up_matrix)
    grad_active = dot_nt(all_grad, down_matrix) * row_scale
    sigmoid_gate = jax.nn.sigmoid(gate_pre)
    silu_gate = gate_pre * sigmoid_gate
    active = (silu_gate * up_pre * row_scale).astype(BF16)
    grad_up_pre = (grad_active * silu_gate).astype(BF16)
    grad_gate_pre = (
        grad_active * up_pre * sigmoid_gate * (1.0 + gate_pre * (1.0 - sigmoid_gate))
    ).astype(BF16)
    grad_partial = dot_nn(grad_gate_pre, gate_matrix) + dot_nn(grad_up_pre, up_matrix)
    grad_partial = lax.psum_scatter(
        grad_partial.astype(BF16), "ep", scatter_dimension=0, tiled=True
    )
    grad_share = lax.psum_scatter(grad_partial, "tp", scatter_dimension=1, tiled=True)
    out_partial = dot_nn(active, down_matrix)
    out_partial = lax.psum_scatter(out_partial.astype(BF16), "ep", scatter_dimension=0, tiled=True)
    mixed = lax.psum_scatter(out_partial, "tp", scatter_dimension=1, tiled=True)
    hidden_share = lax.dynamic_slice_in_dim(hidden, tp_index * share_width, share_width, 1)
    layer_dealt = (hidden_share + mixed.astype(F32)).astype(BF16)
    grad_w_down = dot_tn(active, all_grad).reshape(w_down.shape)
    grad_w_gate = dot_tn(grad_gate_pre, all_in).reshape(w_gate.shape)
    grad_w_up = dot_tn(grad_up_pre, all_in).reshape(w_up.shape)

    grad_float = grad_full.astype(F32)
    grad_moe_in = lax.all_gather(grad_share, "tp", axis=1, tiled=True).astype(F32)
    norm_moe_part = jnp.sum(grad_moe_in * unit_two, axis=0)
    grad_hidden = grad_float + norm_back(grad_moe_in * gain_moe, unit_two, inverse_two)
    grad_attn = grad_hidden.astype(BF16)
    grad_w_out = dot_tn(grad_attn, context_low)
    grad_context = (
        dot_nn(grad_attn, full_out)
        .astype(BF16)
        .reshape(MICRO, micro_rows, kv_here, group_size, HEAD_DIM)
    )
    grad_probs = jnp.einsum("mqkgd,mtkd->mkgqt", grad_context, values, preferred_element_type=F32)
    prob_delta = jnp.sum(attn_probs * grad_probs, axis=-1, keepdims=True)
    grad_scores = (attn_probs * (grad_probs - prob_delta)).astype(BF16)
    grad_queries = (
        jnp.einsum("mkgqt,mtkd->mqkgd", grad_scores, key_rows, preferred_element_type=F32).reshape(
            rows_dev, heads_here, HEAD_DIM
        )
        * score_scale
    )
    grad_keys = (
        jnp.einsum("mkgqt,mqkgd->mtkd", grad_scores, queries, preferred_element_type=F32).reshape(
            rows_dev, kv_here, HEAD_DIM
        )
        * score_scale
    )
    grad_values = jnp.einsum(
        "mkgqt,mqkgd->mtkd", probs_low, grad_context, preferred_element_type=F32
    )
    grad_unit_query = rotate_back(grad_queries, cosine, sine_table)
    grad_unit_key = rotate_back(grad_keys, cosine, sine_table)
    query_gain_part = jnp.sum(grad_unit_query * unit_query, axis=(0, 1))
    key_gain_part = jnp.sum(grad_unit_key * unit_key, axis=(0, 1))
    grad_query_proj = (
        norm_back(grad_unit_query * gain_query, unit_query, inverse_query)
        .reshape(rows_dev, heads_here * HEAD_DIM)
        .astype(BF16)
    )
    grad_key_proj = (
        norm_back(grad_unit_key * gain_key, unit_key, inverse_key)
        .reshape(rows_dev, kv_width)
        .astype(BF16)
    )
    grad_value_proj = grad_values.reshape(rows_dev, kv_width).astype(BF16)
    grad_kv_proj = jnp.concatenate([grad_key_proj, grad_value_proj], axis=1)
    normed_part = dot_nt(grad_query_proj, full_query) + dot_nt(grad_kv_proj, full_kv)
    grad_normed = lax.psum_scatter(
        normed_part.astype(BF16), "tp", scatter_dimension=1, tiled=True
    ).astype(F32)
    grad_packed = jnp.concatenate(
        [
            dot_tn(normed, grad_query_proj).astype(BF16),
            grad_w_out.astype(BF16),
            dot_tn(normed, grad_kv_proj).astype(BF16),
        ],
        axis=1,
    )
    grad_packed = lax.psum_scatter(grad_packed, "ep", scatter_dimension=0, tiled=True).astype(F32)

    start = tp_index * share_width
    gain_share = lax.dynamic_slice_in_dim(gain_attn, start, share_width, 0)
    unit_share = lax.dynamic_slice_in_dim(unit_one, start, share_width, 1)
    hidden_grad_share = lax.dynamic_slice_in_dim(grad_hidden, start, share_width, 1)
    scaled = grad_normed * gain_share
    row_mean = lax.psum(jnp.sum(scaled * unit_share, axis=1), "tp") / model_width
    grad_layer = hidden_grad_share + inverse_one * (scaled - unit_share * row_mean[:, None])
    norm_attn_part = lax.dynamic_update_slice_in_dim(
        jnp.zeros((model_width,), F32), jnp.sum(grad_normed * unit_share, axis=0), start, 0
    )
    small = jnp.concatenate(
        [norm_attn_part, norm_moe_part / tp_count, query_gain_part, key_gain_part]
    )
    small = lax.psum(small, ("ep", "tp"))
    grad_norm_attn = lax.dynamic_slice_in_dim(small, ep_index * part, part, 0)
    grad_norm_moe = lax.dynamic_slice_in_dim(small, model_width + ep_index * part, part, 0)
    grad_query_gain = lax.dynamic_slice_in_dim(
        small, 2 * model_width + ep_index * head_part, head_part, 0
    )
    grad_key_gain = lax.dynamic_slice_in_dim(
        small, 2 * model_width + HEAD_DIM + ep_index * head_part, head_part, 0
    )

    back = jnp.concatenate([layer_dealt, grad_layer.astype(BF16)], axis=1)
    home = exchange(dot_tn(recv, back).astype(BF16), ep_count)
    home = dot_tn(send, home)
    return (
        home[:, :share_width].astype(BF16),
        home[:, share_width:],
        grad_packed[:, :q_width],
        grad_packed[:, 2 * q_width : 2 * q_width + kv_width],
        grad_packed[:, 2 * q_width + kv_width :],
        grad_packed[:, q_width : 2 * q_width],
        grad_norm_attn,
        grad_norm_moe,
        grad_query_gain,
        grad_key_gain,
        grad_w_gate,
        grad_w_up,
        grad_w_down,
    )


def route_scales(routes, route_weights, experts, local_experts, hidden_here, ep_index):
    expert_ids = jnp.arange(experts, dtype=jnp.int32)
    dense = jnp.sum(
        jnp.where(
            routes.T[None, :, :] == expert_ids[:, None, None], route_weights.T[None, :, :], 0.0
        ),
        axis=1,
    )
    terms = []
    for _ in range(SCALE_TERMS):
        terms.append(lax.reduce_precision(dense, 8, 7))
        dense = dense - terms[-1]
    parts = jnp.concatenate(terms, axis=0).astype(BF16)
    flat_expert = ep_index * local_experts + jnp.repeat(
        jnp.arange(local_experts, dtype=jnp.int32), hidden_here
    )
    part_expert = jnp.arange(parts.shape[0], dtype=jnp.int32) % experts
    return (parts, (part_expert[:, None] == flat_expert[None, :]).astype(BF16))


def plane_layer(
    layer_in,
    token_order,
    seq_lengths,
    routes,
    route_weights,
    w_query,
    w_key,
    w_value,
    w_out,
    norm_attn,
    norm_moe,
    query_gain,
    key_gain,
    w_gate,
    w_up,
    w_down,
    grad_out,
):
    ep_count = lax.axis_size("ep")
    tp_count = lax.axis_size("tp")
    tp_index = lax.axis_index("tp")
    ep_index = lax.axis_index("ep")
    local_experts, hidden_here, model_width = w_gate.shape
    experts = local_experts * ep_count
    rows_dev = layer_in.shape[0]
    micro_rows = rows_dev // MICRO
    share_width = layer_in.shape[1]
    score_scale = HEAD_DIM ** (-0.5)

    q_width, kv_width = w_query.shape[1], w_key.shape[1]
    heads_here = q_width // HEAD_DIM
    kv_here = kv_width // HEAD_DIM
    group_size = heads_here // kv_here
    send, recv = deal_matrices(token_order, ep_index, rows_dev, ep_count)
    send_rows = permute_rows(send, jnp.concatenate([layer_in, grad_out], axis=1))
    part = norm_attn.shape[0]
    head_part = query_gain.shape[0]
    scale_parts, pick = route_scales(
        routes, route_weights, experts, local_experts, hidden_here, ep_index
    )
    gain_at = scale_parts.shape[0]
    gains = jnp.zeros((1, 2 * part + 2 * HEAD_DIM), BF16)
    for vector, at in (
        (norm_attn, 0),
        (norm_moe, part),
        (query_gain, 2 * part + ep_index * head_part),
        (key_gain, 2 * part + HEAD_DIM + ep_index * head_part),
    ):
        gains = lax.dynamic_update_slice(gains, vector[None], (0, at))
    small_rows = -(-(gain_at + 1) // 32) * 32
    small = jnp.pad(scale_parts, ((0, 0), (0, gains.shape[1] - scale_parts.shape[1])))
    small = jnp.pad(
        jnp.concatenate([small, gains], axis=0), ((0, small_rows - gain_at - 1), (0, 0))
    )
    segment, position = jax.vmap(positions_of, in_axes=(0, None))(seq_lengths, micro_rows)
    cosine, sine_table = rope_tables(position.reshape(-1), HEAD_DIM // 2)
    cosine_wide = jnp.concatenate([cosine[:, 0], cosine[:, 0]], axis=1)
    sine_wide = jnp.concatenate([-sine_table[:, 0], sine_table[:, 0]], axis=1)
    offsets = jnp.arange(micro_rows, dtype=jnp.int32)
    allowed = (segment[:, :, None] == segment[:, None, :]) & (
        offsets[None, None, :] <= offsets[None, :, None]
    )
    mask = allowed.astype(F32).reshape(rows_dev, micro_rows)
    (
        layer_full,
        grad_full,
        hidden,
        moe_in,
        proj,
        turned,
        key_flat,
        value_flat,
        probs,
        context_low,
        small_all,
        normed,
        all_grad,
        w_in_all,
        full_out,
    ) = front_call(
        gain_at,
        ep_count,
        tp_count,
        send_rows,
        recv,
        small,
        cosine_wide,
        sine_wide,
        mask,
        w_query,
        w_key,
        w_value,
        w_out,
    )

    flat = local_experts * hidden_here
    gate_matrix = w_gate.reshape(flat, model_width)
    up_matrix = w_up.reshape(flat, model_width)
    down_matrix = w_down.reshape(flat, model_width)
    grad_partial, active, grad_w_gate, grad_w_up, grad_w_down = expert_call(
        moe_in, all_grad, small_all, pick, gate_matrix, up_matrix, down_matrix
    )
    grad_moe_in, mixed_plane = mix_call(grad_partial, active, down_matrix, tp_count)
    layer_out, layer_grad, d_query, d_key, d_value, d_out, sums = back_call(
        gain_at,
        ep_count,
        tp_count,
        (
            grad_moe_in,
            mixed_plane,
            layer_full,
            hidden,
            grad_full,
            normed,
            proj,
            turned,
            key_flat,
            value_flat,
            probs,
            context_low,
            small_all,
            cosine_wide,
            sine_wide,
            send,
            recv,
        ),
        w_in_all,
        full_out,
    )
    sums = jnp.sum(sums, axis=0)
    head_at = 2 * part + ep_index * head_part
    return (
        layer_out,
        layer_grad,
        d_query,
        d_key,
        d_value,
        d_out,
        sums[:part],
        sums[part : 2 * part],
        lax.dynamic_slice_in_dim(sums, head_at, head_part, 0),
        lax.dynamic_slice_in_dim(sums, head_at + HEAD_DIM, head_part, 0),
        grad_w_gate.reshape(w_gate.shape),
        grad_w_up.reshape(w_up.shape),
        grad_w_down.reshape(w_down.shape),
    )


def solution(mesh):
    return jax.shard_map(
        on_device,
        mesh=mesh,
        in_specs=(
            P("ep", "tp"),
            P(),
            P("ep", None),
            P("ep", None),
            P("ep", None),
            P("ep", "tp"),
            P("ep", "tp"),
            P("ep", "tp"),
            P("ep", "tp"),
            P("ep"),
            P("ep"),
            P("ep"),
            P("ep"),
            P("ep", "tp", None),
            P("ep", "tp", None),
            P("ep", "tp", None),
            P("ep", "tp"),
        ),
        out_specs=(
            P("ep", "tp"),
            P("ep", "tp"),
            P("ep", "tp"),
            P("ep", "tp"),
            P("ep", "tp"),
            P("ep", "tp"),
            P("ep"),
            P("ep"),
            P("ep"),
            P("ep"),
            P("ep", "tp", None),
            P("ep", "tp", None),
            P("ep", "tp", None),
        ),
        check_vma=False,
    )


def solution(mesh):
    shape = dict(mesh.shape)
    planes = shape["ep"] == 8 and shape["tp"] == 4
    return jax.shard_map(
        plane_layer if planes else plain_layer,
        mesh=mesh,
        in_specs=(
            P("ep", "tp"),
            P(),
            P("ep", None),
            P("ep", None),
            P("ep", None),
            P("ep", "tp"),
            P("ep", "tp"),
            P("ep", "tp"),
            P("ep", "tp"),
            P("ep"),
            P("ep"),
            P("ep"),
            P("ep"),
            P("ep", "tp", None),
            P("ep", "tp", None),
            P("ep", "tp", None),
            P("ep", "tp"),
        ),
        out_specs=(
            P("ep", "tp"),
            P("ep", "tp"),
            P("ep", "tp"),
            P("ep", "tp"),
            P("ep", "tp"),
            P("ep", "tp"),
            P("ep"),
            P("ep"),
            P("ep"),
            P("ep"),
            P("ep", "tp", None),
            P("ep", "tp", None),
            P("ep", "tp", None),
        ),
        check_vma=False,
    )
```

```python
import functools

import jax
import jax.numpy as jnp
from jax import lax
from jax.experimental import pallas as pl
from jax.experimental.pallas import tpu as pltpu
from jax.sharding import PartitionSpec as P

HEAD_DIM = 128
MICRO = 2
F32 = jnp.float32
BF16 = jnp.bfloat16
SCALE_TERMS = 3
VMEM_LIMIT = 66 * 1000 * 1000

epsilon = 1e-06
rope_base = 1000000.0


def positions_of(lengths, row_count):
    offsets = jnp.arange(row_count, dtype=jnp.int32)
    seq_ends = jnp.cumsum(lengths)
    segment = jnp.sum((offsets[:, None] >= seq_ends[None, :]).astype(jnp.int32), axis=1)
    starts = seq_ends - lengths
    in_segment = segment[:, None] == jnp.arange(lengths.shape[0], dtype=jnp.int32)[None, :]
    position = offsets - jnp.sum(jnp.where(in_segment, starts[None, :], 0), axis=1)
    return (segment, position)


def rope_tables(position, half_dim):
    frequency = rope_base ** (-jnp.arange(half_dim, dtype=F32) / half_dim)
    angles = position.astype(F32)[:, None] * frequency[None, :]
    return (jnp.cos(angles)[:, None, :], jnp.sin(angles)[:, None, :])


def rotate(values, cosine, sine_table):
    half_dim = values.shape[-1] // 2
    first_half = values[..., :half_dim]
    second_half = values[..., half_dim:]
    return jnp.concatenate(
        [
            first_half * cosine - second_half * sine_table,
            second_half * cosine + first_half * sine_table,
        ],
        axis=-1,
    )


def rotate_back(incoming, cosine, sine_table):
    return rotate(incoming, cosine, -sine_table)


def deal_matrices(token_order, ep_index, rows_dev, ep_count):
    per_pair = rows_dev // ep_count
    rows = jnp.arange(rows_dev, dtype=jnp.int32)
    home = ep_index * rows_dev + rows
    at = jnp.arange(token_order.shape[0], dtype=jnp.int32)
    place = jnp.sum(jnp.where(token_order[None, :] == home[:, None], at[None, :], 0), axis=1)
    dest = place // rows_dev
    rank = jnp.sum(
        ((dest[:, None] == dest[None, :]) & (place[None, :] < place[:, None])).astype(jnp.int32),
        axis=1,
    )
    send_slot = dest * per_pair + rank
    send = (send_slot[None, :] == rows[:, None]).astype(BF16)
    mine = lax.dynamic_slice_in_dim(token_order, ep_index * rows_dev, rows_dev, 0)
    source = mine // rows_dev
    my_rank = jnp.sum(
        ((source[:, None] == source[None, :]) & (rows[None, :] < rows[:, None])).astype(jnp.int32),
        axis=1,
    )
    recv_slot = source * per_pair + my_rank
    recv = (recv_slot[:, None] == rows[None, :]).astype(BF16)
    return (send, recv)


def inverse_rms(values):
    return lax.rsqrt(jnp.mean(values * values, axis=-1, keepdims=True) + epsilon)


def norm_back(grad_unit, unit_values, inverse):
    return inverse * (
        grad_unit - unit_values * jnp.mean(grad_unit * unit_values, axis=-1, keepdims=True)
    )


def dot_nn(left, right):
    return jnp.dot(left, right, preferred_element_type=F32)


def dot_tn(left_rows, right_rows):
    return lax.dot_general(
        left_rows, right_rows, (((0,), (0,)), ((), ())), preferred_element_type=F32
    )


def dot_nt(left_rows, right_matrix):
    return lax.dot_general(
        left_rows, right_matrix, (((1,), (1,)), ((), ())), preferred_element_type=F32
    )


def permute_rows(matrix, rows):
    return dot_nn(matrix, rows).astype(BF16)


def exchange(rows, ep_count):
    split = rows.reshape(ep_count, rows.shape[0] // ep_count, rows.shape[1])
    moved = lax.all_to_all(split, "ep", split_axis=0, concat_axis=0, tiled=True)
    return moved.reshape(rows.shape)


MESH_ID = pl.DeviceIdType.MESH
HALF = 2
E0, E1, P0, P1, A0, B0, PA0, PB0, A1, B1, PA1, PB1, D0, PD0, D1, PD1 = range(16)
SLOT_E, SLOT_P, SLOT_A, SLOT_B = (E0, E1), (P0, P1), (A0, A1), (B0, B1)
SLOT_D, SLOT_PA, SLOT_PB, SLOT_PD = (D0, D1), (PA0, PA1), (PB0, PB1), (PD0, PD1)
FOR_PARTNER = (P0, P1, PB0, PB1, PA0, PA1, PD0, PD1)


def roles():
    e = lax.axis_index("ep")
    core, x, y = e % 2, (e // 2) % 2, e // 4
    other = 1 - 2 * core
    over_x, over_y = e + 2 - 4 * x, e + 4 - 8 * y
    a = over_x * (1 - core) + over_y * core
    b = over_y * (1 - core) + over_x * core
    d = over_x + over_y - e
    return dict(e=e, p=e + other, a=a, b=b, d=d, pa=a + other, pb=b + other, pd=d + other)


def slot_owner(r):
    names = ("e", "e", "p", "p", "a", "b", "pa", "pb", "a", "b", "pa", "pb", "d", "pd", "d", "pd")
    halves = (0, 1, 0, 1, 0, 0, 0, 0, 1, 1, 1, 1, 0, 0, 1, 1)
    return [(r[name], half) for name, half in zip(names, halves)]


def greet(plane, line):
    barrier = pltpu.get_barrier_semaphore()
    for device in plane:
        pl.semaphore_signal(barrier, inc=1, device_id={"ep": device}, device_id_type=MESH_ID)
    for device in line:
        pl.semaphore_signal(barrier, inc=1, device_id={"tp": device}, device_id_type=MESH_ID)
    pl.semaphore_wait(barrier, len(plane) + len(line))


def send_to(src, dst, send_sem, recv_sem, **device):
    return pltpu.make_async_remote_copy(
        src_ref=src,
        dst_ref=dst,
        send_sem=send_sem,
        recv_sem=recv_sem,
        device_id=device,
        device_id_type=MESH_ID,
    )


class PlaneGather:
    kinds = 7

    def __init__(self, r, held, half, send, recv):
        self.r, self.held, self.half, self.send, self.recv = r, held, half, send, recv

    def slot(self, index):
        return self.held.at[pl.ds(index * self.half, self.half)]

    def copy(self, kind, k):
        source, target, device = (
            (SLOT_E, SLOT_A, "a"),
            (SLOT_E, SLOT_B, "b"),
            (SLOT_E, SLOT_P, "p"),
            (SLOT_A, SLOT_D, "b"),
            (SLOT_A, SLOT_PB, "p"),
            (SLOT_B, SLOT_PA, "p"),
            (SLOT_D, SLOT_PD, "p"),
        )[kind]
        return send_to(
            self.slot(source[k]),
            self.slot(target[k]),
            self.send.at[kind, k],
            self.recv.at[kind, k],
            ep=self.r[device],
        )

    def begin(self):
        for k in range(HALF):
            for kind in range(3):
                self.copy(kind, k).start()

    def arrived(self, kind, k):
        self.copy(kind, k).wait_recv()

    def pass_near(self, k):
        self.arrived(0, k)
        self.copy(3, k).start()
        self.copy(4, k).start()
        self.arrived(1, k)
        self.copy(5, k).start()

    def pass_far(self, k):
        self.arrived(3, k)
        self.copy(6, k).start()

    def sent(self):
        for k in range(HALF):
            for kind in range(self.kinds):
                self.copy(kind, k).wait_send()


class PlaneSum:
    def __init__(self, r, part, near, far, first, second, half, sems):
        self.r, self.part, self.half = r, part, half
        self.near, self.far, self.first, self.second = near, far, first, second
        self.near_send, self.near_recv, self.send, self.recv = sems

    def slot(self, index):
        return self.part.at[pl.ds(index * self.half, self.half)]

    def rows(self, buffer, index):
        return buffer.at[pl.ds(index * self.half, self.half)]

    def near_copy(self, index):
        return send_to(
            self.slot(FOR_PARTNER[index]),
            self.rows(self.near, index),
            self.near_send.at[index],
            self.near_recv.at[index],
            ep=self.r["p"],
        )

    def far_copy(self, kind, k):
        source, target, device = (
            (SLOT_D, self.far, "b"),
            (SLOT_A, self.first, "a"),
            (SLOT_B, self.second, "b"),
        )[kind]
        return send_to(
            self.slot(source[k]),
            self.rows(target, k),
            self.send.at[kind, k],
            self.recv.at[kind, k],
            ep=self.r[device],
        )

    def add_up(self, slot, others):
        total = self.slot(slot)[...].astype(F32)
        for other in others:
            total = total + other[...].astype(F32)
        return total

    def near_sum(self, name, k):
        index = 2 * name + k
        slot = (SLOT_E, SLOT_A, SLOT_B, SLOT_D)[name][k]
        self.near_copy(index).wait_recv()
        return slot, [self.rows(self.near, index)]

    def pass_far(self, k):
        slot, others = self.near_sum(3, k)
        self.slot(slot)[...] = self.add_up(slot, others).astype(BF16)
        self.far_copy(0, k).start()

    def pass_second(self, k):
        slot, others = self.near_sum(2, k)
        self.slot(slot)[...] = self.add_up(slot, others).astype(BF16)
        self.far_copy(2, k).start()

    def pass_first(self, k):
        slot, others = self.near_sum(1, k)
        self.far_copy(0, k).wait_recv()
        self.slot(slot)[...] = self.add_up(slot, others + [self.rows(self.far, k)]).astype(BF16)
        self.far_copy(1, k).start()

    def total(self, k):
        slot, others = self.near_sum(0, k)
        self.far_copy(1, k).wait_recv()
        self.far_copy(2, k).wait_recv()
        return self.add_up(slot, others + [self.rows(self.first, k), self.rows(self.second, k)])

    def sent(self):
        for index in range(4 * HALF):
            self.near_copy(index).wait_send()
        for kind in range(3):
            for k in range(HALF):
                self.far_copy(kind, k).wait_send()


def plane_sum_scratch(half, width, kinds=3):
    return [
        pltpu.VMEM((8 * half, width), BF16),
        pltpu.VMEM((2 * half, width), BF16),
        pltpu.VMEM((2 * half, width), BF16),
        pltpu.VMEM((2 * half, width), BF16),
        pltpu.SemaphoreType.DMA((4 * HALF,)),
        pltpu.SemaphoreType.DMA((4 * HALF,)),
        pltpu.SemaphoreType.DMA((kinds, HALF)),
        pltpu.SemaphoreType.DMA((kinds, HALF)),
    ]


def any_spec():
    return pl.BlockSpec(memory_space=pl.ANY)


def vmem_spec():
    return pl.BlockSpec(memory_space=pltpu.VMEM)


def comm_params(collective_id):
    return pltpu.CompilerParams(
        collective_id=collective_id, has_side_effects=True, vmem_limit_bytes=VMEM_LIMIT
    )


def expert_body(
    flat,
    rows,
    parts,
    own_hbm,
    grad_hbm,
    scale_hbm,
    pick_ref,
    gate_hbm,
    up_hbm,
    down_hbm,
    total_ref,
    mixed_hbm,
    d_gate_hbm,
    d_up_hbm,
    d_down_hbm,
    held,
    grads,
    scales,
    both,
    down,
    grad_act,
    grad_both,
    active,
    d_weights,
    part,
    near,
    far,
    first,
    second,
    near_send,
    near_recv,
    sum_send,
    sum_recv,
    gather_send,
    gather_recv,
    mixed_near,
    mixed_send,
    mixed_recv,
    local_sem,
    grad_sem,
    out_sem,
    mixed_sem,
):
    r = roles()
    half = rows // HALF
    unit = 2 * half
    owners = slot_owner(r)
    loads = [
        pltpu.make_async_copy(own_hbm, held.at[pl.ds(0, rows)], local_sem.at[0]),
        pltpu.make_async_copy(gate_hbm, both.at[pl.ds(0, flat)], local_sem.at[1]),
        pltpu.make_async_copy(up_hbm, both.at[pl.ds(flat, flat)], local_sem.at[2]),
        pltpu.make_async_copy(down_hbm, down, local_sem.at[3]),
    ]
    for load in loads:
        load.start()
    stride = scale_hbm.shape[0] // 8
    slots = []
    for index, (owner, k) in enumerate(owners):
        slots.append(
            (
                pltpu.make_async_copy(
                    scale_hbm.at[pl.ds(owner * stride, parts), pl.ds(k * half, half)],
                    scales.at[index],
                    grad_sem.at[0, index],
                ),
                pltpu.make_async_copy(
                    grad_hbm.at[pl.ds(owner * rows + k * half, half)],
                    grads.at[pl.ds(index * half, half)],
                    grad_sem.at[1, index],
                ),
            )
        )
        for load in slots[-1]:
            load.start()
    greet([r["p"], r["a"], r["b"]], [])
    gather = PlaneGather(r, held, half, gather_send, gather_recv)
    loads[0].wait()
    gather.begin()
    for load in loads[1:]:
        load.wait()
    for pair in slots:
        for load in pair:
            load.wait()
    psum = PlaneSum(
        r, part, near, far, first, second, half, (near_send, near_recv, sum_send, sum_recv)
    )

    def expand(index):
        return jnp.concatenate(
            [dot_tn(scales[2 * index], pick_ref[...]), dot_tn(scales[2 * index + 1], pick_ref[...])],
            axis=0,
        )

    @pl.loop(0, 8)
    def _(index):
        at = pl.ds(pl.multiple_of(index * unit, unit), unit)
        grad_act[at, :] = dot_nt(grads[at, :], down[...]) * expand(index)

    @pl.loop(0, 8)
    def _(index):
        @pl.when(index == 1)
        def _():
            gather.arrived(2, 0)
            gather.arrived(2, 1)

        for k, first_unit in ((0, 2), (1, 4)):

            @pl.when(index == first_unit)
            def _():
                gather.pass_near(k)

            @pl.when(index == first_unit + 1)
            def _():
                gather.arrived(4, k)
                gather.arrived(5, k)

            @pl.when(index == 6 + k)
            def _():
                gather.pass_far(k)
                gather.arrived(6, k)

        at = pl.ds(pl.multiple_of(index * unit, unit), unit)
        pre = dot_nt(held[at, :], both[...])
        gate_pre, up_pre = pre[:, :flat], pre[:, flat:]
        grad_active = grad_act[at, :]
        sigmoid_gate = jax.nn.sigmoid(gate_pre)
        silu_gate = gate_pre * sigmoid_gate
        active[at, :] = (silu_gate * up_pre * expand(index)).astype(BF16)
        grad_both[at, flat:] = (grad_active * silu_gate).astype(BF16)
        grad_both[at, :flat] = (
            grad_active * up_pre * sigmoid_gate * (1.0 + gate_pre * (1.0 - sigmoid_gate))
        ).astype(BF16)
        part[at, :] = dot_nn(grad_both[at, :], both[...]).astype(BF16)

        @pl.when(index == 1)
        def _():
            psum.near_copy(0).start()
            psum.near_copy(1).start()

        for k, last_unit in ((0, 3), (1, 5)):

            @pl.when(index == last_unit)
            def _():
                psum.near_copy(2 + k).start()
                psum.near_copy(4 + k).start()

            @pl.when(index == last_unit + 1)
            def _():
                psum.pass_second(k)

            @pl.when(index == 6 + k)
            def _():
                psum.near_copy(6 + k).start()

    psum.pass_far(0)
    psum.pass_far(1)
    group = 128
    pieces = flat // group

    def weight_out(which):
        target = (d_down_hbm, d_gate_hbm, d_up_hbm)[which]
        return pltpu.make_async_copy(
            d_weights.at[pl.ds(which * flat, flat)], target, out_sem.at[which]
        )

    @pl.loop(0, pieces)
    def _(index):
        place = pl.ds(pl.multiple_of(index * group, group), group)
        d_weights[place, :] = dot_tn(active[:, place], grads[...]).astype(BF16)

    weight_out(0).start()

    mixed = PlaneSum(
        r, grads, mixed_near, None, None, None, half, (mixed_send, mixed_recv, None, None)
    )

    @pl.loop(0, 8)
    def _(step):
        index = (step + 6) % 8
        at = pl.ds(pl.multiple_of(index * unit, unit), unit)
        grads[at, :] = dot_nn(active[at, :], down[...]).astype(BF16)
        for unit_done, copies in ((6, (6,)), (7, (7,)), (1, (0, 1)), (3, (2, 4)), (5, (3, 5))):

            @pl.when(index == unit_done)
            def _():
                for copy in copies:
                    mixed.near_copy(copy).start()

    psum.pass_first(0)
    psum.pass_first(1)

    @pl.loop(0, 2 * pieces)
    def _(index):
        lanes = pl.ds(pl.multiple_of(index * group, group), group)
        place = pl.ds(pl.multiple_of(flat + index * group, group), group)
        d_weights[place, :] = dot_tn(grad_both[:, lanes], held[...]).astype(BF16)

    weight_out(1).start()
    weight_out(2).start()
    mixed_outs = []
    for name in range(4):
        for k in range(HALF):
            slot, others = mixed.near_sum(name, k)
            mixed.slot(slot)[...] = mixed.add_up(slot, others).astype(BF16)
            index = HALF * name + k
            mixed_outs.append(
                pltpu.make_async_copy(
                    mixed.slot(slot),
                    mixed_hbm.at[pl.ds(index * half, half)],
                    mixed_sem.at[index],
                )
            )
            mixed_outs[-1].start()
    for k in range(HALF):
        total_ref[pl.ds(k * half, half), :] = psum.total(k).astype(BF16)
    for which in range(3):
        weight_out(which).wait()
    for copy in mixed_outs:
        copy.wait()
    for index in range(4 * HALF):
        mixed.near_copy(index).wait_send()
    gather.sent()
    psum.sent()


def expert_call(own, all_grad, scale_parts, pick, gate_matrix, up_matrix, down_matrix):
    rows, width = own.shape
    flat = gate_matrix.shape[0]
    everything = all_grad.shape[0]
    parts = pick.shape[0]
    half = rows // HALF
    weight = jax.ShapeDtypeStruct((flat, width), BF16)
    return pl.pallas_call(
        functools.partial(expert_body, flat, rows, parts),
        out_shape=(
            jax.ShapeDtypeStruct((rows, width), BF16),
            jax.ShapeDtypeStruct((4 * rows, width), BF16),
            weight,
            weight,
            weight,
        ),
        in_specs=[any_spec(), any_spec(), any_spec(), vmem_spec()] + [any_spec()] * 3,
        out_specs=(vmem_spec(), any_spec(), any_spec(), any_spec(), any_spec()),
        scratch_shapes=[
            pltpu.VMEM((everything, width), BF16),
            pltpu.VMEM((everything, width), BF16),
            pltpu.VMEM((16, parts, half), BF16),
            pltpu.VMEM((2 * flat, width), BF16),
            pltpu.VMEM((flat, width), BF16),
            pltpu.VMEM((everything, flat), F32),
            pltpu.VMEM((everything, 2 * flat), BF16),
            pltpu.VMEM((everything, flat), BF16),
            pltpu.VMEM((3 * flat, width), BF16),
            pltpu.VMEM((everything, width), BF16),
        ]
        + plane_sum_scratch(half, width)
        + [
            pltpu.SemaphoreType.DMA((PlaneGather.kinds, HALF)),
            pltpu.SemaphoreType.DMA((PlaneGather.kinds, HALF)),
            pltpu.VMEM((4 * rows, width), BF16),
            pltpu.SemaphoreType.DMA((4 * HALF,)),
            pltpu.SemaphoreType.DMA((4 * HALF,)),
            pltpu.SemaphoreType.DMA((4,)),
            pltpu.SemaphoreType.DMA((2, 16)),
            pltpu.SemaphoreType.DMA((3,)),
            pltpu.SemaphoreType.DMA((4 * HALF,)),
        ],
        compiler_params=comm_params(1),
        name="experts",
    )(own, all_grad, scale_parts, pick, gate_matrix, up_matrix, down_matrix)


class LineSum:
    def __init__(self, count, source, arrived, send, recv):
        self.count, self.source, self.arrived, self.send, self.recv = (
            count,
            source,
            arrived,
            send,
            recv,
        )
        self.z = lax.axis_index("tp")
        self.share = source.shape[1] // count

    def columns(self, z):
        return pl.ds(pl.multiple_of(z * self.share, self.share), self.share)

    def copy(self, j):
        target = (self.z + j) % self.count
        return send_to(
            self.source.at[:, self.columns(target)],
            self.arrived.at[j - 1],
            self.send.at[j - 1],
            self.recv.at[j - 1],
            tp=target,
        )

    def begin(self):
        for j in range(1, self.count):
            self.copy(j).start()

    def total(self):
        total = self.source[:, self.columns(self.z)].astype(F32)
        for j in range(1, self.count):
            self.copy(j).wait_recv()
            total = total + self.arrived[j - 1].astype(F32)
        return total

    def sent(self):
        for j in range(1, self.count):
            self.copy(j).wait_send()


class OrderedGather(PlaneGather):
    def place(self, name, k):
        return self.held.at[pl.ds((self.r[name] * HALF + k) * self.half, self.half)]

    def copy(self, kind, k):
        source, device = (
            ("e", "a"),
            ("e", "b"),
            ("e", "p"),
            ("a", "b"),
            ("a", "p"),
            ("b", "p"),
            ("d", "p"),
        )[kind]
        block = self.place(source, k)
        return send_to(
            block, block, self.send.at[kind, k], self.recv.at[kind, k], ep=self.r[device]
        )

    def arrived(self, kind, k):
        source, device = (
            ("a", "a"),
            ("b", "b"),
            ("p", "p"),
            ("d", "b"),
            ("pb", "p"),
            ("pa", "p"),
            ("pd", "p"),
        )[kind]
        block = self.place(source, k)
        send_to(
            block, block, self.send.at[kind, k], self.recv.at[kind, k], ep=self.r[device]
        ).wait_recv()

    def finish(self):
        for k in range(HALF):
            for kind in (2, 4, 5, 6):
                self.arrived(kind, k)


class LineGather:
    def __init__(self, count, whole, up_send, up_recv, down_send, down_recv):
        self.count, self.whole = count, whole
        self.up_sems, self.down_sems = (up_send, up_recv), (down_send, down_recv)
        self.z = lax.axis_index("tp")
        self.share = whole.shape[1] // count

    def columns(self, z):
        return pl.ds(pl.multiple_of(z * self.share, self.share), self.share)

    def move(self, share, j, sems, target):
        block = self.whole.at[:, self.columns(share)]
        return send_to(block, block, sems[0].at[j - 1], sems[1].at[j - 1], tp=target)

    def up(self, j):
        return self.move(self.z - j + 1, j, self.up_sems, self.z + 1)

    def down(self, j):
        return self.move(self.z + j - 1, j, self.down_sems, self.z - 1)

    def sends(self, j, act):
        @pl.when((self.z < self.count - 1) & (self.z >= j - 1))
        def _():
            act(self.up(j))

        @pl.when((self.z > 0) & (self.z + j <= self.count))
        def _():
            act(self.down(j))

    def begin(self):
        self.sends(1, lambda copy: copy.start())

    def step(self, j):
        @pl.when(self.z >= j)
        def _():
            self.move(self.z - j, j, self.up_sems, self.z - 1).wait_recv()

        @pl.when(self.z + j < self.count)
        def _():
            self.move(self.z + j, j, self.down_sems, self.z + 1).wait_recv()

        if j + 1 < self.count:
            self.sends(j + 1, lambda copy: copy.start())

    def wait(self):
        for j in range(1, self.count):
            self.step(j)

    def sent(self):
        for j in range(1, self.count):
            self.sends(j, lambda copy: copy.wait_send())


def line_peers(count):
    z = lax.axis_index("tp")
    return [(z + j) % count for j in range(1, count)]


class FarSum:
    def __init__(self, r, part, far, first, second, half, send, recv):
        self.r, self.part, self.half = r, part, half
        self.far, self.first, self.second = far, first, second
        self.send, self.recv = send, recv

    def rows(self, buffer, index):
        return buffer.at[pl.ds(index * self.half, self.half)]

    def copy(self, kind, k):
        block, target, device = (
            (3, self.far, "b"),
            (1, self.first, "a"),
            (2, self.second, "b"),
        )[kind]
        return send_to(
            self.rows(self.part, HALF * block + k),
            self.rows(target, k),
            self.send.at[kind, k],
            self.recv.at[kind, k],
            ep=self.r[device],
        )

    def pass_first(self, k):
        self.copy(0, k).wait_recv()
        block = self.rows(self.part, HALF + k)
        block[...] = (block[...].astype(F32) + self.rows(self.far, k)[...].astype(F32)).astype(BF16)
        self.copy(1, k).start()

    def total(self, k):
        self.copy(1, k).wait_recv()
        self.copy(2, k).wait_recv()
        total = self.rows(self.part, k)[...].astype(F32)
        return total + self.rows(self.first, k)[...].astype(F32) + self.rows(self.second, k)[...].astype(F32)

    def sent(self):
        for kind in range(3):
            for k in range(HALF):
                self.copy(kind, k).wait_send()


def turn(values, cosine, sine_table):
    return values * cosine + pltpu.roll(values, HEAD_DIM // 2, 1) * sine_table


def unit_of(values):
    return values * lax.rsqrt(jnp.mean(values * values, axis=-1, keepdims=True) + epsilon)


def front_body(
    gain_at,
    ep_count,
    tp_count,
    rows,
    heads,
    send_ref,
    recv_ref,
    small_ref,
    cosine_ref,
    sine_ref,
    mask_ref,
    query_hbm,
    key_hbm,
    value_hbm,
    out_hbm,
    x_ref,
    grad_ref,
    hidden_ref,
    moe_ref,
    proj_ref,
    turned_ref,
    keys_ref,
    values_ref,
    probs_ref,
    context_ref,
    small_all,
    normed,
    all_grad,
    w_in_hbm,
    w_out_hbm,
    w_in,
    w_out,
    dealt,
    x_wire,
    grad_wire,
    back_wire,
    attn,
    line,
    deal_send,
    deal_recv,
    small_send,
    small_recv,
    in_send,
    in_recv,
    out_send,
    out_recv,
    grad_send,
    grad_recv,
    x_line,
    grad_line,
    back_line,
    line_send,
    line_recv,
    local_sem,
):
    r = roles()
    e = r["e"]
    z = lax.axis_index("tp")
    half = rows // HALF
    q_width = heads * HEAD_DIM
    share = x_wire.shape[1] // tp_count
    per_pair = rows // ep_count
    micro_rows = rows // MICRO
    own = pl.ds(e * rows, rows)
    loads = [
        pltpu.make_async_copy(query_hbm, w_in.at[own, pl.ds(0, q_width)], local_sem.at[0]),
        pltpu.make_async_copy(key_hbm, w_in.at[own, pl.ds(q_width, HEAD_DIM)], local_sem.at[1]),
        pltpu.make_async_copy(
            value_hbm, w_in.at[own, pl.ds(q_width + HEAD_DIM, HEAD_DIM)], local_sem.at[2]
        ),
        pltpu.make_async_copy(out_hbm, w_out.at[own], local_sem.at[3]),
    ]
    for load in loads:
        load.start()
    small_rows = small_ref.shape[0]
    small_all[pl.ds(e * small_rows, small_rows), :] = small_ref[...]
    others = [(e + j) % ep_count for j in range(1, ep_count)]
    greet(others, line_peers(tp_count))

    def deal(j, source, target):
        return send_to(
            send_ref.at[pl.ds(target * per_pair, per_pair)],
            dealt.at[pl.ds(source * per_pair, per_pair)],
            deal_send.at[j - 1],
            deal_recv.at[j - 1],
            ep=target,
        )

    for j in range(1, ep_count):
        deal(j, e, (e + j) % ep_count).start()
    mine = pl.ds(pl.multiple_of(e * per_pair, per_pair), per_pair)
    dealt[mine, :] = send_ref[mine, :]
    gather_small = OrderedGather(r, small_all, small_rows // HALF, small_send, small_recv)
    gather_in = OrderedGather(r, w_in, half, in_send, in_recv)
    gather_out = OrderedGather(r, w_out, half, out_send, out_recv)
    gather_grad = OrderedGather(r, all_grad, half, grad_send, grad_recv)
    gather_small.begin()
    for load in loads:
        load.wait()
    gather_in.begin()
    for j in range(1, ep_count):
        deal(j, (e + ep_count - j) % ep_count, (e + j) % ep_count).wait_recv()
    x_gather = LineGather(tp_count, x_wire, *[x_line.at[i] for i in range(4)])
    grad_gather = LineGather(tp_count, grad_wire, *[grad_line.at[i] for i in range(4)])
    x_wire[:, x_gather.columns(z)] = dealt[:, :share]
    grad_wire[:, x_gather.columns(z)] = dealt[:, share:]
    x_gather.begin()
    for k in range(HALF):
        gather_small.pass_near(k)
    x_gather.step(1)
    gather_in.pass_near(0)
    x_gather.step(2)
    grad_gather.begin()
    gather_in.pass_near(1)
    gather_out.begin()
    x_gather.step(3)
    for k in range(HALF):
        gather_small.pass_far(k)
    gather_small.finish()

    def gain_row(place, column, width):
        at = place * small_rows + gain_at
        return small_all[at : at + 1, column : column + width].astype(F32)

    x_rows = dot_nn(recv_ref[...], x_wire[...])
    x_ref[...] = x_rows.astype(BF16)
    unit_one = unit_of(x_rows)
    for place in range(ep_count):
        at = slice(place * rows, (place + 1) * rows)
        normed[:, at] = (unit_one[:, at] * gain_row(place, 0, rows)).astype(BF16)
    for k in range(HALF):
        gather_in.pass_far(k)
    grad_gather.step(1)
    gather_in.finish()
    gather_out.pass_near(0)

    proj_ref[...] = dot_nn(normed[...], w_in[...])
    grad_gather.step(2)
    gather_out.pass_near(1)
    column = 2 * rows
    gain_query = sum(gain_row(place, column, HEAD_DIM) for place in range(ep_count))
    gain_key = sum(gain_row(place, column + HEAD_DIM, HEAD_DIM) for place in range(ep_count))
    cosine, sine_table = cosine_ref[...], sine_ref[...]
    keys_ref[...] = turn(
        unit_of(proj_ref[:, q_width : q_width + HEAD_DIM]) * gain_key, cosine, sine_table
    ).astype(BF16)
    values_ref[...] = proj_ref[:, q_width + HEAD_DIM :].astype(BF16)

    grad_gather.step(3)
    grad_ref[...] = dot_nn(recv_ref[...], grad_wire[...]).astype(BF16)
    grad_here = pltpu.make_async_copy(grad_ref, all_grad.at[own], local_sem.at[4])
    grad_here.start()
    grad_here.wait()
    gather_grad.begin()

    @pl.loop(0, heads)
    def _(head):
        lanes = pl.ds(pl.multiple_of(head * HEAD_DIM, HEAD_DIM), HEAD_DIM)
        queries = turn(unit_of(proj_ref[:, lanes]) * gain_query, cosine, sine_table).astype(BF16)
        for micro in range(MICRO):
            at = pl.ds(
                pl.multiple_of((micro * heads + head) * micro_rows, micro_rows), micro_rows
            )
            turned_ref[at, :] = queries[micro * micro_rows : (micro + 1) * micro_rows]

    for k in range(HALF):
        gather_out.pass_far(k)
    for micro in range(MICRO):
        within = slice(micro * micro_rows, (micro + 1) * micro_rows)
        stacked = slice(micro * heads * micro_rows, (micro + 1) * heads * micro_rows)
        scores = dot_nt(turned_ref[stacked, :], keys_ref[within, :]) * HEAD_DIM ** (-0.5)
        mask = mask_ref[within, :]
        scores = scores.reshape(heads, micro_rows, micro_rows)
        scores = jnp.where(mask[None] > 0.0, scores, -1e30)
        exponent = jnp.exp(scores - jnp.max(scores, axis=-1, keepdims=True))
        probs = exponent / jnp.sum(exponent, axis=-1, keepdims=True)
        probs = probs.reshape(heads * micro_rows, micro_rows)
        probs_ref[stacked, :] = probs
        context = dot_nn(probs.astype(BF16), values_ref[within, :]).astype(BF16)
        for head in range(heads):
            context_ref[within, head * HEAD_DIM : (head + 1) * HEAD_DIM] = context[
                head * micro_rows : (head + 1) * micro_rows
            ]

    gather_out.finish()

    attn[...] = dot_nt(context_ref[...], w_out[...]).astype(BF16)
    over_line = LineSum(tp_count, attn, line, line_send, line_recv)
    over_line.begin()
    w_in_out = pltpu.make_async_copy(w_in, w_in_hbm, local_sem.at[0])
    w_out_out = pltpu.make_async_copy(w_out, w_out_hbm, local_sem.at[1])
    w_in_out.start()
    w_out_out.start()
    gather_grad.pass_near(0)
    total = over_line.total()
    back = LineGather(tp_count, back_wire, *[back_line.at[i] for i in range(4)])
    back_wire[:, back.columns(z)] = total.astype(BF16)
    back.begin()
    back.step(1)
    gather_grad.pass_near(1)
    back.step(2)
    gather_grad.pass_far(0)
    back.step(3)
    hidden = x_ref[...].astype(F32) + back_wire[...].astype(F32)
    hidden_ref[...] = hidden
    unit_two = unit_of(hidden)
    for place in range(ep_count):
        at = slice(place * rows, (place + 1) * rows)
        moe_ref[:, at] = (unit_two[:, at] * gain_row(place, rows, rows)).astype(BF16)
    gather_grad.pass_far(1)
    gather_grad.finish()
    for j in range(1, ep_count):
        deal(j, e, (e + j) % ep_count).wait_send()
    x_gather.sent()
    grad_gather.sent()
    back.sent()
    over_line.sent()
    for gather in (gather_small, gather_in, gather_out, gather_grad):
        gather.sent()
    w_in_out.wait()
    w_out_out.wait()


def front_call(
    gain_at, ep_count, tp_count, send_rows, recv, small, cosine, sine_table, mask, query, key, value, out
):
    rows = send_rows.shape[0]
    share = send_rows.shape[1] // 2
    width = share * tp_count
    q_width = query.shape[1]
    heads = q_width // HEAD_DIM
    everything = rows * ep_count
    in_width = q_width + 2 * HEAD_DIM
    micro_rows = rows // MICRO
    shape = jax.ShapeDtypeStruct
    gather_sems = pltpu.SemaphoreType.DMA((PlaneGather.kinds, HALF))
    line_sems = pltpu.SemaphoreType.DMA((4, tp_count - 1))
    return pl.pallas_call(
        functools.partial(front_body, gain_at, ep_count, tp_count, rows, heads),
        out_shape=(
            shape((rows, width), BF16),
            shape((rows, width), BF16),
            shape((rows, width), F32),
            shape((rows, width), BF16),
            shape((rows, in_width), F32),
            shape((heads * rows, HEAD_DIM), BF16),
            shape((rows, HEAD_DIM), BF16),
            shape((rows, HEAD_DIM), BF16),
            shape((heads * rows, micro_rows), F32),
            shape((rows, q_width), BF16),
            shape((ep_count * small.shape[0], small.shape[1]), BF16),
            shape((rows, width), BF16),
            shape((everything, width), BF16),
            shape((everything, in_width), BF16),
            shape((everything, q_width), BF16),
        ),
        in_specs=[vmem_spec()] * 6 + [any_spec()] * 4,
        out_specs=tuple([vmem_spec()] * 12 + [any_spec()] * 3),
        scratch_shapes=[
            pltpu.VMEM((everything, in_width), BF16),
            pltpu.VMEM((everything, q_width), BF16),
            pltpu.VMEM(send_rows.shape, BF16),
            pltpu.VMEM((rows, width), BF16),
            pltpu.VMEM((rows, width), BF16),
            pltpu.VMEM((rows, width), BF16),
            pltpu.VMEM((rows, width), BF16),
            pltpu.VMEM((tp_count - 1, rows, share), BF16),
            pltpu.SemaphoreType.DMA((ep_count - 1,)),
            pltpu.SemaphoreType.DMA((ep_count - 1,)),
        ]
        + [gather_sems] * 8
        + [line_sems] * 3
        + [pltpu.SemaphoreType.DMA((tp_count - 1,))] * 2
        + [pltpu.SemaphoreType.DMA((5,))],
        compiler_params=comm_params(3),
        name="front",
    )(send_rows, recv, small, cosine, sine_table, mask, query, key, value, out)


def fold(values):
    rows, width = values.shape
    return jnp.sum(values.reshape(rows // 8, 8, width), axis=0)


class Straight:
    def __init__(self, axis, count, source, landed, send, recv):
        self.axis, self.count, self.source, self.landed = axis, count, source, landed
        self.send, self.recv = send, recv
        self.me = lax.axis_index(axis)

    def copy(self, j):
        target = (self.me + j) % self.count
        return send_to(
            self.source(target),
            self.landed(j),
            self.send.at[j - 1],
            self.recv.at[j - 1],
            **{self.axis: target},
        )

    def begin(self):
        for j in range(1, self.count):
            self.copy(j).start()

    def wait(self):
        for j in range(1, self.count):
            self.copy(j).wait_recv()

    def sent(self):
        for j in range(1, self.count):
            self.copy(j).wait_send()


def back_body(
    gain_at,
    ep_count,
    tp_count,
    rows,
    heads,
    operand_count,
    partial_ref,
    mixed_hbm,
    w_in_hbm,
    w_out_hbm,
    *rest,
):
    operand_hbm, rest = rest[:operand_count], rest[operand_count:]
    outs, rest = rest[:5], rest[5:]
    operand_refs, rest = rest[:operand_count], rest[operand_count:]
    back_steps(
        gain_at,
        ep_count,
        tp_count,
        rows,
        heads,
        operand_hbm,
        operand_refs,
        partial_ref,
        mixed_hbm,
        w_in_hbm,
        w_out_hbm,
        *outs,
        *rest,
    )


def back_steps(
    gain_at,
    ep_count,
    tp_count,
    rows,
    heads,
    operand_hbm,
    operand_refs,
    partial_ref,
    mixed_hbm,
    w_in_hbm,
    w_out_hbm,
    layer_out,
    layer_grad,
    d_in,
    d_out,
    sums_out,
    w_in,
    w_out,
    mixed_part,
    mixed_far,
    mixed_first,
    mixed_second,
    mixed_ref,
    grad_moe_ref,
    grad_line,
    grad_attn,
    stacked_grad,
    grad_turned,
    grad_proj,
    normed_part,
    mixed_line,
    normed_line,
    row_sums,
    row_line,
    sums,
    sums_near,
    sums_line,
    home_send,
    home_recv,
    out_part,
    in_part,
    *rest,
):
    (
        x_ref,
        hidden_ref,
        grad_ref,
        normed_ref,
        proj_ref,
        turned_ref,
        keys_ref,
        values_ref,
        probs_ref,
        context_ref,
        small_all,
        cosine_ref,
        sine_ref,
        send_ref,
        recv_ref,
    ) = operand_refs
    out_bufs, out_sems = rest[0:4], rest[4:8]
    in_bufs, in_sems = rest[8:12], rest[12:16]
    mixed_sems, normed_sems, row_sems, sum_sems, sum_line_sems, home_sems = (
        rest[16:18],
        rest[18:20],
        rest[20:22],
        rest[22:24],
        rest[24:26],
        rest[26:28],
    )
    far_sems, grad_sems, gather_sem, operand_sem, mixed_sem, local_sem = (
        rest[28:30],
        rest[30:32],
        *rest[32:36],
    )
    r = roles()
    e = r["e"]
    z = lax.axis_index("tp")
    half = rows // HALF
    width = x_ref.shape[1]
    share = width // tp_count
    q_width = heads * HEAD_DIM
    micro_rows = rows // MICRO
    per_pair = rows // ep_count
    small_rows = small_all.shape[0] // ep_count
    loads = [
        pltpu.make_async_copy(w_out_hbm, w_out, local_sem.at[0]),
        pltpu.make_async_copy(w_in_hbm, w_in, local_sem.at[1]),
    ]
    blocks = [
        pltpu.make_async_copy(
            mixed_hbm.at[pl.ds(index * half, half)],
            mixed_part.at[pl.ds(index * half, half)],
            mixed_sem.at[index],
        )
        for index in range(4 * HALF)
    ]
    for index in (6, 7, 4, 5, 2, 3, 0, 1):
        blocks[index].start()
    operand_loads = [
        pltpu.make_async_copy(source, target, operand_sem.at[index])
        for index, (source, target) in enumerate(zip(operand_hbm, operand_refs))
    ]
    for load in operand_loads + loads:
        load.start()
    greet([(e + j) % ep_count for j in range(1, ep_count)], line_peers(tp_count))

    grad_sum = LineSum(tp_count, partial_ref, grad_line, *grad_sems)
    grad_sum.begin()
    over_chips = FarSum(r, mixed_part, mixed_far, mixed_first, mixed_second, half, *far_sems)
    for kind, block in ((0, 6), (2, 4)):
        for k in range(HALF):
            blocks[block + k].wait()
            over_chips.copy(kind, k).start()
    for index in range(4):
        blocks[index].wait()
    for load in operand_loads:
        load.wait()
    spread = LineGather(tp_count, grad_moe_ref, *[gather_sem.at[i] for i in range(4)])
    grad_moe_ref[:, spread.columns(z)] = grad_sum.total().astype(BF16)
    spread.begin()
    spread.step(1)
    over_chips.pass_first(0)
    spread.step(2)
    over_chips.pass_first(1)
    spread.step(3)
    mixed_sum = LineSum(tp_count, mixed_ref, mixed_line, *mixed_sems)
    out_sum = PlaneSum(r, out_part, *out_bufs, half, out_sems)
    in_sum = PlaneSum(r, in_part, *in_bufs, half, in_sems)

    def gain_row(place, column, wide):
        at = place * small_rows + gain_at
        return small_all[at : at + 1, column : column + wide].astype(F32)

    hidden = hidden_ref[...]
    inverse_two = lax.rsqrt(jnp.mean(hidden * hidden, axis=-1, keepdims=True) + epsilon)
    unit_two = hidden * inverse_two
    grad_moe = grad_moe_ref[...].astype(F32)
    moe_sums = fold(grad_moe * unit_two)
    gain_moe = jnp.concatenate([gain_row(place, rows, rows) for place in range(ep_count)], axis=1)
    scaled = grad_moe * gain_moe
    grad_hidden = grad_ref[...].astype(F32) + inverse_two * (
        scaled - unit_two * jnp.mean(scaled * unit_two, axis=-1, keepdims=True)
    )
    grad_attn[...] = grad_hidden.astype(BF16)
    sums[...] = jnp.zeros_like(sums)
    for place in range(ep_count):
        sums[place * 8 : place * 8 + 8, rows : 2 * rows] = moe_sums[
            :, place * rows : (place + 1) * rows
        ]

    near_of = {"pd": (6, 7), "pb": (2, 3), "pa": (4, 5), "p": (0, 1)}
    slots_of = {
        "pd": SLOT_PD,
        "d": SLOT_D,
        "pb": SLOT_PB,
        "b": SLOT_B,
        "pa": SLOT_PA,
        "a": SLOT_A,
        "p": SLOT_P,
        "e": SLOT_E,
    }

    def weight_blocks(plane, left, right):
        for name, slots in slots_of.items():
            lanes = pl.ds(pl.multiple_of(r[name] * rows, rows), rows)
            block = dot_tn(left[:, lanes], right[...]).astype(BF16)
            for k in range(HALF):
                plane.slot(slots[k])[...] = block[k * half : (k + 1) * half]
                if name in near_of:
                    plane.near_copy(near_of[name][k]).start()

    weight_blocks(out_sum, grad_attn, context_ref)
    loads[0].wait()
    grad_context = dot_nn(grad_attn[...], w_out[...]).astype(BF16)
    for micro in range(MICRO):
        for head in range(heads):
            at = (micro * heads + head) * micro_rows
            stacked_grad[at : at + micro_rows, :] = grad_context[
                micro * micro_rows : (micro + 1) * micro_rows,
                head * HEAD_DIM : (head + 1) * HEAD_DIM,
            ]
    for k in range(HALF):
        out_sum.pass_far(k)
    for k in range(HALF):
        out_sum.pass_second(k)

    cosine, sine_table = cosine_ref[...], -sine_ref[...]
    column = 2 * rows
    gain_query = sum(gain_row(place, column, HEAD_DIM) for place in range(ep_count))
    gain_key = sum(gain_row(place, column + HEAD_DIM, HEAD_DIM) for place in range(ep_count))
    scale = HEAD_DIM ** (-0.5)
    grad_keys = []
    for micro in range(MICRO):
        within = slice(micro * micro_rows, (micro + 1) * micro_rows)
        stacked = slice(micro * heads * micro_rows, (micro + 1) * heads * micro_rows)
        probs = probs_ref[stacked, :]
        grad_probs = dot_nt(stacked_grad[stacked, :], values_ref[within, :])
        delta = jnp.sum(probs * grad_probs, axis=-1, keepdims=True)
        grad_scores = (probs * (grad_probs - delta)).astype(BF16)
        grad_turned[stacked, :] = dot_nn(grad_scores, keys_ref[within, :]) * scale
        grad_keys.append(dot_tn(grad_scores, turned_ref[stacked, :]) * scale)
        grad_proj[within, q_width + HEAD_DIM :] = dot_tn(
            probs.astype(BF16), stacked_grad[stacked, :]
        ).astype(BF16)

    def unturn(grad, values, gain):
        unturned = turn(grad, cosine, sine_table)
        inverse = lax.rsqrt(jnp.mean(values * values, axis=-1, keepdims=True) + epsilon)
        unit = values * inverse
        scaled = unturned * gain
        result = inverse * (scaled - unit * jnp.mean(scaled * unit, axis=-1, keepdims=True))
        return fold(unturned * unit), result.astype(BF16)

    key_sums, grad_key = unturn(
        jnp.concatenate(grad_keys, axis=0), proj_ref[:, q_width : q_width + HEAD_DIM], gain_key
    )
    grad_proj[:, q_width : q_width + HEAD_DIM] = grad_key
    for k in range(HALF):
        out_sum.pass_first(k)
    for k in range(HALF):
        mixed_ref[pl.ds(k * half, half), :] = over_chips.total(k).astype(BF16)
    mixed_sum.begin()

    def one_head(head, total):
        lanes = pl.ds(pl.multiple_of(head * HEAD_DIM, HEAD_DIM), HEAD_DIM)
        grads = [
            grad_turned[
                pl.ds(pl.multiple_of((micro * heads + head) * micro_rows, micro_rows), micro_rows),
                :,
            ]
            for micro in range(MICRO)
        ]
        part, grad = unturn(jnp.concatenate(grads, axis=0), proj_ref[:, lanes], gain_query)
        grad_proj[:, lanes] = grad
        return total + part

    query_sums = lax.fori_loop(0, heads, one_head, jnp.zeros((8, HEAD_DIM), F32))
    for place in range(ep_count):
        at = slice(place * 8, place * 8 + 8)
        sums[at, column : column + HEAD_DIM] = query_sums
        sums[at, column + HEAD_DIM :] = key_sums

    x_rows = x_ref[...].astype(F32)
    inverse_one = lax.rsqrt(jnp.mean(x_rows * x_rows, axis=-1, keepdims=True) + epsilon)
    gain_attn = jnp.concatenate([gain_row(place, 0, rows) for place in range(ep_count)], axis=1)
    loads[1].wait()
    partial = dot_nt(grad_proj[...], w_in[...])
    normed_part[...] = partial.astype(BF16)
    normed_sum = LineSum(tp_count, normed_part, normed_line, *normed_sems)
    normed_sum.begin()
    weight_blocks(in_sum, normed_ref, grad_proj)
    along = jnp.sum(partial * gain_attn * (x_rows * inverse_one), axis=-1, keepdims=True)
    row_sums[...] = jnp.transpose(jnp.broadcast_to(along, (rows, HEAD_DIM)))[:8]
    over_rows = Straight("tp", tp_count, lambda _: row_sums, lambda j: row_line.at[j - 1], *row_sems)
    over_rows.begin()
    for k in range(HALF):
        in_sum.pass_far(k)
    for k in range(HALF):
        in_sum.pass_second(k)
    for k in range(HALF):
        d_out[pl.ds(k * half, half), :] = out_sum.total(k).astype(BF16)
    for k in range(HALF):
        in_sum.pass_first(k)

    lanes = pl.ds(pl.multiple_of(z * share, share), share)
    layer_rows = (hidden_ref[:, lanes] + mixed_sum.total()).astype(BF16)
    over_rows.wait()
    all_rows = row_sums[...]
    for j in range(1, tp_count):
        all_rows = all_rows + row_line[j - 1]
    mean = jnp.transpose(jnp.broadcast_to(all_rows[:1], (HEAD_DIM, rows)))[:, :1] / width
    grad_normed = normed_sum.total()
    unit_share = x_ref[:, lanes].astype(F32) * inverse_one
    places = share // rows
    gain_share = []
    for place in range(places):
        at = pl.multiple_of((z * places + place) * small_rows + gain_at, 16)
        gain_share.append(small_all[pl.ds(at, 16), :rows][:1].astype(F32))
    scaled = grad_normed * jnp.concatenate(gain_share, axis=1)
    grad_rows = grad_attn[:, lanes].astype(F32) + inverse_one * (scaled - unit_share * mean)
    both = jnp.concatenate([layer_rows, grad_rows.astype(BF16)], axis=1)
    home_send[...] = dot_tn(recv_ref[...], both).astype(BF16)
    home = Straight(
        "ep",
        ep_count,
        lambda target: home_send.at[pl.ds(pl.multiple_of(target * per_pair, per_pair), per_pair)],
        lambda j: home_recv.at[pl.ds(pl.multiple_of(e * per_pair, per_pair), per_pair)],
        *home_sems,
    )
    home.begin()
    norm_sums = fold(grad_normed * unit_share)
    for place in range(places):
        at = pl.multiple_of((z * places + place) * 8, 8)
        sums[pl.ds(at, 8), :rows] = norm_sums[:, place * rows : (place + 1) * rows]
    over_plane = Straight(
        "ep",
        ep_count,
        lambda target: sums.at[pl.ds(pl.multiple_of(target * 8, 8), 8)],
        lambda j: sums_near.at[j - 1],
        *sum_sems,
    )
    over_plane.begin()
    mine = pl.ds(pl.multiple_of(e * per_pair, per_pair), per_pair)
    home_recv[mine, :] = home_send[mine, :]
    over_plane.wait()
    plane_sums = sums[pl.ds(pl.multiple_of(e * 8, 8), 8), :]
    for j in range(1, ep_count):
        plane_sums = plane_sums + sums_near[j - 1]
    sums_line[0] = plane_sums
    over_line = Straight(
        "tp", tp_count, lambda _: sums_line.at[0], lambda j: sums_line.at[j], *sum_line_sems
    )
    over_line.begin()
    for j in range(1, ep_count):
        source = (e + ep_count - j) % ep_count
        block = home_recv.at[pl.ds(pl.multiple_of(source * per_pair, per_pair), per_pair)]
        send_to(block, block, home_sems[0].at[j - 1], home_sems[1].at[j - 1], ep=source).wait_recv()
    arrived = dot_tn(send_ref[...], home_recv[...])
    layer_out[...] = arrived[:, :share].astype(BF16)
    layer_grad[...] = arrived[:, share:].astype(BF16)
    over_line.wait()
    line_sums = plane_sums
    for j in range(1, tp_count):
        line_sums = line_sums + sums_line[j]
    sums_out[:, :rows] = line_sums[:, :rows]
    sums_out[:, rows : 2 * rows] = plane_sums[:, rows : 2 * rows]
    sums_out[:, 2 * rows :] = line_sums[:, 2 * rows :]
    for k in range(HALF):
        d_in[pl.ds(k * half, half), :] = in_sum.total(k).astype(BF16)
    for op in (
        grad_sum,
        over_chips,
        spread,
        mixed_sum,
        normed_sum,
        over_rows,
        home,
        over_plane,
        over_line,
        out_sum,
        in_sum,
    ):
        op.sent()


def back_call(gain_at, ep_count, tp_count, partial, mixed, w_in_all, w_out_all, operands):
    rows, width = partial.shape
    share = width // tp_count
    in_width = w_in_all.shape[1]
    q_width = w_out_all.shape[1]
    heads = q_width // HEAD_DIM
    half = rows // HALF
    everything = rows * ep_count
    sums_width = 2 * rows + 2 * HEAD_DIM
    shape = jax.ShapeDtypeStruct

    def pair(count):
        return [pltpu.SemaphoreType.DMA((count,))] * 2

    return pl.pallas_call(
        functools.partial(back_body, gain_at, ep_count, tp_count, rows, heads, len(operands)),
        out_shape=(
            shape((rows, share), BF16),
            shape((rows, share), BF16),
            shape((rows, in_width), BF16),
            shape((rows, q_width), BF16),
            shape((8, sums_width), F32),
        ),
        in_specs=[vmem_spec()] + [any_spec()] * (3 + len(operands)),
        out_specs=tuple([vmem_spec()] * 5),
        scratch_shapes=[pltpu.VMEM(operand.shape, operand.dtype) for operand in operands]
        + [
            pltpu.VMEM((everything, in_width), BF16),
            pltpu.VMEM((everything, q_width), BF16),
            pltpu.VMEM((4 * rows, width), BF16),
            pltpu.VMEM((rows, width), BF16),
            pltpu.VMEM((rows, width), BF16),
            pltpu.VMEM((rows, width), BF16),
            pltpu.VMEM((rows, width), BF16),
            pltpu.VMEM((rows, width), BF16),
            pltpu.VMEM((tp_count - 1, rows, share), BF16),
            pltpu.VMEM((rows, width), BF16),
            pltpu.VMEM((heads * rows, HEAD_DIM), BF16),
            pltpu.VMEM((heads * rows, HEAD_DIM), F32),
            pltpu.VMEM((rows, in_width), BF16),
            pltpu.VMEM((rows, width), BF16),
            pltpu.VMEM((tp_count - 1, rows, share), BF16),
            pltpu.VMEM((tp_count - 1, rows, share), BF16),
            pltpu.VMEM((8, rows), F32),
            pltpu.VMEM((tp_count - 1, 8, rows), F32),
            pltpu.VMEM((8 * ep_count, sums_width), F32),
            pltpu.VMEM((ep_count - 1, 8, sums_width), F32),
            pltpu.VMEM((tp_count, 8, sums_width), F32),
            pltpu.VMEM((rows, 2 * share), BF16),
            pltpu.VMEM((rows, 2 * share), BF16),
            pltpu.VMEM((everything, q_width), BF16),
            pltpu.VMEM((everything, in_width), BF16),
        ]
        + plane_sum_scratch(half, q_width)
        + plane_sum_scratch(half, in_width)
        + pair(tp_count - 1) * 3
        + pair(ep_count - 1)
        + pair(tp_count - 1)
        + pair(ep_count - 1)
        + [pltpu.SemaphoreType.DMA((3, HALF))] * 2
        + pair(tp_count - 1)
        + [
            pltpu.SemaphoreType.DMA((4, tp_count - 1)),
            pltpu.SemaphoreType.DMA((len(operands),)),
            pltpu.SemaphoreType.DMA((4 * HALF,)),
            pltpu.SemaphoreType.DMA((2,)),
        ],
        compiler_params=comm_params(4),
        name="back",
    )(partial, mixed, w_in_all, w_out_all, *operands)


def plain_layer(
    layer_in,
    token_order,
    seq_lengths,
    routes,
    route_weights,
    w_query,
    w_key,
    w_value,
    w_out,
    norm_attn,
    norm_moe,
    query_gain,
    key_gain,
    w_gate,
    w_up,
    w_down,
    grad_out,
):
    ep_count = lax.axis_size("ep")
    tp_count = lax.axis_size("tp")
    tp_index = lax.axis_index("tp")
    ep_index = lax.axis_index("ep")
    local_experts, hidden_here, model_width = w_gate.shape
    experts = local_experts * ep_count
    rows_dev = layer_in.shape[0]
    micro_rows = rows_dev // MICRO
    share_width = layer_in.shape[1]
    score_scale = HEAD_DIM ** (-0.5)

    send, recv = deal_matrices(token_order, ep_index, rows_dev, ep_count)
    both = jnp.concatenate([layer_in, grad_out], axis=1)
    got = permute_rows(recv, exchange(permute_rows(send, both), ep_count))
    layer_full = lax.all_gather(got[:, :share_width], "tp", axis=1, tiled=True)
    grad_full = lax.all_gather(got[:, share_width:], "tp", axis=1, tiled=True)

    q_width, kv_width = w_query.shape[1], w_key.shape[1]
    packed = jnp.concatenate([w_query, w_out, w_key, w_value], axis=1)
    packed = lax.all_gather(packed, "ep", axis=0, tiled=True)
    full_query = packed[:, :q_width]
    full_out = packed[:, q_width : 2 * q_width]
    full_kv = packed[:, 2 * q_width :]
    gains = jnp.concatenate([norm_attn, norm_moe, query_gain, key_gain]).reshape(1, -1)
    gains = lax.all_gather(gains, "ep", axis=0, tiled=True).astype(F32)
    part = norm_attn.shape[0]
    head_part = query_gain.shape[0]
    gain_attn = gains[:, :part].reshape(-1)
    gain_moe = gains[:, part : 2 * part].reshape(-1)
    gain_query = gains[:, 2 * part : 2 * part + head_part].reshape(-1)
    gain_key = gains[:, 2 * part + head_part :].reshape(-1)

    expert_ids = jnp.arange(experts, dtype=jnp.int32)
    dense = jnp.sum(
        jnp.where(routes[:, :, None] == expert_ids[None, None, :], route_weights[:, :, None], 0.0),
        axis=1,
    )
    scale_all = lax.all_gather(dense, "ep", axis=0, tiled=True)
    scale = lax.dynamic_slice_in_dim(scale_all, ep_index * local_experts, local_experts, 1)
    all_grad = lax.all_gather(grad_full, "ep", axis=0, tiled=True)

    heads_here = q_width // HEAD_DIM
    kv_here = kv_width // HEAD_DIM
    group_size = heads_here // kv_here
    segment, position = jax.vmap(positions_of, in_axes=(0, None))(seq_lengths, micro_rows)
    cosine, sine_table = rope_tables(position.reshape(-1), HEAD_DIM // 2)
    layer_float = layer_full.astype(F32)
    inverse_one = inverse_rms(layer_float)
    unit_one = layer_float * inverse_one
    normed = (unit_one * gain_attn).astype(BF16)
    query_proj = dot_nn(normed, full_query).reshape(rows_dev, heads_here, HEAD_DIM)
    kv_proj = dot_nn(normed, full_kv)
    key_proj = kv_proj[:, :kv_width].reshape(rows_dev, kv_here, HEAD_DIM)
    value_proj = kv_proj[:, kv_width:].reshape(rows_dev, kv_here, HEAD_DIM)
    inverse_query = inverse_rms(query_proj)
    unit_query = query_proj * inverse_query
    inverse_key = inverse_rms(key_proj)
    unit_key = key_proj * inverse_key
    queries = (
        rotate(unit_query * gain_query, cosine, sine_table)
        .astype(BF16)
        .reshape(MICRO, micro_rows, kv_here, group_size, HEAD_DIM)
    )
    key_rows = (
        rotate(unit_key * gain_key, cosine, sine_table)
        .astype(BF16)
        .reshape(MICRO, micro_rows, kv_here, HEAD_DIM)
    )
    values = value_proj.astype(BF16).reshape(MICRO, micro_rows, kv_here, HEAD_DIM)
    scores = (
        jnp.einsum("mqkgd,mtkd->mkgqt", queries, key_rows, preferred_element_type=F32)
        * score_scale
    )
    offsets = jnp.arange(micro_rows, dtype=jnp.int32)
    allowed = (segment[:, :, None] == segment[:, None, :]) & (
        offsets[None, None, :] <= offsets[None, :, None]
    )
    scores = jnp.where(allowed[:, None, None], scores, -1e30)
    row_peak = jnp.max(scores, axis=-1, keepdims=True)
    exponent = jnp.exp(scores - row_peak)
    attn_probs = exponent / jnp.sum(exponent, axis=-1, keepdims=True)
    probs_low = attn_probs.astype(BF16)
    context = jnp.einsum("mkgqt,mtkd->mqkgd", probs_low, values, preferred_element_type=F32)
    context_low = context.reshape(rows_dev, heads_here * HEAD_DIM).astype(BF16)
    attn_part = dot_nt(context_low, full_out)
    attn_out = lax.psum(attn_part.astype(BF16), "tp").astype(F32)
    hidden = layer_float + attn_out
    inverse_two = inverse_rms(hidden)
    unit_two = hidden * inverse_two
    moe_in = (unit_two * gain_moe).astype(BF16)

    all_in = lax.all_gather(moe_in, "ep", axis=0, tiled=True)
    flat = local_experts * hidden_here
    gate_matrix = w_gate.reshape(flat, model_width)
    up_matrix = w_up.reshape(flat, model_width)
    down_matrix = w_down.reshape(flat, model_width)
    row_scale = jnp.repeat(scale, hidden_here, axis=1)
    gate_pre = dot_nt(all_in, gate_matrix)
    up_pre = dot_nt(all_in, up_matrix)
    grad_active = dot_nt(all_grad, down_matrix) * row_scale
    sigmoid_gate = jax.nn.sigmoid(gate_pre)
    silu_gate = gate_pre * sigmoid_gate
    active = (silu_gate * up_pre * row_scale).astype(BF16)
    grad_up_pre = (grad_active * silu_gate).astype(BF16)
    grad_gate_pre = (
        grad_active * up_pre * sigmoid_gate * (1.0 + gate_pre * (1.0 - sigmoid_gate))
    ).astype(BF16)
    grad_partial = dot_nn(grad_gate_pre, gate_matrix) + dot_nn(grad_up_pre, up_matrix)
    grad_partial = lax.psum_scatter(
        grad_partial.astype(BF16), "ep", scatter_dimension=0, tiled=True
    )
    grad_share = lax.psum_scatter(grad_partial, "tp", scatter_dimension=1, tiled=True)
    out_partial = dot_nn(active, down_matrix)
    out_partial = lax.psum_scatter(out_partial.astype(BF16), "ep", scatter_dimension=0, tiled=True)
    mixed = lax.psum_scatter(out_partial, "tp", scatter_dimension=1, tiled=True)
    hidden_share = lax.dynamic_slice_in_dim(hidden, tp_index * share_width, share_width, 1)
    layer_dealt = (hidden_share + mixed.astype(F32)).astype(BF16)
    grad_w_down = dot_tn(active, all_grad).reshape(w_down.shape)
    grad_w_gate = dot_tn(grad_gate_pre, all_in).reshape(w_gate.shape)
    grad_w_up = dot_tn(grad_up_pre, all_in).reshape(w_up.shape)

    grad_float = grad_full.astype(F32)
    grad_moe_in = lax.all_gather(grad_share, "tp", axis=1, tiled=True).astype(F32)
    norm_moe_part = jnp.sum(grad_moe_in * unit_two, axis=0)
    grad_hidden = grad_float + norm_back(grad_moe_in * gain_moe, unit_two, inverse_two)
    grad_attn = grad_hidden.astype(BF16)
    grad_w_out = dot_tn(grad_attn, context_low)
    grad_context = (
        dot_nn(grad_attn, full_out)
        .astype(BF16)
        .reshape(MICRO, micro_rows, kv_here, group_size, HEAD_DIM)
    )
    grad_probs = jnp.einsum("mqkgd,mtkd->mkgqt", grad_context, values, preferred_element_type=F32)
    prob_delta = jnp.sum(attn_probs * grad_probs, axis=-1, keepdims=True)
    grad_scores = (attn_probs * (grad_probs - prob_delta)).astype(BF16)
    grad_queries = (
        jnp.einsum("mkgqt,mtkd->mqkgd", grad_scores, key_rows, preferred_element_type=F32).reshape(
            rows_dev, heads_here, HEAD_DIM
        )
        * score_scale
    )
    grad_keys = (
        jnp.einsum("mkgqt,mqkgd->mtkd", grad_scores, queries, preferred_element_type=F32).reshape(
            rows_dev, kv_here, HEAD_DIM
        )
        * score_scale
    )
    grad_values = jnp.einsum(
        "mkgqt,mqkgd->mtkd", probs_low, grad_context, preferred_element_type=F32
    )
    grad_unit_query = rotate_back(grad_queries, cosine, sine_table)
    grad_unit_key = rotate_back(grad_keys, cosine, sine_table)
    query_gain_part = jnp.sum(grad_unit_query * unit_query, axis=(0, 1))
    key_gain_part = jnp.sum(grad_unit_key * unit_key, axis=(0, 1))
    grad_query_proj = (
        norm_back(grad_unit_query * gain_query, unit_query, inverse_query)
        .reshape(rows_dev, heads_here * HEAD_DIM)
        .astype(BF16)
    )
    grad_key_proj = (
        norm_back(grad_unit_key * gain_key, unit_key, inverse_key)
        .reshape(rows_dev, kv_width)
        .astype(BF16)
    )
    grad_value_proj = grad_values.reshape(rows_dev, kv_width).astype(BF16)
    grad_kv_proj = jnp.concatenate([grad_key_proj, grad_value_proj], axis=1)
    normed_part = dot_nt(grad_query_proj, full_query) + dot_nt(grad_kv_proj, full_kv)
    grad_normed = lax.psum_scatter(
        normed_part.astype(BF16), "tp", scatter_dimension=1, tiled=True
    ).astype(F32)
    grad_packed = jnp.concatenate(
        [
            dot_tn(normed, grad_query_proj).astype(BF16),
            grad_w_out.astype(BF16),
            dot_tn(normed, grad_kv_proj).astype(BF16),
        ],
        axis=1,
    )
    grad_packed = lax.psum_scatter(grad_packed, "ep", scatter_dimension=0, tiled=True).astype(F32)

    start = tp_index * share_width
    gain_share = lax.dynamic_slice_in_dim(gain_attn, start, share_width, 0)
    unit_share = lax.dynamic_slice_in_dim(unit_one, start, share_width, 1)
    hidden_grad_share = lax.dynamic_slice_in_dim(grad_hidden, start, share_width, 1)
    scaled = grad_normed * gain_share
    row_mean = lax.psum(jnp.sum(scaled * unit_share, axis=1), "tp") / model_width
    grad_layer = hidden_grad_share + inverse_one * (scaled - unit_share * row_mean[:, None])
    norm_attn_part = lax.dynamic_update_slice_in_dim(
        jnp.zeros((model_width,), F32), jnp.sum(grad_normed * unit_share, axis=0), start, 0
    )
    small = jnp.concatenate(
        [norm_attn_part, norm_moe_part / tp_count, query_gain_part, key_gain_part]
    )
    small = lax.psum(small, ("ep", "tp"))
    grad_norm_attn = lax.dynamic_slice_in_dim(small, ep_index * part, part, 0)
    grad_norm_moe = lax.dynamic_slice_in_dim(small, model_width + ep_index * part, part, 0)
    grad_query_gain = lax.dynamic_slice_in_dim(
        small, 2 * model_width + ep_index * head_part, head_part, 0
    )
    grad_key_gain = lax.dynamic_slice_in_dim(
        small, 2 * model_width + HEAD_DIM + ep_index * head_part, head_part, 0
    )

    back = jnp.concatenate([layer_dealt, grad_layer.astype(BF16)], axis=1)
    home = exchange(dot_tn(recv, back).astype(BF16), ep_count)
    home = dot_tn(send, home)
    return (
        home[:, :share_width].astype(BF16),
        home[:, share_width:],
        grad_packed[:, :q_width],
        grad_packed[:, 2 * q_width : 2 * q_width + kv_width],
        grad_packed[:, 2 * q_width + kv_width :],
        grad_packed[:, q_width : 2 * q_width],
        grad_norm_attn,
        grad_norm_moe,
        grad_query_gain,
        grad_key_gain,
        grad_w_gate,
        grad_w_up,
        grad_w_down,
    )


def route_scales(routes, route_weights, experts, local_experts, hidden_here, ep_index):
    expert_ids = jnp.arange(experts, dtype=jnp.int32)
    dense = jnp.sum(
        jnp.where(
            routes.T[None, :, :] == expert_ids[:, None, None], route_weights.T[None, :, :], 0.0
        ),
        axis=1,
    )
    terms = []
    for _ in range(SCALE_TERMS):
        terms.append(lax.reduce_precision(dense, 8, 7))
        dense = dense - terms[-1]
    parts = jnp.concatenate(terms, axis=0).astype(BF16)
    flat_expert = ep_index * local_experts + jnp.repeat(
        jnp.arange(local_experts, dtype=jnp.int32), hidden_here
    )
    part_expert = jnp.arange(parts.shape[0], dtype=jnp.int32) % experts
    return (parts, (part_expert[:, None] == flat_expert[None, :]).astype(BF16))


def plane_layer(
    layer_in,
    token_order,
    seq_lengths,
    routes,
    route_weights,
    w_query,
    w_key,
    w_value,
    w_out,
    norm_attn,
    norm_moe,
    query_gain,
    key_gain,
    w_gate,
    w_up,
    w_down,
    grad_out,
):
    ep_count = lax.axis_size("ep")
    tp_count = lax.axis_size("tp")
    tp_index = lax.axis_index("tp")
    ep_index = lax.axis_index("ep")
    local_experts, hidden_here, model_width = w_gate.shape
    experts = local_experts * ep_count
    rows_dev = layer_in.shape[0]
    micro_rows = rows_dev // MICRO
    share_width = layer_in.shape[1]
    score_scale = HEAD_DIM ** (-0.5)

    q_width, kv_width = w_query.shape[1], w_key.shape[1]
    heads_here = q_width // HEAD_DIM
    kv_here = kv_width // HEAD_DIM
    group_size = heads_here // kv_here
    send, recv = deal_matrices(token_order, ep_index, rows_dev, ep_count)
    send_rows = permute_rows(send, jnp.concatenate([layer_in, grad_out], axis=1))
    part = norm_attn.shape[0]
    head_part = query_gain.shape[0]
    scale_parts, pick = route_scales(
        routes, route_weights, experts, local_experts, hidden_here, ep_index
    )
    gain_at = scale_parts.shape[0]
    gains = jnp.zeros((1, 2 * part + 2 * HEAD_DIM), BF16)
    for vector, at in (
        (norm_attn, 0),
        (norm_moe, part),
        (query_gain, 2 * part + ep_index * head_part),
        (key_gain, 2 * part + HEAD_DIM + ep_index * head_part),
    ):
        gains = lax.dynamic_update_slice(gains, vector[None], (0, at))
    small_rows = -(-(gain_at + 1) // 32) * 32
    small = jnp.pad(scale_parts, ((0, 0), (0, gains.shape[1] - scale_parts.shape[1])))
    small = jnp.pad(
        jnp.concatenate([small, gains], axis=0), ((0, small_rows - gain_at - 1), (0, 0))
    )
    segment, position = jax.vmap(positions_of, in_axes=(0, None))(seq_lengths, micro_rows)
    cosine, sine_table = rope_tables(position.reshape(-1), HEAD_DIM // 2)
    cosine_wide = jnp.concatenate([cosine[:, 0], cosine[:, 0]], axis=1)
    sine_wide = jnp.concatenate([-sine_table[:, 0], sine_table[:, 0]], axis=1)
    offsets = jnp.arange(micro_rows, dtype=jnp.int32)
    allowed = (segment[:, :, None] == segment[:, None, :]) & (
        offsets[None, None, :] <= offsets[None, :, None]
    )
    mask = allowed.astype(F32).reshape(rows_dev, micro_rows)
    (
        layer_full,
        grad_full,
        hidden,
        moe_in,
        proj,
        turned,
        key_flat,
        value_flat,
        probs,
        context_low,
        small_all,
        normed,
        all_grad,
        w_in_all,
        full_out,
    ) = front_call(
        gain_at,
        ep_count,
        tp_count,
        send_rows,
        recv,
        small,
        cosine_wide,
        sine_wide,
        mask,
        w_query,
        w_key,
        w_value,
        w_out,
    )

    flat = local_experts * hidden_here
    gate_matrix = w_gate.reshape(flat, model_width)
    up_matrix = w_up.reshape(flat, model_width)
    down_matrix = w_down.reshape(flat, model_width)
    grad_partial, mixed_part, grad_w_gate, grad_w_up, grad_w_down = expert_call(
        moe_in, all_grad, small_all, pick, gate_matrix, up_matrix, down_matrix
    )
    layer_out, layer_grad, d_in, d_out, sums = back_call(
        gain_at,
        ep_count,
        tp_count,
        grad_partial,
        mixed_part,
        w_in_all,
        full_out,
        (
            layer_full,
            hidden,
            grad_full,
            normed,
            proj,
            turned,
            key_flat,
            value_flat,
            probs,
            context_low,
            small_all,
            cosine_wide,
            sine_wide,
            send,
            recv,
        ),
    )
    sums = jnp.sum(sums, axis=0)
    head_at = 2 * part + ep_index * head_part
    return (
        layer_out,
        layer_grad.astype(F32),
        d_in[:, :q_width].astype(F32),
        d_in[:, q_width : q_width + kv_width].astype(F32),
        d_in[:, q_width + kv_width :].astype(F32),
        d_out.astype(F32),
        sums[:part],
        sums[part : 2 * part],
        lax.dynamic_slice_in_dim(sums, head_at, head_part, 0),
        lax.dynamic_slice_in_dim(sums, head_at + HEAD_DIM, head_part, 0),
        grad_w_gate.astype(F32).reshape(w_gate.shape),
        grad_w_up.astype(F32).reshape(w_up.shape),
        grad_w_down.astype(F32).reshape(w_down.shape),
    )


def solution(mesh):
    shape = dict(mesh.shape)
    planes = shape["ep"] == 8 and shape["tp"] == 4
    return jax.shard_map(
        plane_layer if planes else plain_layer,
        mesh=mesh,
        in_specs=(
            P("ep", "tp"),
            P(),
            P("ep", None),
            P("ep", None),
            P("ep", None),
            P("ep", "tp"),
            P("ep", "tp"),
            P("ep", "tp"),
            P("ep", "tp"),
            P("ep"),
            P("ep"),
            P("ep"),
            P("ep"),
            P("ep", "tp", None),
            P("ep", "tp", None),
            P("ep", "tp", None),
            P("ep", "tp"),
        ),
        out_specs=(
            P("ep", "tp"),
            P("ep", "tp"),
            P("ep", "tp"),
            P("ep", "tp"),
            P("ep", "tp"),
            P("ep", "tp"),
            P("ep"),
            P("ep"),
            P("ep"),
            P("ep"),
            P("ep", "tp", None),
            P("ep", "tp", None),
            P("ep", "tp", None),
        ),
        check_vma=False,
    )
```

```python
import functools

import jax
import jax.numpy as jnp
from jax import lax
from jax.experimental import pallas as pl
from jax.experimental.pallas import tpu as pltpu
from jax.sharding import PartitionSpec as P

HEAD_DIM = 128
MICRO = 2
F32 = jnp.float32
BF16 = jnp.bfloat16
SCALE_TERMS = 3
VMEM_LIMIT = 67 * 1000 * 1000

epsilon = 1e-06
rope_base = 1000000.0


def positions_of(lengths, row_count):
    offsets = jnp.arange(row_count, dtype=jnp.int32)
    seq_ends = jnp.cumsum(lengths)
    segment = jnp.sum((offsets[:, None] >= seq_ends[None, :]).astype(jnp.int32), axis=1)
    starts = seq_ends - lengths
    in_segment = segment[:, None] == jnp.arange(lengths.shape[0], dtype=jnp.int32)[None, :]
    position = offsets - jnp.sum(jnp.where(in_segment, starts[None, :], 0), axis=1)
    return (segment, position)


def rope_tables(position, half_dim):
    frequency = rope_base ** (-jnp.arange(half_dim, dtype=F32) / half_dim)
    angles = position.astype(F32)[:, None] * frequency[None, :]
    return (jnp.cos(angles)[:, None, :], jnp.sin(angles)[:, None, :])


def rotate(values, cosine, sine_table):
    half_dim = values.shape[-1] // 2
    first_half = values[..., :half_dim]
    second_half = values[..., half_dim:]
    return jnp.concatenate(
        [
            first_half * cosine - second_half * sine_table,
            second_half * cosine + first_half * sine_table,
        ],
        axis=-1,
    )


def rotate_back(incoming, cosine, sine_table):
    return rotate(incoming, cosine, -sine_table)


def deal_matrices(token_order, ep_index, rows_dev, ep_count):
    per_pair = rows_dev // ep_count
    rows = jnp.arange(rows_dev, dtype=jnp.int32)
    home = ep_index * rows_dev + rows
    at = jnp.arange(token_order.shape[0], dtype=jnp.int32)
    place = jnp.sum(jnp.where(token_order[None, :] == home[:, None], at[None, :], 0), axis=1)
    dest = place // rows_dev
    rank = jnp.sum(
        ((dest[:, None] == dest[None, :]) & (place[None, :] < place[:, None])).astype(jnp.int32),
        axis=1,
    )
    send_slot = dest * per_pair + rank
    send = (send_slot[None, :] == rows[:, None]).astype(BF16)
    mine = lax.dynamic_slice_in_dim(token_order, ep_index * rows_dev, rows_dev, 0)
    source = mine // rows_dev
    my_rank = jnp.sum(
        ((source[:, None] == source[None, :]) & (rows[None, :] < rows[:, None])).astype(jnp.int32),
        axis=1,
    )
    recv_slot = source * per_pair + my_rank
    recv = (recv_slot[:, None] == rows[None, :]).astype(BF16)
    return (send, recv)


def inverse_rms(values):
    return lax.rsqrt(jnp.mean(values * values, axis=-1, keepdims=True) + epsilon)


def norm_back(grad_unit, unit_values, inverse):
    return inverse * (
        grad_unit - unit_values * jnp.mean(grad_unit * unit_values, axis=-1, keepdims=True)
    )


def dot_nn(left, right):
    return jnp.dot(left, right, preferred_element_type=F32)


def dot_tn(left_rows, right_rows):
    return lax.dot_general(
        left_rows, right_rows, (((0,), (0,)), ((), ())), preferred_element_type=F32
    )


def dot_nt(left_rows, right_matrix):
    return lax.dot_general(
        left_rows, right_matrix, (((1,), (1,)), ((), ())), preferred_element_type=F32
    )


def permute_rows(matrix, rows):
    return dot_nn(matrix, rows).astype(BF16)


def exchange(rows, ep_count):
    split = rows.reshape(ep_count, rows.shape[0] // ep_count, rows.shape[1])
    moved = lax.all_to_all(split, "ep", split_axis=0, concat_axis=0, tiled=True)
    return moved.reshape(rows.shape)


MESH_ID = pl.DeviceIdType.MESH
HALF = 2
LINE_CHUNKS = 16
E0, E1, P0, P1, A0, B0, PA0, PB0, A1, B1, PA1, PB1, D0, PD0, D1, PD1 = range(16)
SLOT_E, SLOT_P, SLOT_A, SLOT_B = (E0, E1), (P0, P1), (A0, A1), (B0, B1)
SLOT_D, SLOT_PA, SLOT_PB, SLOT_PD = (D0, D1), (PA0, PA1), (PB0, PB1), (PD0, PD1)
FOR_PARTNER = (P0, P1, PB0, PB1, PA0, PA1, PD0, PD1)


def roles():
    e = lax.axis_index("ep")
    core, x, y = e % 2, (e // 2) % 2, e // 4
    other = 1 - 2 * core
    over_x, over_y = e + 2 - 4 * x, e + 4 - 8 * y
    a = over_x * (1 - core) + over_y * core
    b = over_y * (1 - core) + over_x * core
    d = over_x + over_y - e
    return dict(e=e, p=e + other, a=a, b=b, d=d, pa=a + other, pb=b + other, pd=d + other)


def slot_owner(r):
    names = ("e", "e", "p", "p", "a", "b", "pa", "pb", "a", "b", "pa", "pb", "d", "pd", "d", "pd")
    halves = (0, 1, 0, 1, 0, 0, 0, 0, 1, 1, 1, 1, 0, 0, 1, 1)
    return [(r[name], half) for name, half in zip(names, halves)]


def greet(plane, line):
    barrier = pltpu.get_barrier_semaphore()
    for device in plane:
        pl.semaphore_signal(barrier, inc=1, device_id={"ep": device}, device_id_type=MESH_ID)
    for device in line:
        pl.semaphore_signal(barrier, inc=1, device_id={"tp": device}, device_id_type=MESH_ID)
    pl.semaphore_wait(barrier, len(plane) + len(line))


def send_to(src, dst, send_sem, recv_sem, **device):
    return pltpu.make_async_remote_copy(
        src_ref=src,
        dst_ref=dst,
        send_sem=send_sem,
        recv_sem=recv_sem,
        device_id=device,
        device_id_type=MESH_ID,
    )


class PlaneGather:
    kinds = 7

    def __init__(self, r, held, half, send, recv):
        self.r, self.held, self.half, self.send, self.recv = r, held, half, send, recv

    def slot(self, index):
        return self.held.at[pl.ds(index * self.half, self.half)]

    def copy(self, kind, k):
        source, target, device = (
            (SLOT_E, SLOT_A, "a"),
            (SLOT_E, SLOT_B, "b"),
            (SLOT_E, SLOT_P, "p"),
            (SLOT_A, SLOT_D, "b"),
            (SLOT_A, SLOT_PB, "p"),
            (SLOT_B, SLOT_PA, "p"),
            (SLOT_D, SLOT_PD, "p"),
        )[kind]
        return send_to(
            self.slot(source[k]),
            self.slot(target[k]),
            self.send.at[kind, k],
            self.recv.at[kind, k],
            ep=self.r[device],
        )

    def begin(self):
        for k in range(HALF):
            for kind in range(3):
                self.copy(kind, k).start()

    def arrived(self, kind, k):
        self.copy(kind, k).wait_recv()

    def pass_near(self, k):
        self.arrived(0, k)
        self.copy(3, k).start()
        self.copy(4, k).start()
        self.arrived(1, k)
        self.copy(5, k).start()

    def pass_far(self, k):
        self.arrived(3, k)
        self.copy(6, k).start()

    def sent(self):
        for k in range(HALF):
            for kind in range(self.kinds):
                self.copy(kind, k).wait_send()


class PlaneSum:
    def __init__(self, r, part, near, far, first, second, half, sems):
        self.r, self.part, self.half = r, part, half
        self.near, self.far, self.first, self.second = near, far, first, second
        self.near_send, self.near_recv, self.send, self.recv = sems

    def slot(self, index):
        return self.part.at[pl.ds(index * self.half, self.half)]

    def rows(self, buffer, index):
        return buffer.at[pl.ds(index * self.half, self.half)]

    def near_copy(self, index):
        return send_to(
            self.slot(FOR_PARTNER[index]),
            self.rows(self.near, index),
            self.near_send.at[index],
            self.near_recv.at[index],
            ep=self.r["p"],
        )

    def far_copy(self, kind, k):
        source, target, device = (
            (SLOT_D, self.far, "b"),
            (SLOT_A, self.first, "a"),
            (SLOT_B, self.second, "b"),
        )[kind]
        return send_to(
            self.slot(source[k]),
            self.rows(target, k),
            self.send.at[kind, k],
            self.recv.at[kind, k],
            ep=self.r[device],
        )

    def add_up(self, slot, others):
        total = self.slot(slot)[...].astype(F32)
        for other in others:
            total = total + other[...].astype(F32)
        return total

    def near_sum(self, name, k):
        index = 2 * name + k
        slot = (SLOT_E, SLOT_A, SLOT_B, SLOT_D)[name][k]
        self.near_copy(index).wait_recv()
        return slot, [self.rows(self.near, index)]

    def pass_far(self, k):
        slot, others = self.near_sum(3, k)
        self.slot(slot)[...] = self.add_up(slot, others).astype(BF16)
        self.far_copy(0, k).start()

    def pass_second(self, k):
        slot, others = self.near_sum(2, k)
        self.slot(slot)[...] = self.add_up(slot, others).astype(BF16)
        self.far_copy(2, k).start()

    def pass_first(self, k):
        slot, others = self.near_sum(1, k)
        self.far_copy(0, k).wait_recv()
        self.slot(slot)[...] = self.add_up(slot, others + [self.rows(self.far, k)]).astype(BF16)
        self.far_copy(1, k).start()

    def total(self, k):
        slot, others = self.near_sum(0, k)
        self.far_copy(1, k).wait_recv()
        self.far_copy(2, k).wait_recv()
        return self.add_up(slot, others + [self.rows(self.first, k), self.rows(self.second, k)])

    def sent(self):
        for index in range(4 * HALF):
            self.near_copy(index).wait_send()
        for kind in range(3):
            for k in range(HALF):
                self.far_copy(kind, k).wait_send()


def plane_sum_scratch(half, width, kinds=3):
    return [
        pltpu.VMEM((8 * half, width), BF16),
        pltpu.VMEM((2 * half, width), BF16),
        pltpu.VMEM((2 * half, width), BF16),
        pltpu.VMEM((2 * half, width), BF16),
        pltpu.SemaphoreType.DMA((4 * HALF,)),
        pltpu.SemaphoreType.DMA((4 * HALF,)),
        pltpu.SemaphoreType.DMA((kinds, HALF)),
        pltpu.SemaphoreType.DMA((kinds, HALF)),
    ]


def any_spec():
    return pl.BlockSpec(memory_space=pl.ANY)


def vmem_spec():
    return pl.BlockSpec(memory_space=pltpu.VMEM)


def comm_params(collective_id):
    return pltpu.CompilerParams(
        collective_id=collective_id, has_side_effects=True, vmem_limit_bytes=VMEM_LIMIT
    )


def expert_body(
    flat,
    rows,
    parts,
    own_hbm,
    grad_hbm,
    scale_hbm,
    pick_ref,
    gate_hbm,
    up_hbm,
    down_hbm,
    total_ref,
    mixed_hbm,
    d_gate_hbm,
    d_up_hbm,
    d_down_hbm,
    held,
    grads,
    scales,
    both,
    down,
    grad_act,
    grad_both,
    active,
    d_weights,
    part,
    near,
    far,
    first,
    second,
    near_send,
    near_recv,
    sum_send,
    sum_recv,
    gather_send,
    gather_recv,
    mixed_near,
    mixed_send,
    mixed_recv,
    local_sem,
    grad_sem,
    out_sem,
    mixed_sem,
):
    r = roles()
    half = rows // HALF
    unit = 2 * half
    owners = slot_owner(r)
    loads = [
        pltpu.make_async_copy(own_hbm, held.at[pl.ds(0, rows)], local_sem.at[0]),
        pltpu.make_async_copy(gate_hbm, both.at[pl.ds(0, flat)], local_sem.at[1]),
        pltpu.make_async_copy(up_hbm, both.at[pl.ds(flat, flat)], local_sem.at[2]),
        pltpu.make_async_copy(down_hbm, down, local_sem.at[3]),
    ]
    for load in loads:
        load.start()
    stride = scale_hbm.shape[0] // 8
    slots = []
    for index, (owner, k) in enumerate(owners):
        slots.append(
            (
                pltpu.make_async_copy(
                    scale_hbm.at[pl.ds(owner * stride, parts), pl.ds(k * half, half)],
                    scales.at[index],
                    grad_sem.at[0, index],
                ),
                pltpu.make_async_copy(
                    grad_hbm.at[pl.ds(owner * rows + k * half, half)],
                    grads.at[pl.ds(index * half, half)],
                    grad_sem.at[1, index],
                ),
            )
        )
        for load in slots[-1]:
            load.start()
    greet([r["p"], r["a"], r["b"]], [])
    gather = PlaneGather(r, held, half, gather_send, gather_recv)
    loads[0].wait()
    gather.begin()
    for load in loads[1:]:
        load.wait()
    for pair in slots:
        for load in pair:
            load.wait()
    psum = PlaneSum(
        r, part, near, far, first, second, half, (near_send, near_recv, sum_send, sum_recv)
    )

    def expand(index):
        return jnp.concatenate(
            [dot_tn(scales[2 * index], pick_ref[...]), dot_tn(scales[2 * index + 1], pick_ref[...])],
            axis=0,
        )

    @pl.loop(0, 8)
    def _(index):
        at = pl.ds(pl.multiple_of(index * unit, unit), unit)
        grad_act[at, :] = dot_nt(grads[at, :], down[...]) * expand(index)

    @pl.loop(0, 8)
    def _(index):
        @pl.when(index == 1)
        def _():
            gather.arrived(2, 0)
            gather.arrived(2, 1)

        for k, first_unit in ((0, 2), (1, 4)):

            @pl.when(index == first_unit)
            def _():
                gather.pass_near(k)

            @pl.when(index == first_unit + 1)
            def _():
                gather.arrived(4, k)
                gather.arrived(5, k)

            @pl.when(index == 6 + k)
            def _():
                gather.pass_far(k)
                gather.arrived(6, k)

        at = pl.ds(pl.multiple_of(index * unit, unit), unit)
        pre = dot_nt(held[at, :], both[...])
        gate_pre, up_pre = pre[:, :flat], pre[:, flat:]
        grad_active = grad_act[at, :]
        sigmoid_gate = jax.nn.sigmoid(gate_pre)
        silu_gate = gate_pre * sigmoid_gate
        active[at, :] = (silu_gate * up_pre * expand(index)).astype(BF16)
        grad_both[at, flat:] = (grad_active * silu_gate).astype(BF16)
        grad_both[at, :flat] = (
            grad_active * up_pre * sigmoid_gate * (1.0 + gate_pre * (1.0 - sigmoid_gate))
        ).astype(BF16)
        part[at, :] = dot_nn(grad_both[at, :], both[...]).astype(BF16)

        @pl.when(index == 1)
        def _():
            psum.near_copy(0).start()
            psum.near_copy(1).start()

        for k, last_unit in ((0, 3), (1, 5)):

            @pl.when(index == last_unit)
            def _():
                psum.near_copy(2 + k).start()
                psum.near_copy(4 + k).start()

            @pl.when(index == last_unit + 1)
            def _():
                psum.pass_second(k)

            @pl.when(index == 6 + k)
            def _():
                psum.near_copy(6 + k).start()

    psum.pass_far(0)
    psum.pass_far(1)
    group = 128
    pieces = flat // group

    def weight_out(which):
        target = (d_down_hbm, d_gate_hbm, d_up_hbm)[which]
        return pltpu.make_async_copy(
            d_weights.at[pl.ds(which * flat, flat)], target, out_sem.at[which]
        )

    @pl.loop(0, pieces)
    def _(index):
        place = pl.ds(pl.multiple_of(index * group, group), group)
        d_weights[place, :] = dot_tn(active[:, place], grads[...]).astype(BF16)

    weight_out(0).start()

    mixed = PlaneSum(
        r, grads, mixed_near, None, None, None, half, (mixed_send, mixed_recv, None, None)
    )

    @pl.loop(0, 8)
    def _(step):
        index = (step + 6) % 8
        at = pl.ds(pl.multiple_of(index * unit, unit), unit)
        grads[at, :] = dot_nn(active[at, :], down[...]).astype(BF16)
        for unit_done, copies in ((6, (6,)), (7, (7,)), (1, (0, 1)), (3, (2, 4)), (5, (3, 5))):

            @pl.when(index == unit_done)
            def _():
                for copy in copies:
                    mixed.near_copy(copy).start()

    psum.pass_first(0)
    psum.pass_first(1)

    @pl.loop(0, 2 * pieces)
    def _(index):
        lanes = pl.ds(pl.multiple_of(index * group, group), group)
        place = pl.ds(pl.multiple_of(flat + index * group, group), group)
        d_weights[place, :] = dot_tn(grad_both[:, lanes], held[...]).astype(BF16)

    weight_out(1).start()
    weight_out(2).start()
    mixed_outs = []
    for name in range(4):
        for k in range(HALF):
            slot, others = mixed.near_sum(name, k)
            mixed.slot(slot)[...] = mixed.add_up(slot, others).astype(BF16)
            index = HALF * name + k
            mixed_outs.append(
                pltpu.make_async_copy(
                    mixed.slot(slot),
                    mixed_hbm.at[pl.ds(index * half, half)],
                    mixed_sem.at[index],
                )
            )
            mixed_outs[-1].start()
    for k in range(HALF):
        total_ref[pl.ds(k * half, half), :] = psum.total(k).astype(BF16)
    for which in range(3):
        weight_out(which).wait()
    for copy in mixed_outs:
        copy.wait()
    for index in range(4 * HALF):
        mixed.near_copy(index).wait_send()
    gather.sent()
    psum.sent()


def expert_call(own, all_grad, scale_parts, pick, gate_matrix, up_matrix, down_matrix):
    rows, width = own.shape
    flat = gate_matrix.shape[0]
    everything = all_grad.shape[0]
    parts = pick.shape[0]
    half = rows // HALF
    weight = jax.ShapeDtypeStruct((flat, width), BF16)
    return pl.pallas_call(
        functools.partial(expert_body, flat, rows, parts),
        out_shape=(
            jax.ShapeDtypeStruct((rows, width), BF16),
            jax.ShapeDtypeStruct((4 * rows, width), BF16),
            weight,
            weight,
            weight,
        ),
        in_specs=[any_spec(), any_spec(), any_spec(), vmem_spec()] + [any_spec()] * 3,
        out_specs=(vmem_spec(), any_spec(), any_spec(), any_spec(), any_spec()),
        scratch_shapes=[
            pltpu.VMEM((everything, width), BF16),
            pltpu.VMEM((everything, width), BF16),
            pltpu.VMEM((16, parts, half), BF16),
            pltpu.VMEM((2 * flat, width), BF16),
            pltpu.VMEM((flat, width), BF16),
            pltpu.VMEM((everything, flat), F32),
            pltpu.VMEM((everything, 2 * flat), BF16),
            pltpu.VMEM((everything, flat), BF16),
            pltpu.VMEM((3 * flat, width), BF16),
            pltpu.VMEM((everything, width), BF16),
        ]
        + plane_sum_scratch(half, width)
        + [
            pltpu.SemaphoreType.DMA((PlaneGather.kinds, HALF)),
            pltpu.SemaphoreType.DMA((PlaneGather.kinds, HALF)),
            pltpu.VMEM((4 * rows, width), BF16),
            pltpu.SemaphoreType.DMA((4 * HALF,)),
            pltpu.SemaphoreType.DMA((4 * HALF,)),
            pltpu.SemaphoreType.DMA((4,)),
            pltpu.SemaphoreType.DMA((2, 16)),
            pltpu.SemaphoreType.DMA((3,)),
            pltpu.SemaphoreType.DMA((4 * HALF,)),
        ],
        compiler_params=comm_params(1),
        name="experts",
    )(own, all_grad, scale_parts, pick, gate_matrix, up_matrix, down_matrix)


class LineSum:
    def __init__(self, count, source, arrived, send, recv, parts=1):
        self.count, self.source, self.arrived, self.send, self.recv = (
            count,
            source,
            arrived,
            send,
            recv,
        )
        self.z = lax.axis_index("tp")
        self.share = source.shape[1] // count
        self.parts, self.part = parts, source.shape[0] // parts

    def columns(self, z):
        return pl.ds(pl.multiple_of(z * self.share, self.share), self.share)

    def copy(self, j, k):
        target = (self.z + j) % self.count
        rows = pl.ds(k * self.part, self.part)
        return send_to(
            self.source.at[rows, self.columns(target)],
            self.arrived.at[j - 1, rows],
            self.send.at[k, j - 1],
            self.recv.at[k, j - 1],
            tp=target,
        )

    def begin(self, k=0):
        for j in range(1, self.count):
            self.copy(j, k).start()

    def total(self):
        for k in range(self.parts):
            for j in range(1, self.count):
                self.copy(j, k).wait_recv()
        total = self.source[:, self.columns(self.z)].astype(F32)
        for j in range(1, self.count):
            total = total + self.arrived[j - 1].astype(F32)
        return total

    def sent(self):
        for k in range(self.parts):
            for j in range(1, self.count):
                self.copy(j, k).wait_send()


class LineTotal:
    def __init__(self, count, chunks, source, up_in, down_in, up_out, down_out, sems):
        self.count, self.chunks, self.source = count, chunks, source
        self.landed, self.onward, self.sems = (up_in, down_in), (up_out, down_out), sems
        self.z = lax.axis_index("tp")
        self.rows = source.shape[0] // chunks

    def copy(self, way, chunk, buffer, device):
        at = pl.ds(pl.multiple_of(chunk * self.rows, self.rows), self.rows)
        return send_to(
            buffer.at[at],
            self.landed[way].at[at],
            self.sems.at[way, 0, chunk],
            self.sems.at[way, 1, chunk],
            tp=device,
        )

    def is_first(self, way):
        return self.z == (0, self.count - 1)[way]

    def sends(self, way):
        return self.z != (self.count - 1, 0)[way]

    def begin(self):
        for way, ahead in ((0, 1), (1, -1)):

            @pl.when(self.is_first(way))
            def _():
                self.landed[way][...] = jnp.zeros_like(self.landed[way])

                @pl.loop(0, self.chunks)
                def _(chunk):
                    self.copy(way, chunk, self.source, self.z + ahead).start()

    def forward(self, way, chunk):
        ahead = (1, -1)[way]
        at = pl.ds(pl.multiple_of(chunk * self.rows, self.rows), self.rows)

        @pl.when(jnp.logical_not(self.is_first(way)))
        def _():
            self.copy(way, chunk, self.onward[way], self.z - ahead).wait_recv()

            @pl.when(self.sends(way))
            def _():
                self.onward[way][at, :] = (
                    self.landed[way][at, :].astype(F32) + self.source[at, :].astype(F32)
                ).astype(BF16)
                self.copy(way, chunk, self.onward[way], self.z + ahead).start()

    def run(self, beside):
        lower = self.z < self.count // 2

        @pl.loop(0, self.chunks + 1)
        def _(step):
            for ahead, is_here in ((0, lower), (1, jnp.logical_not(lower))):

                @pl.when(is_here & (step < self.chunks))
                def _():
                    self.forward(ahead, step)

                @pl.when(is_here & (step > 0))
                def _():
                    self.forward(1 - ahead, step - 1)

            for at, action in beside:

                @pl.when(step == at)
                def _():
                    action()

    def total(self):
        total = self.source[...].astype(F32) + self.landed[0][...].astype(F32)
        return total + self.landed[1][...].astype(F32)

    def sent(self):
        for way, ahead in ((0, 1), (1, -1)):

            @pl.when(self.sends(way))
            def _():
                @pl.loop(0, self.chunks)
                def _(chunk):
                    self.copy(way, chunk, self.source, self.z + ahead).wait_send()


def line_total_scratch(rows, width):
    return [pltpu.VMEM((rows, width), BF16)] * 4 + [pltpu.SemaphoreType.DMA((2, 2, LINE_CHUNKS))]


class OrderedGather(PlaneGather):
    def place(self, name, k):
        return self.held.at[pl.ds((self.r[name] * HALF + k) * self.half, self.half)]

    def copy(self, kind, k):
        source, device = (
            ("e", "a"),
            ("e", "b"),
            ("e", "p"),
            ("a", "b"),
            ("a", "p"),
            ("b", "p"),
            ("d", "p"),
        )[kind]
        block = self.place(source, k)
        return send_to(
            block, block, self.send.at[kind, k], self.recv.at[kind, k], ep=self.r[device]
        )

    def arrived(self, kind, k):
        source, device = (
            ("a", "a"),
            ("b", "b"),
            ("p", "p"),
            ("d", "b"),
            ("pb", "p"),
            ("pa", "p"),
            ("pd", "p"),
        )[kind]
        block = self.place(source, k)
        send_to(
            block, block, self.send.at[kind, k], self.recv.at[kind, k], ep=self.r[device]
        ).wait_recv()

    def finish(self):
        for k in range(HALF):
            for kind in (2, 4, 5, 6):
                self.arrived(kind, k)


class LineGather:
    def __init__(self, count, whole, up_send, up_recv, down_send, down_recv):
        self.count, self.whole = count, whole
        self.up_sems, self.down_sems = (up_send, up_recv), (down_send, down_recv)
        self.z = lax.axis_index("tp")
        self.share = whole.shape[1] // count

    def columns(self, z):
        return pl.ds(pl.multiple_of(z * self.share, self.share), self.share)

    def move(self, share, j, sems, target):
        block = self.whole.at[:, self.columns(share)]
        return send_to(block, block, sems[0].at[j - 1], sems[1].at[j - 1], tp=target)

    def up(self, j):
        return self.move(self.z - j + 1, j, self.up_sems, self.z + 1)

    def down(self, j):
        return self.move(self.z + j - 1, j, self.down_sems, self.z - 1)

    def sends(self, j, act):
        @pl.when((self.z < self.count - 1) & (self.z >= j - 1))
        def _():
            act(self.up(j))

        @pl.when((self.z > 0) & (self.z + j <= self.count))
        def _():
            act(self.down(j))

    def begin(self):
        self.sends(1, lambda copy: copy.start())

    def step(self, j):
        @pl.when(self.z >= j)
        def _():
            self.move(self.z - j, j, self.up_sems, self.z - 1).wait_recv()

        @pl.when(self.z + j < self.count)
        def _():
            self.move(self.z + j, j, self.down_sems, self.z + 1).wait_recv()

        if j + 1 < self.count:
            self.sends(j + 1, lambda copy: copy.start())

    def wait(self):
        for j in range(1, self.count):
            self.step(j)

    def sent(self):
        for j in range(1, self.count):
            self.sends(j, lambda copy: copy.wait_send())


def line_peers(count):
    z = lax.axis_index("tp")
    return [(z + j) % count for j in range(1, count)]


class FarSum:
    def __init__(self, r, part, far, first, second, half, send, recv):
        self.r, self.part, self.half = r, part, half
        self.far, self.first, self.second = far, first, second
        self.send, self.recv = send, recv

    def rows(self, buffer, index):
        return buffer.at[pl.ds(index * self.half, self.half)]

    def copy(self, kind, k):
        block, target, device = (
            (3, self.far, "b"),
            (1, self.first, "a"),
            (2, self.second, "b"),
        )[kind]
        return send_to(
            self.rows(self.part, HALF * block + k),
            self.rows(target, k),
            self.send.at[kind, k],
            self.recv.at[kind, k],
            ep=self.r[device],
        )

    def pass_first(self, k):
        self.copy(0, k).wait_recv()
        block = self.rows(self.part, HALF + k)
        block[...] = (block[...].astype(F32) + self.rows(self.far, k)[...].astype(F32)).astype(BF16)
        self.copy(1, k).start()

    def total(self, k):
        self.copy(1, k).wait_recv()
        self.copy(2, k).wait_recv()
        total = self.rows(self.part, k)[...].astype(F32)
        return total + self.rows(self.first, k)[...].astype(F32) + self.rows(self.second, k)[...].astype(F32)

    def sent(self):
        for kind in range(3):
            for k in range(HALF):
                self.copy(kind, k).wait_send()


def turn(values, cosine, sine_table):
    return values * cosine + pltpu.roll(values, HEAD_DIM // 2, 1) * sine_table


def unit_of(values):
    return values * lax.rsqrt(jnp.mean(values * values, axis=-1, keepdims=True) + epsilon)


def front_body(
    gain_at,
    ep_count,
    tp_count,
    rows,
    heads,
    send_ref,
    recv_ref,
    small_ref,
    cosine_ref,
    sine_ref,
    mask_ref,
    query_hbm,
    key_hbm,
    value_hbm,
    out_hbm,
    x_ref,
    grad_ref,
    hidden_ref,
    moe_ref,
    proj_ref,
    turned_ref,
    keys_ref,
    values_ref,
    probs_ref,
    context_ref,
    small_all,
    normed,
    all_grad,
    w_in_hbm,
    w_out_hbm,
    w_in,
    w_out,
    dealt,
    x_wire,
    grad_wire,
    attn,
    up_in,
    down_in,
    up_out,
    down_out,
    total_sems,
    deal_send,
    deal_recv,
    small_send,
    small_recv,
    in_send,
    in_recv,
    out_send,
    out_recv,
    grad_send,
    grad_recv,
    x_line,
    grad_line,
    local_sem,
):
    r = roles()
    e = r["e"]
    z = lax.axis_index("tp")
    half = rows // HALF
    q_width = heads * HEAD_DIM
    share = x_wire.shape[1] // tp_count
    per_pair = rows // ep_count
    micro_rows = rows // MICRO
    own = pl.ds(e * rows, rows)
    loads = [
        pltpu.make_async_copy(query_hbm, w_in.at[own, pl.ds(0, q_width)], local_sem.at[0]),
        pltpu.make_async_copy(key_hbm, w_in.at[own, pl.ds(q_width, HEAD_DIM)], local_sem.at[1]),
        pltpu.make_async_copy(
            value_hbm, w_in.at[own, pl.ds(q_width + HEAD_DIM, HEAD_DIM)], local_sem.at[2]
        ),
        pltpu.make_async_copy(out_hbm, w_out.at[own], local_sem.at[3]),
    ]
    for load in loads:
        load.start()
    small_rows = small_ref.shape[0]
    small_all[pl.ds(e * small_rows, small_rows), :] = small_ref[...]
    others = [(e + j) % ep_count for j in range(1, ep_count)]
    greet(others, line_peers(tp_count))

    def deal(j, source, target):
        return send_to(
            send_ref.at[pl.ds(target * per_pair, per_pair)],
            dealt.at[pl.ds(source * per_pair, per_pair)],
            deal_send.at[j - 1],
            deal_recv.at[j - 1],
            ep=target,
        )

    for j in range(1, ep_count):
        deal(j, e, (e + j) % ep_count).start()
    mine = pl.ds(pl.multiple_of(e * per_pair, per_pair), per_pair)
    dealt[mine, :] = send_ref[mine, :]
    gather_small = OrderedGather(r, small_all, small_rows // HALF, small_send, small_recv)
    gather_in = OrderedGather(r, w_in, half, in_send, in_recv)
    gather_out = OrderedGather(r, w_out, half, out_send, out_recv)
    gather_grad = OrderedGather(r, all_grad, half, grad_send, grad_recv)
    gather_small.begin()
    for load in loads:
        load.wait()
    gather_in.begin()
    for j in range(1, ep_count):
        deal(j, (e + ep_count - j) % ep_count, (e + j) % ep_count).wait_recv()
    x_gather = LineGather(tp_count, x_wire, *[x_line.at[i] for i in range(4)])
    grad_gather = LineGather(tp_count, grad_wire, *[grad_line.at[i] for i in range(4)])
    x_wire[:, x_gather.columns(z)] = dealt[:, :share]
    grad_wire[:, x_gather.columns(z)] = dealt[:, share:]
    x_gather.begin()
    for k in range(HALF):
        gather_small.pass_near(k)
    x_gather.step(1)
    gather_in.pass_near(0)
    x_gather.step(2)
    grad_gather.begin()
    gather_in.pass_near(1)
    gather_out.begin()
    x_gather.step(3)
    for k in range(HALF):
        gather_small.pass_far(k)
    gather_small.finish()

    def gain_row(place, column, width):
        at = place * small_rows + gain_at
        return small_all[at : at + 1, column : column + width].astype(F32)

    x_rows = dot_nn(recv_ref[...], x_wire[...])
    x_ref[...] = x_rows.astype(BF16)
    unit_one = unit_of(x_rows)
    for place in range(ep_count):
        at = slice(place * rows, (place + 1) * rows)
        normed[:, at] = (unit_one[:, at] * gain_row(place, 0, rows)).astype(BF16)
    for k in range(HALF):
        gather_in.pass_far(k)
    grad_gather.step(1)
    gather_in.finish()
    gather_out.pass_near(0)

    proj_ref[...] = dot_nn(normed[...], w_in[...])
    grad_gather.step(2)
    gather_out.pass_near(1)
    column = 2 * rows
    gain_query = sum(gain_row(place, column, HEAD_DIM) for place in range(ep_count))
    gain_key = sum(gain_row(place, column + HEAD_DIM, HEAD_DIM) for place in range(ep_count))
    cosine, sine_table = cosine_ref[...], sine_ref[...]
    keys_ref[...] = turn(
        unit_of(proj_ref[:, q_width : q_width + HEAD_DIM]) * gain_key, cosine, sine_table
    ).astype(BF16)
    values_ref[...] = proj_ref[:, q_width + HEAD_DIM :].astype(BF16)


    @pl.loop(0, heads)
    def _(head):
        lanes = pl.ds(pl.multiple_of(head * HEAD_DIM, HEAD_DIM), HEAD_DIM)
        queries = turn(unit_of(proj_ref[:, lanes]) * gain_query, cosine, sine_table).astype(BF16)
        for micro in range(MICRO):
            at = pl.ds(
                pl.multiple_of((micro * heads + head) * micro_rows, micro_rows), micro_rows
            )
            turned_ref[at, :] = queries[micro * micro_rows : (micro + 1) * micro_rows]

    for k in range(HALF):
        gather_out.pass_far(k)
    for micro in range(MICRO):
        within = slice(micro * micro_rows, (micro + 1) * micro_rows)
        stacked = slice(micro * heads * micro_rows, (micro + 1) * heads * micro_rows)
        scores = dot_nt(turned_ref[stacked, :], keys_ref[within, :]) * HEAD_DIM ** (-0.5)
        mask = mask_ref[within, :]
        scores = scores.reshape(heads, micro_rows, micro_rows)
        scores = jnp.where(mask[None] > 0.0, scores, -1e30)
        exponent = jnp.exp(scores - jnp.max(scores, axis=-1, keepdims=True))
        probs = exponent / jnp.sum(exponent, axis=-1, keepdims=True)
        probs = probs.reshape(heads * micro_rows, micro_rows)
        probs_ref[stacked, :] = probs
        context = dot_nn(probs.astype(BF16), values_ref[within, :]).astype(BF16)
        for head in range(heads):
            context_ref[within, head * HEAD_DIM : (head + 1) * HEAD_DIM] = context[
                head * micro_rows : (head + 1) * micro_rows
            ]

    grad_gather.step(3)
    grad_ref[...] = dot_nn(recv_ref[...], grad_wire[...]).astype(BF16)
    grad_here = pltpu.make_async_copy(grad_ref, all_grad.at[own], local_sem.at[4])
    grad_here.start()
    grad_here.wait()
    gather_grad.begin()
    gather_out.finish()

    attn[...] = dot_nt(context_ref[...], w_out[...]).astype(BF16)
    over_line = LineTotal(tp_count, LINE_CHUNKS, attn, up_in, down_in, up_out, down_out, total_sems)
    over_line.begin()
    w_in_out = pltpu.make_async_copy(w_in, w_in_hbm, local_sem.at[0])
    w_out_out = pltpu.make_async_copy(w_out, w_out_hbm, local_sem.at[1])
    w_in_out.start()
    w_out_out.start()
    over_line.run(
        (
            (LINE_CHUNKS * 5 // 8, lambda: gather_grad.pass_near(0)),
            (LINE_CHUNKS, lambda: gather_grad.pass_near(1)),
        )
    )
    hidden = x_ref[...].astype(F32) + over_line.total()
    hidden_ref[...] = hidden
    gather_grad.pass_far(0)
    unit_two = unit_of(hidden)
    for place in range(ep_count):
        at = slice(place * rows, (place + 1) * rows)
        moe_ref[:, at] = (unit_two[:, at] * gain_row(place, rows, rows)).astype(BF16)
    gather_grad.pass_far(1)
    gather_grad.finish()
    for j in range(1, ep_count):
        deal(j, e, (e + j) % ep_count).wait_send()
    x_gather.sent()
    grad_gather.sent()
    over_line.sent()
    for gather in (gather_small, gather_in, gather_out, gather_grad):
        gather.sent()
    w_in_out.wait()
    w_out_out.wait()


def front_call(
    gain_at, ep_count, tp_count, send_rows, recv, small, cosine, sine_table, mask, query, key, value, out
):
    rows = send_rows.shape[0]
    share = send_rows.shape[1] // 2
    width = share * tp_count
    q_width = query.shape[1]
    heads = q_width // HEAD_DIM
    everything = rows * ep_count
    in_width = q_width + 2 * HEAD_DIM
    micro_rows = rows // MICRO
    shape = jax.ShapeDtypeStruct
    gather_sems = pltpu.SemaphoreType.DMA((PlaneGather.kinds, HALF))
    line_sems = pltpu.SemaphoreType.DMA((4, tp_count - 1))
    return pl.pallas_call(
        functools.partial(front_body, gain_at, ep_count, tp_count, rows, heads),
        out_shape=(
            shape((rows, width), BF16),
            shape((rows, width), BF16),
            shape((rows, width), F32),
            shape((rows, width), BF16),
            shape((rows, in_width), F32),
            shape((heads * rows, HEAD_DIM), BF16),
            shape((rows, HEAD_DIM), BF16),
            shape((rows, HEAD_DIM), BF16),
            shape((heads * rows, micro_rows), F32),
            shape((rows, q_width), BF16),
            shape((ep_count * small.shape[0], small.shape[1]), BF16),
            shape((rows, width), BF16),
            shape((everything, width), BF16),
            shape((everything, in_width), BF16),
            shape((everything, q_width), BF16),
        ),
        in_specs=[vmem_spec()] * 6 + [any_spec()] * 4,
        out_specs=tuple([vmem_spec()] * 12 + [any_spec()] * 3),
        scratch_shapes=[
            pltpu.VMEM((everything, in_width), BF16),
            pltpu.VMEM((everything, q_width), BF16),
            pltpu.VMEM(send_rows.shape, BF16),
            pltpu.VMEM((rows, width), BF16),
            pltpu.VMEM((rows, width), BF16),
            pltpu.VMEM((rows, width), BF16),
        ]
        + line_total_scratch(rows, width)
        + [pltpu.SemaphoreType.DMA((ep_count - 1,))] * 2
        + [gather_sems] * 8
        + [line_sems] * 2
        + [pltpu.SemaphoreType.DMA((5,))],
        compiler_params=comm_params(3),
        name="front",
    )(send_rows, recv, small, cosine, sine_table, mask, query, key, value, out)


def fold(values):
    rows, width = values.shape
    return jnp.sum(values.reshape(rows // 8, 8, width), axis=0)


class Straight:
    def __init__(self, axis, count, source, landed, send, recv):
        self.axis, self.count, self.source, self.landed = axis, count, source, landed
        self.send, self.recv = send, recv
        self.me = lax.axis_index(axis)

    def copy(self, j):
        target = (self.me + j) % self.count
        return send_to(
            self.source(target),
            self.landed(j),
            self.send.at[j - 1],
            self.recv.at[j - 1],
            **{self.axis: target},
        )

    def begin(self):
        for j in range(1, self.count):
            self.copy(j).start()

    def wait(self):
        for j in range(1, self.count):
            self.copy(j).wait_recv()

    def sent(self):
        for j in range(1, self.count):
            self.copy(j).wait_send()


def back_body(
    gain_at,
    ep_count,
    tp_count,
    rows,
    heads,
    operand_count,
    partial_ref,
    mixed_hbm,
    w_in_hbm,
    w_out_hbm,
    *rest,
):
    operand_hbm, rest = rest[:operand_count], rest[operand_count:]
    outs, rest = rest[:5], rest[5:]
    operand_refs, rest = rest[:operand_count], rest[operand_count:]
    back_steps(
        gain_at,
        ep_count,
        tp_count,
        rows,
        heads,
        operand_hbm,
        operand_refs,
        partial_ref,
        mixed_hbm,
        w_in_hbm,
        w_out_hbm,
        *outs,
        *rest,
    )


def back_steps(
    gain_at,
    ep_count,
    tp_count,
    rows,
    heads,
    operand_hbm,
    operand_refs,
    partial_ref,
    mixed_hbm,
    w_in_hbm,
    w_out_hbm,
    layer_out,
    layer_grad,
    d_in,
    d_out,
    sums_out,
    w_in,
    w_out,
    mixed_part,
    mixed_far,
    mixed_first,
    mixed_second,
    mixed_ref,
    up_in,
    down_in,
    up_out,
    down_out,
    total_sems,
    grad_attn,
    stacked_grad,
    grad_turned,
    grad_proj,
    normed_part,
    mixed_line,
    normed_line,
    row_sums,
    row_line,
    sums,
    sums_near,
    sums_line,
    home_send,
    home_recv,
    out_part,
    in_part,
    *rest,
):
    (
        x_ref,
        hidden_ref,
        grad_ref,
        normed_ref,
        proj_ref,
        turned_ref,
        keys_ref,
        values_ref,
        probs_ref,
        context_ref,
        small_all,
        cosine_ref,
        sine_ref,
        send_ref,
        recv_ref,
    ) = operand_refs
    out_bufs, out_sems = rest[0:4], rest[4:8]
    in_bufs, in_sems = rest[8:12], rest[12:16]
    mixed_sems, normed_sems, row_sems, sum_sems, sum_line_sems, home_sems = (
        rest[16:18],
        rest[18:20],
        rest[20:22],
        rest[22:24],
        rest[24:26],
        rest[26:28],
    )
    far_sems, operand_sem, mixed_sem, local_sem = (rest[28:30], *rest[30:33])
    r = roles()
    e = r["e"]
    z = lax.axis_index("tp")
    half = rows // HALF
    width = x_ref.shape[1]
    share = width // tp_count
    q_width = heads * HEAD_DIM
    micro_rows = rows // MICRO
    per_pair = rows // ep_count
    small_rows = small_all.shape[0] // ep_count
    loads = [
        pltpu.make_async_copy(w_out_hbm, w_out, local_sem.at[0]),
        pltpu.make_async_copy(w_in_hbm, w_in, local_sem.at[1]),
    ]
    blocks = [
        pltpu.make_async_copy(
            mixed_hbm.at[pl.ds(index * half, half)],
            mixed_part.at[pl.ds(index * half, half)],
            mixed_sem.at[index],
        )
        for index in range(4 * HALF)
    ]
    for index in (6, 4, 7, 5, 2, 3, 0, 1):
        blocks[index].start()
    operand_loads = [
        pltpu.make_async_copy(source, target, operand_sem.at[index])
        for index, (source, target) in enumerate(zip(operand_hbm, operand_refs))
    ]
    for load in operand_loads + loads:
        load.start()
    greet([(e + j) % ep_count for j in range(1, ep_count)], line_peers(tp_count))

    grad_sum = LineTotal(
        tp_count, LINE_CHUNKS, partial_ref, up_in, down_in, up_out, down_out, total_sems
    )
    grad_sum.begin()
    over_chips = FarSum(r, mixed_part, mixed_far, mixed_first, mixed_second, half, *far_sems)
    for k in range(HALF):
        for kind, block in ((0, 6), (2, 4)):
            blocks[block + k].wait()
            over_chips.copy(kind, k).start()
    for index in range(4):
        blocks[index].wait()
    mixed_sum = LineSum(tp_count, mixed_ref, mixed_line, *mixed_sems, HALF)

    def mixed_half(k):
        mixed_ref[pl.ds(k * half, half), :] = over_chips.total(k).astype(BF16)
        mixed_sum.begin(k)

    grad_sum.run(
        (
            (LINE_CHUNKS // 4, lambda: over_chips.pass_first(0)),
            (LINE_CHUNKS * 5 // 8, lambda: over_chips.pass_first(1)),
        )
    )
    mixed_half(0)
    for load in operand_loads:
        load.wait()
    out_sum = PlaneSum(r, out_part, *out_bufs, half, out_sems)
    in_sum = PlaneSum(r, in_part, *in_bufs, half, in_sems)

    def gain_row(place, column, wide):
        at = place * small_rows + gain_at
        return small_all[at : at + 1, column : column + wide].astype(F32)

    hidden = hidden_ref[...]
    inverse_two = lax.rsqrt(jnp.mean(hidden * hidden, axis=-1, keepdims=True) + epsilon)
    unit_two = hidden * inverse_two
    grad_moe = grad_sum.total()
    moe_sums = fold(grad_moe * unit_two)
    gain_moe = jnp.concatenate([gain_row(place, rows, rows) for place in range(ep_count)], axis=1)
    scaled = grad_moe * gain_moe
    grad_hidden = grad_ref[...].astype(F32) + inverse_two * (
        scaled - unit_two * jnp.mean(scaled * unit_two, axis=-1, keepdims=True)
    )
    grad_attn[...] = grad_hidden.astype(BF16)
    sums[...] = jnp.zeros_like(sums)
    for place in range(ep_count):
        sums[place * 8 : place * 8 + 8, rows : 2 * rows] = moe_sums[
            :, place * rows : (place + 1) * rows
        ]

    near_of = {"pd": (6, 7), "pb": (2, 3), "pa": (4, 5), "p": (0, 1)}
    slots_of = {
        "pd": SLOT_PD,
        "d": SLOT_D,
        "pb": SLOT_PB,
        "b": SLOT_B,
        "pa": SLOT_PA,
        "a": SLOT_A,
        "p": SLOT_P,
        "e": SLOT_E,
    }

    def weight_blocks(plane, left, right):
        for name, slots in slots_of.items():
            lanes = pl.ds(pl.multiple_of(r[name] * rows, rows), rows)
            block = dot_tn(left[:, lanes], right[...]).astype(BF16)
            for k in range(HALF):
                plane.slot(slots[k])[...] = block[k * half : (k + 1) * half]
                if name in near_of:
                    plane.near_copy(near_of[name][k]).start()

    weight_blocks(out_sum, grad_attn, context_ref)
    loads[0].wait()
    grad_context = dot_nn(grad_attn[...], w_out[...]).astype(BF16)
    for micro in range(MICRO):
        for head in range(heads):
            at = (micro * heads + head) * micro_rows
            stacked_grad[at : at + micro_rows, :] = grad_context[
                micro * micro_rows : (micro + 1) * micro_rows,
                head * HEAD_DIM : (head + 1) * HEAD_DIM,
            ]
    for k in range(HALF):
        out_sum.pass_far(k)
    for k in range(HALF):
        out_sum.pass_second(k)
    mixed_half(1)

    cosine, sine_table = cosine_ref[...], -sine_ref[...]
    column = 2 * rows
    gain_query = sum(gain_row(place, column, HEAD_DIM) for place in range(ep_count))
    gain_key = sum(gain_row(place, column + HEAD_DIM, HEAD_DIM) for place in range(ep_count))
    scale = HEAD_DIM ** (-0.5)
    grad_keys = []
    for micro in range(MICRO):
        within = slice(micro * micro_rows, (micro + 1) * micro_rows)
        stacked = slice(micro * heads * micro_rows, (micro + 1) * heads * micro_rows)
        probs = probs_ref[stacked, :]
        grad_probs = dot_nt(stacked_grad[stacked, :], values_ref[within, :])
        delta = jnp.sum(probs * grad_probs, axis=-1, keepdims=True)
        grad_scores = (probs * (grad_probs - delta)).astype(BF16)
        grad_turned[stacked, :] = dot_nn(grad_scores, keys_ref[within, :]) * scale
        grad_keys.append(dot_tn(grad_scores, turned_ref[stacked, :]) * scale)
        grad_proj[within, q_width + HEAD_DIM :] = dot_tn(
            probs.astype(BF16), stacked_grad[stacked, :]
        ).astype(BF16)

    def unturn(grad, values, gain):
        unturned = turn(grad, cosine, sine_table)
        inverse = lax.rsqrt(jnp.mean(values * values, axis=-1, keepdims=True) + epsilon)
        unit = values * inverse
        scaled = unturned * gain
        result = inverse * (scaled - unit * jnp.mean(scaled * unit, axis=-1, keepdims=True))
        return fold(unturned * unit), result.astype(BF16)

    key_sums, grad_key = unturn(
        jnp.concatenate(grad_keys, axis=0), proj_ref[:, q_width : q_width + HEAD_DIM], gain_key
    )
    grad_proj[:, q_width : q_width + HEAD_DIM] = grad_key
    for k in range(HALF):
        out_sum.pass_first(k)

    def one_head(head, total):
        lanes = pl.ds(pl.multiple_of(head * HEAD_DIM, HEAD_DIM), HEAD_DIM)
        grads = [
            grad_turned[
                pl.ds(pl.multiple_of((micro * heads + head) * micro_rows, micro_rows), micro_rows),
                :,
            ]
            for micro in range(MICRO)
        ]
        part, grad = unturn(jnp.concatenate(grads, axis=0), proj_ref[:, lanes], gain_query)
        grad_proj[:, lanes] = grad
        return total + part

    query_sums = lax.fori_loop(0, heads, one_head, jnp.zeros((8, HEAD_DIM), F32))
    for place in range(ep_count):
        at = slice(place * 8, place * 8 + 8)
        sums[at, column : column + HEAD_DIM] = query_sums
        sums[at, column + HEAD_DIM :] = key_sums

    x_rows = x_ref[...].astype(F32)
    inverse_one = lax.rsqrt(jnp.mean(x_rows * x_rows, axis=-1, keepdims=True) + epsilon)
    gain_attn = jnp.concatenate([gain_row(place, 0, rows) for place in range(ep_count)], axis=1)
    loads[1].wait()
    partial = dot_nt(grad_proj[...], w_in[...])
    normed_part[...] = partial.astype(BF16)
    normed_sum = LineSum(tp_count, normed_part, normed_line, *normed_sems)
    normed_sum.begin()
    weight_blocks(in_sum, normed_ref, grad_proj)
    along = jnp.sum(partial * gain_attn * (x_rows * inverse_one), axis=-1, keepdims=True)
    row_sums[...] = jnp.transpose(jnp.broadcast_to(along, (rows, HEAD_DIM)))[:8]
    over_rows = Straight("tp", tp_count, lambda _: row_sums, lambda j: row_line.at[j - 1], *row_sems)
    over_rows.begin()
    for k in range(HALF):
        in_sum.pass_far(k)
    for k in range(HALF):
        in_sum.pass_second(k)
    for k in range(HALF):
        d_out[pl.ds(k * half, half), :] = out_sum.total(k).astype(BF16)
    for k in range(HALF):
        in_sum.pass_first(k)

    lanes = pl.ds(pl.multiple_of(z * share, share), share)
    layer_rows = (hidden_ref[:, lanes] + mixed_sum.total()).astype(BF16)
    over_rows.wait()
    all_rows = row_sums[...]
    for j in range(1, tp_count):
        all_rows = all_rows + row_line[j - 1]
    mean = jnp.transpose(jnp.broadcast_to(all_rows[:1], (HEAD_DIM, rows)))[:, :1] / width
    grad_normed = normed_sum.total()
    unit_share = x_ref[:, lanes].astype(F32) * inverse_one
    places = share // rows
    gain_share = []
    for place in range(places):
        at = pl.multiple_of((z * places + place) * small_rows + gain_at, 16)
        gain_share.append(small_all[pl.ds(at, 16), :rows][:1].astype(F32))
    scaled = grad_normed * jnp.concatenate(gain_share, axis=1)
    grad_rows = grad_attn[:, lanes].astype(F32) + inverse_one * (scaled - unit_share * mean)
    both = jnp.concatenate([layer_rows, grad_rows.astype(BF16)], axis=1)
    home_send[...] = dot_tn(recv_ref[...], both).astype(BF16)
    home = Straight(
        "ep",
        ep_count,
        lambda target: home_send.at[pl.ds(pl.multiple_of(target * per_pair, per_pair), per_pair)],
        lambda j: home_recv.at[pl.ds(pl.multiple_of(e * per_pair, per_pair), per_pair)],
        *home_sems,
    )
    home.begin()
    norm_sums = fold(grad_normed * unit_share)
    for place in range(places):
        at = pl.multiple_of((z * places + place) * 8, 8)
        sums[pl.ds(at, 8), :rows] = norm_sums[:, place * rows : (place + 1) * rows]
    over_plane = Straight(
        "ep",
        ep_count,
        lambda target: sums.at[pl.ds(pl.multiple_of(target * 8, 8), 8)],
        lambda j: sums_near.at[j - 1],
        *sum_sems,
    )
    over_plane.begin()
    mine = pl.ds(pl.multiple_of(e * per_pair, per_pair), per_pair)
    home_recv[mine, :] = home_send[mine, :]
    over_plane.wait()
    plane_sums = sums[pl.ds(pl.multiple_of(e * 8, 8), 8), :]
    for j in range(1, ep_count):
        plane_sums = plane_sums + sums_near[j - 1]
    sums_line[0] = plane_sums
    over_line = Straight(
        "tp", tp_count, lambda _: sums_line.at[0], lambda j: sums_line.at[j], *sum_line_sems
    )
    over_line.begin()
    for j in range(1, ep_count):
        source = (e + ep_count - j) % ep_count
        block = home_recv.at[pl.ds(pl.multiple_of(source * per_pair, per_pair), per_pair)]
        send_to(block, block, home_sems[0].at[j - 1], home_sems[1].at[j - 1], ep=source).wait_recv()
    arrived = dot_tn(send_ref[...], home_recv[...])
    layer_out[...] = arrived[:, :share].astype(BF16)
    layer_grad[...] = arrived[:, share:].astype(BF16)
    over_line.wait()
    line_sums = plane_sums
    for j in range(1, tp_count):
        line_sums = line_sums + sums_line[j]
    sums_out[:, :rows] = line_sums[:, :rows]
    sums_out[:, rows : 2 * rows] = plane_sums[:, rows : 2 * rows]
    sums_out[:, 2 * rows :] = line_sums[:, 2 * rows :]
    for k in range(HALF):
        d_in[pl.ds(k * half, half), :] = in_sum.total(k).astype(BF16)
    for op in (
        grad_sum,
        over_chips,
        mixed_sum,
        normed_sum,
        over_rows,
        home,
        over_plane,
        over_line,
        out_sum,
        in_sum,
    ):
        op.sent()


def back_call(gain_at, ep_count, tp_count, partial, mixed, w_in_all, w_out_all, operands):
    rows, width = partial.shape
    share = width // tp_count
    in_width = w_in_all.shape[1]
    q_width = w_out_all.shape[1]
    heads = q_width // HEAD_DIM
    half = rows // HALF
    everything = rows * ep_count
    sums_width = 2 * rows + 2 * HEAD_DIM
    shape = jax.ShapeDtypeStruct

    def pair(count):
        return [pltpu.SemaphoreType.DMA((count,))] * 2

    return pl.pallas_call(
        functools.partial(back_body, gain_at, ep_count, tp_count, rows, heads, len(operands)),
        out_shape=(
            shape((rows, share), BF16),
            shape((rows, share), BF16),
            shape((rows, in_width), BF16),
            shape((rows, q_width), BF16),
            shape((8, sums_width), F32),
        ),
        in_specs=[vmem_spec()] + [any_spec()] * (3 + len(operands)),
        out_specs=tuple([vmem_spec()] * 5),
        scratch_shapes=[pltpu.VMEM(operand.shape, operand.dtype) for operand in operands]
        + [
            pltpu.VMEM((everything, in_width), BF16),
            pltpu.VMEM((everything, q_width), BF16),
            pltpu.VMEM((4 * rows, width), BF16),
            pltpu.VMEM((rows, width), BF16),
            pltpu.VMEM((rows, width), BF16),
            pltpu.VMEM((rows, width), BF16),
            pltpu.VMEM((rows, width), BF16),
        ]
        + line_total_scratch(rows, width)
        + [
            pltpu.VMEM((rows, width), BF16),
            pltpu.VMEM((heads * rows, HEAD_DIM), BF16),
            pltpu.VMEM((heads * rows, HEAD_DIM), F32),
            pltpu.VMEM((rows, in_width), BF16),
            pltpu.VMEM((rows, width), BF16),
            pltpu.VMEM((tp_count - 1, rows, share), BF16),
            pltpu.VMEM((tp_count - 1, rows, share), BF16),
            pltpu.VMEM((8, rows), F32),
            pltpu.VMEM((tp_count - 1, 8, rows), F32),
            pltpu.VMEM((8 * ep_count, sums_width), F32),
            pltpu.VMEM((ep_count - 1, 8, sums_width), F32),
            pltpu.VMEM((tp_count, 8, sums_width), F32),
            pltpu.VMEM((rows, 2 * share), BF16),
            pltpu.VMEM((rows, 2 * share), BF16),
            pltpu.VMEM((everything, q_width), BF16),
            pltpu.VMEM((everything, in_width), BF16),
        ]
        + plane_sum_scratch(half, q_width)
        + plane_sum_scratch(half, in_width)
        + [pltpu.SemaphoreType.DMA((HALF, tp_count - 1))] * 2
        + [pltpu.SemaphoreType.DMA((1, tp_count - 1))] * 2
        + pair(tp_count - 1)
        + pair(ep_count - 1)
        + pair(tp_count - 1)
        + pair(ep_count - 1)
        + [pltpu.SemaphoreType.DMA((3, HALF))] * 2
        + [
            pltpu.SemaphoreType.DMA((len(operands),)),
            pltpu.SemaphoreType.DMA((4 * HALF,)),
            pltpu.SemaphoreType.DMA((2,)),
        ],
        compiler_params=comm_params(4),
        name="back",
    )(partial, mixed, w_in_all, w_out_all, *operands)


def plain_layer(
    layer_in,
    token_order,
    seq_lengths,
    routes,
    route_weights,
    w_query,
    w_key,
    w_value,
    w_out,
    norm_attn,
    norm_moe,
    query_gain,
    key_gain,
    w_gate,
    w_up,
    w_down,
    grad_out,
):
    ep_count = lax.axis_size("ep")
    tp_count = lax.axis_size("tp")
    tp_index = lax.axis_index("tp")
    ep_index = lax.axis_index("ep")
    local_experts, hidden_here, model_width = w_gate.shape
    experts = local_experts * ep_count
    rows_dev = layer_in.shape[0]
    micro_rows = rows_dev // MICRO
    share_width = layer_in.shape[1]
    score_scale = HEAD_DIM ** (-0.5)

    send, recv = deal_matrices(token_order, ep_index, rows_dev, ep_count)
    both = jnp.concatenate([layer_in, grad_out], axis=1)
    got = permute_rows(recv, exchange(permute_rows(send, both), ep_count))
    layer_full = lax.all_gather(got[:, :share_width], "tp", axis=1, tiled=True)
    grad_full = lax.all_gather(got[:, share_width:], "tp", axis=1, tiled=True)

    q_width, kv_width = w_query.shape[1], w_key.shape[1]
    packed = jnp.concatenate([w_query, w_out, w_key, w_value], axis=1)
    packed = lax.all_gather(packed, "ep", axis=0, tiled=True)
    full_query = packed[:, :q_width]
    full_out = packed[:, q_width : 2 * q_width]
    full_kv = packed[:, 2 * q_width :]
    gains = jnp.concatenate([norm_attn, norm_moe, query_gain, key_gain]).reshape(1, -1)
    gains = lax.all_gather(gains, "ep", axis=0, tiled=True).astype(F32)
    part = norm_attn.shape[0]
    head_part = query_gain.shape[0]
    gain_attn = gains[:, :part].reshape(-1)
    gain_moe = gains[:, part : 2 * part].reshape(-1)
    gain_query = gains[:, 2 * part : 2 * part + head_part].reshape(-1)
    gain_key = gains[:, 2 * part + head_part :].reshape(-1)

    expert_ids = jnp.arange(experts, dtype=jnp.int32)
    dense = jnp.sum(
        jnp.where(routes[:, :, None] == expert_ids[None, None, :], route_weights[:, :, None], 0.0),
        axis=1,
    )
    scale_all = lax.all_gather(dense, "ep", axis=0, tiled=True)
    scale = lax.dynamic_slice_in_dim(scale_all, ep_index * local_experts, local_experts, 1)
    all_grad = lax.all_gather(grad_full, "ep", axis=0, tiled=True)

    heads_here = q_width // HEAD_DIM
    kv_here = kv_width // HEAD_DIM
    group_size = heads_here // kv_here
    segment, position = jax.vmap(positions_of, in_axes=(0, None))(seq_lengths, micro_rows)
    cosine, sine_table = rope_tables(position.reshape(-1), HEAD_DIM // 2)
    layer_float = layer_full.astype(F32)
    inverse_one = inverse_rms(layer_float)
    unit_one = layer_float * inverse_one
    normed = (unit_one * gain_attn).astype(BF16)
    query_proj = dot_nn(normed, full_query).reshape(rows_dev, heads_here, HEAD_DIM)
    kv_proj = dot_nn(normed, full_kv)
    key_proj = kv_proj[:, :kv_width].reshape(rows_dev, kv_here, HEAD_DIM)
    value_proj = kv_proj[:, kv_width:].reshape(rows_dev, kv_here, HEAD_DIM)
    inverse_query = inverse_rms(query_proj)
    unit_query = query_proj * inverse_query
    inverse_key = inverse_rms(key_proj)
    unit_key = key_proj * inverse_key
    queries = (
        rotate(unit_query * gain_query, cosine, sine_table)
        .astype(BF16)
        .reshape(MICRO, micro_rows, kv_here, group_size, HEAD_DIM)
    )
    key_rows = (
        rotate(unit_key * gain_key, cosine, sine_table)
        .astype(BF16)
        .reshape(MICRO, micro_rows, kv_here, HEAD_DIM)
    )
    values = value_proj.astype(BF16).reshape(MICRO, micro_rows, kv_here, HEAD_DIM)
    scores = (
        jnp.einsum("mqkgd,mtkd->mkgqt", queries, key_rows, preferred_element_type=F32)
        * score_scale
    )
    offsets = jnp.arange(micro_rows, dtype=jnp.int32)
    allowed = (segment[:, :, None] == segment[:, None, :]) & (
        offsets[None, None, :] <= offsets[None, :, None]
    )
    scores = jnp.where(allowed[:, None, None], scores, -1e30)
    row_peak = jnp.max(scores, axis=-1, keepdims=True)
    exponent = jnp.exp(scores - row_peak)
    attn_probs = exponent / jnp.sum(exponent, axis=-1, keepdims=True)
    probs_low = attn_probs.astype(BF16)
    context = jnp.einsum("mkgqt,mtkd->mqkgd", probs_low, values, preferred_element_type=F32)
    context_low = context.reshape(rows_dev, heads_here * HEAD_DIM).astype(BF16)
    attn_part = dot_nt(context_low, full_out)
    attn_out = lax.psum(attn_part.astype(BF16), "tp").astype(F32)
    hidden = layer_float + attn_out
    inverse_two = inverse_rms(hidden)
    unit_two = hidden * inverse_two
    moe_in = (unit_two * gain_moe).astype(BF16)

    all_in = lax.all_gather(moe_in, "ep", axis=0, tiled=True)
    flat = local_experts * hidden_here
    gate_matrix = w_gate.reshape(flat, model_width)
    up_matrix = w_up.reshape(flat, model_width)
    down_matrix = w_down.reshape(flat, model_width)
    row_scale = jnp.repeat(scale, hidden_here, axis=1)
    gate_pre = dot_nt(all_in, gate_matrix)
    up_pre = dot_nt(all_in, up_matrix)
    grad_active = dot_nt(all_grad, down_matrix) * row_scale
    sigmoid_gate = jax.nn.sigmoid(gate_pre)
    silu_gate = gate_pre * sigmoid_gate
    active = (silu_gate * up_pre * row_scale).astype(BF16)
    grad_up_pre = (grad_active * silu_gate).astype(BF16)
    grad_gate_pre = (
        grad_active * up_pre * sigmoid_gate * (1.0 + gate_pre * (1.0 - sigmoid_gate))
    ).astype(BF16)
    grad_partial = dot_nn(grad_gate_pre, gate_matrix) + dot_nn(grad_up_pre, up_matrix)
    grad_partial = lax.psum_scatter(
        grad_partial.astype(BF16), "ep", scatter_dimension=0, tiled=True
    )
    grad_share = lax.psum_scatter(grad_partial, "tp", scatter_dimension=1, tiled=True)
    out_partial = dot_nn(active, down_matrix)
    out_partial = lax.psum_scatter(out_partial.astype(BF16), "ep", scatter_dimension=0, tiled=True)
    mixed = lax.psum_scatter(out_partial, "tp", scatter_dimension=1, tiled=True)
    hidden_share = lax.dynamic_slice_in_dim(hidden, tp_index * share_width, share_width, 1)
    layer_dealt = (hidden_share + mixed.astype(F32)).astype(BF16)
    grad_w_down = dot_tn(active, all_grad).reshape(w_down.shape)
    grad_w_gate = dot_tn(grad_gate_pre, all_in).reshape(w_gate.shape)
    grad_w_up = dot_tn(grad_up_pre, all_in).reshape(w_up.shape)

    grad_float = grad_full.astype(F32)
    grad_moe_in = lax.all_gather(grad_share, "tp", axis=1, tiled=True).astype(F32)
    norm_moe_part = jnp.sum(grad_moe_in * unit_two, axis=0)
    grad_hidden = grad_float + norm_back(grad_moe_in * gain_moe, unit_two, inverse_two)
    grad_attn = grad_hidden.astype(BF16)
    grad_w_out = dot_tn(grad_attn, context_low)
    grad_context = (
        dot_nn(grad_attn, full_out)
        .astype(BF16)
        .reshape(MICRO, micro_rows, kv_here, group_size, HEAD_DIM)
    )
    grad_probs = jnp.einsum("mqkgd,mtkd->mkgqt", grad_context, values, preferred_element_type=F32)
    prob_delta = jnp.sum(attn_probs * grad_probs, axis=-1, keepdims=True)
    grad_scores = (attn_probs * (grad_probs - prob_delta)).astype(BF16)
    grad_queries = (
        jnp.einsum("mkgqt,mtkd->mqkgd", grad_scores, key_rows, preferred_element_type=F32).reshape(
            rows_dev, heads_here, HEAD_DIM
        )
        * score_scale
    )
    grad_keys = (
        jnp.einsum("mkgqt,mqkgd->mtkd", grad_scores, queries, preferred_element_type=F32).reshape(
            rows_dev, kv_here, HEAD_DIM
        )
        * score_scale
    )
    grad_values = jnp.einsum(
        "mkgqt,mqkgd->mtkd", probs_low, grad_context, preferred_element_type=F32
    )
    grad_unit_query = rotate_back(grad_queries, cosine, sine_table)
    grad_unit_key = rotate_back(grad_keys, cosine, sine_table)
    query_gain_part = jnp.sum(grad_unit_query * unit_query, axis=(0, 1))
    key_gain_part = jnp.sum(grad_unit_key * unit_key, axis=(0, 1))
    grad_query_proj = (
        norm_back(grad_unit_query * gain_query, unit_query, inverse_query)
        .reshape(rows_dev, heads_here * HEAD_DIM)
        .astype(BF16)
    )
    grad_key_proj = (
        norm_back(grad_unit_key * gain_key, unit_key, inverse_key)
        .reshape(rows_dev, kv_width)
        .astype(BF16)
    )
    grad_value_proj = grad_values.reshape(rows_dev, kv_width).astype(BF16)
    grad_kv_proj = jnp.concatenate([grad_key_proj, grad_value_proj], axis=1)
    normed_part = dot_nt(grad_query_proj, full_query) + dot_nt(grad_kv_proj, full_kv)
    grad_normed = lax.psum_scatter(
        normed_part.astype(BF16), "tp", scatter_dimension=1, tiled=True
    ).astype(F32)
    grad_packed = jnp.concatenate(
        [
            dot_tn(normed, grad_query_proj).astype(BF16),
            grad_w_out.astype(BF16),
            dot_tn(normed, grad_kv_proj).astype(BF16),
        ],
        axis=1,
    )
    grad_packed = lax.psum_scatter(grad_packed, "ep", scatter_dimension=0, tiled=True).astype(F32)

    start = tp_index * share_width
    gain_share = lax.dynamic_slice_in_dim(gain_attn, start, share_width, 0)
    unit_share = lax.dynamic_slice_in_dim(unit_one, start, share_width, 1)
    hidden_grad_share = lax.dynamic_slice_in_dim(grad_hidden, start, share_width, 1)
    scaled = grad_normed * gain_share
    row_mean = lax.psum(jnp.sum(scaled * unit_share, axis=1), "tp") / model_width
    grad_layer = hidden_grad_share + inverse_one * (scaled - unit_share * row_mean[:, None])
    norm_attn_part = lax.dynamic_update_slice_in_dim(
        jnp.zeros((model_width,), F32), jnp.sum(grad_normed * unit_share, axis=0), start, 0
    )
    small = jnp.concatenate(
        [norm_attn_part, norm_moe_part / tp_count, query_gain_part, key_gain_part]
    )
    small = lax.psum(small, ("ep", "tp"))
    grad_norm_attn = lax.dynamic_slice_in_dim(small, ep_index * part, part, 0)
    grad_norm_moe = lax.dynamic_slice_in_dim(small, model_width + ep_index * part, part, 0)
    grad_query_gain = lax.dynamic_slice_in_dim(
        small, 2 * model_width + ep_index * head_part, head_part, 0
    )
    grad_key_gain = lax.dynamic_slice_in_dim(
        small, 2 * model_width + HEAD_DIM + ep_index * head_part, head_part, 0
    )

    back = jnp.concatenate([layer_dealt, grad_layer.astype(BF16)], axis=1)
    home = exchange(dot_tn(recv, back).astype(BF16), ep_count)
    home = dot_tn(send, home)
    return (
        home[:, :share_width].astype(BF16),
        home[:, share_width:],
        grad_packed[:, :q_width],
        grad_packed[:, 2 * q_width : 2 * q_width + kv_width],
        grad_packed[:, 2 * q_width + kv_width :],
        grad_packed[:, q_width : 2 * q_width],
        grad_norm_attn,
        grad_norm_moe,
        grad_query_gain,
        grad_key_gain,
        grad_w_gate,
        grad_w_up,
        grad_w_down,
    )


def route_scales(routes, route_weights, experts, local_experts, hidden_here, ep_index):
    expert_ids = jnp.arange(experts, dtype=jnp.int32)
    dense = jnp.sum(
        jnp.where(
            routes.T[None, :, :] == expert_ids[:, None, None], route_weights.T[None, :, :], 0.0
        ),
        axis=1,
    )
    terms = []
    for _ in range(SCALE_TERMS):
        terms.append(lax.reduce_precision(dense, 8, 7))
        dense = dense - terms[-1]
    parts = jnp.concatenate(terms, axis=0).astype(BF16)
    flat_expert = ep_index * local_experts + jnp.repeat(
        jnp.arange(local_experts, dtype=jnp.int32), hidden_here
    )
    part_expert = jnp.arange(parts.shape[0], dtype=jnp.int32) % experts
    return (parts, (part_expert[:, None] == flat_expert[None, :]).astype(BF16))


def plane_layer(
    layer_in,
    token_order,
    seq_lengths,
    routes,
    route_weights,
    w_query,
    w_key,
    w_value,
    w_out,
    norm_attn,
    norm_moe,
    query_gain,
    key_gain,
    w_gate,
    w_up,
    w_down,
    grad_out,
):
    ep_count = lax.axis_size("ep")
    tp_count = lax.axis_size("tp")
    tp_index = lax.axis_index("tp")
    ep_index = lax.axis_index("ep")
    local_experts, hidden_here, model_width = w_gate.shape
    experts = local_experts * ep_count
    rows_dev = layer_in.shape[0]
    micro_rows = rows_dev // MICRO
    share_width = layer_in.shape[1]
    score_scale = HEAD_DIM ** (-0.5)

    q_width, kv_width = w_query.shape[1], w_key.shape[1]
    heads_here = q_width // HEAD_DIM
    kv_here = kv_width // HEAD_DIM
    group_size = heads_here // kv_here
    send, recv = deal_matrices(token_order, ep_index, rows_dev, ep_count)
    send_rows = permute_rows(send, jnp.concatenate([layer_in, grad_out], axis=1))
    part = norm_attn.shape[0]
    head_part = query_gain.shape[0]
    scale_parts, pick = route_scales(
        routes, route_weights, experts, local_experts, hidden_here, ep_index
    )
    gain_at = scale_parts.shape[0]
    gains = jnp.zeros((1, 2 * part + 2 * HEAD_DIM), BF16)
    for vector, at in (
        (norm_attn, 0),
        (norm_moe, part),
        (query_gain, 2 * part + ep_index * head_part),
        (key_gain, 2 * part + HEAD_DIM + ep_index * head_part),
    ):
        gains = lax.dynamic_update_slice(gains, vector[None], (0, at))
    small_rows = -(-(gain_at + 1) // 32) * 32
    small = jnp.pad(scale_parts, ((0, 0), (0, gains.shape[1] - scale_parts.shape[1])))
    small = jnp.pad(
        jnp.concatenate([small, gains], axis=0), ((0, small_rows - gain_at - 1), (0, 0))
    )
    segment, position = jax.vmap(positions_of, in_axes=(0, None))(seq_lengths, micro_rows)
    cosine, sine_table = rope_tables(position.reshape(-1), HEAD_DIM // 2)
    cosine_wide = jnp.concatenate([cosine[:, 0], cosine[:, 0]], axis=1)
    sine_wide = jnp.concatenate([-sine_table[:, 0], sine_table[:, 0]], axis=1)
    offsets = jnp.arange(micro_rows, dtype=jnp.int32)
    allowed = (segment[:, :, None] == segment[:, None, :]) & (
        offsets[None, None, :] <= offsets[None, :, None]
    )
    mask = allowed.astype(F32).reshape(rows_dev, micro_rows)
    (
        layer_full,
        grad_full,
        hidden,
        moe_in,
        proj,
        turned,
        key_flat,
        value_flat,
        probs,
        context_low,
        small_all,
        normed,
        all_grad,
        w_in_all,
        full_out,
    ) = front_call(
        gain_at,
        ep_count,
        tp_count,
        send_rows,
        recv,
        small,
        cosine_wide,
        sine_wide,
        mask,
        w_query,
        w_key,
        w_value,
        w_out,
    )

    flat = local_experts * hidden_here
    gate_matrix = w_gate.reshape(flat, model_width)
    up_matrix = w_up.reshape(flat, model_width)
    down_matrix = w_down.reshape(flat, model_width)
    grad_partial, mixed_part, grad_w_gate, grad_w_up, grad_w_down = expert_call(
        moe_in, all_grad, small_all, pick, gate_matrix, up_matrix, down_matrix
    )
    layer_out, layer_grad, d_in, d_out, sums = back_call(
        gain_at,
        ep_count,
        tp_count,
        grad_partial,
        mixed_part,
        w_in_all,
        full_out,
        (
            layer_full,
            hidden,
            grad_full,
            normed,
            proj,
            turned,
            key_flat,
            value_flat,
            probs,
            context_low,
            small_all,
            cosine_wide,
            sine_wide,
            send,
            recv,
        ),
    )
    sums = jnp.sum(sums, axis=0)
    head_at = 2 * part + ep_index * head_part
    return (
        layer_out,
        layer_grad.astype(F32),
        d_in[:, :q_width].astype(F32),
        d_in[:, q_width : q_width + kv_width].astype(F32),
        d_in[:, q_width + kv_width :].astype(F32),
        d_out.astype(F32),
        sums[:part],
        sums[part : 2 * part],
        lax.dynamic_slice_in_dim(sums, head_at, head_part, 0),
        lax.dynamic_slice_in_dim(sums, head_at + HEAD_DIM, head_part, 0),
        grad_w_gate.astype(F32).reshape(w_gate.shape),
        grad_w_up.astype(F32).reshape(w_up.shape),
        grad_w_down.astype(F32).reshape(w_down.shape),
    )


def solution(mesh):
    shape = dict(mesh.shape)
    planes = shape["ep"] == 8 and shape["tp"] == 4
    return jax.shard_map(
        plane_layer if planes else plain_layer,
        mesh=mesh,
        in_specs=(
            P("ep", "tp"),
            P(),
            P("ep", None),
            P("ep", None),
            P("ep", None),
            P("ep", "tp"),
            P("ep", "tp"),
            P("ep", "tp"),
            P("ep", "tp"),
            P("ep"),
            P("ep"),
            P("ep"),
            P("ep"),
            P("ep", "tp", None),
            P("ep", "tp", None),
            P("ep", "tp", None),
            P("ep", "tp"),
        ),
        out_specs=(
            P("ep", "tp"),
            P("ep", "tp"),
            P("ep", "tp"),
            P("ep", "tp"),
            P("ep", "tp"),
            P("ep", "tp"),
            P("ep"),
            P("ep"),
            P("ep"),
            P("ep"),
            P("ep", "tp", None),
            P("ep", "tp", None),
            P("ep", "tp", None),
        ),
        check_vma=False,
    )
```
